32 devices in a mesh: wide: 16 (over z, y, x), narrow: 2 (over core).
Axes of the slice: x: 2, y: 2, z: 4, core: 2. Of those that a mesh axis runs over, the one named last changes fastest.
Arguments:
- tokens: bfloat16 [32, 96, 6400], P(('wide', 'narrow')), may hold values from -6 to 6
- image_sides: int32 [32], P(('wide', 'narrow')), may hold values from 56 to 80, as said below
- grad_out: bfloat16 [32, 96, 6400], P(('wide', 'narrow')), may hold values from -6 to 6
- master: float32 [144960], P('wide')
- first_moment: float32 [144960], P('wide')
- second_moment: float32 [144960], P('wide'), as said below
- weight_average: float32 [144960], P('wide')
Outputs:
- block_out: bfloat16 [32, 96, 6400], P(('wide', 'narrow'))
- grad_in: bfloat16 [32, 96, 6400], P(('wide', 'narrow'))
- new_master: float32 [144960], P('wide')
- new_first: float32 [144960], P('wide')
- new_second: float32 [144960], P('wide')
- new_average: float32 [144960], P('wide')
The draws below stay inside these ranges and needn't reach their ends.
Inputs may be any that keep to these rules, and one draw needn't show every extreme that they name: `image_sides`: each image's side is one of three values: 4 times (14), 4 times (16), or 80; the first image's side is 80. `second_moment`: every entry is positive.
All inputs are finite; a program needn't handle non-finite values.
Results may differ from the reference program's by a relative error of at most 0.012.
Values may be sent and summed in bfloat16 or wider, within the bound.
No kernel may reach another device: no remote copies, remote signals or barrier semaphores. Data moves between devices by JAX's collectives and lax.ppermute only.
A program may use at most 256 MiB of HBM per device.

```python
import math
import jax
import jax.numpy as jnp
from jax import lax

D = 96
HID = 384
KSTR = 4
KG = 20
STEP = 5
GRID = 80
TOK = 6400
KK = 400
REL = 159
IMAGES = 32
NPAD = 144960


def segment_list_drawn():
    return [('w_qkv', (3 * D, D), D ** (-0.5)), ('b_qkv', (3 * D,), 0.2), ('pool_q', (D, 9), 1.0 / 3.0), ('pool_k', (D, 9), 1.0 / 3.0), ('pool_v', (D, 9), 1.0 / 3.0), ('rel_h', (REL, D), 0.5 * D ** (-0.5)), ('rel_w', (REL, D), 0.5 * D ** (-0.5)), ('w_proj', (D, D), D ** (-0.5)), ('b_proj', (D,), 0.2), ('w_fc1', (HID, D), D ** (-0.5)), ('b_fc1', (HID,), 0.2), ('w_fc2', (D, HID), HID ** (-0.5)), ('b_fc2', (D,), 0.2), ('ln1_g', (D,), 0.5), ('ln1_b', (D,), 0.2), ('ln2_g', (D,), 0.5), ('ln2_b', (D,), 0.2)]


def segment_scales():
    scales = []
    gain_flags = []
    used_len = 0
    for segment_name, piece_shape, spread in segment_list_drawn():
        length = math.prod(piece_shape)
        scales.append(jnp.full((length,), spread, jnp.float32))
        is_gain = 1.0 if segment_name in ('ln1_g', 'ln2_g') else 0.0
        gain_flags.append(jnp.full((length,), is_gain, jnp.float32))
        used_len += length
    scales.append(jnp.full((NPAD - used_len,), D ** (-0.5), jnp.float32))
    gain_flags.append(jnp.zeros((NPAD - used_len,), jnp.float32))
    return (jnp.concatenate(scales), jnp.concatenate(gain_flags))


def parameter_like(key):
    scales, gain_flags = segment_scales()
    noise_draw = jax.random.normal(key, (NPAD,), jnp.float32)
    gain_part = 1.0 + scales * jax.random.uniform(jax.random.fold_in(key, 5), (NPAD,), jnp.float32, -1.0, 1.0)
    return jnp.where(gain_flags > 0, gain_part, scales * noise_draw)


def grad_size():
    return GRID * (2.0 * IMAGES) ** (-0.5)


def draw_image_sides(key, part):
    picked = jax.random.randint(jax.random.fold_in(key, 23), (IMAGES,), 0, 3)
    sides = KSTR * jnp.where(picked == 0, KG - 6, jnp.where(picked == 1, KG - 4, KG))
    return sides.at[0].set(GRID).astype(jnp.int32)


def draw_master(key, part):
    return parameter_like(jax.random.fold_in(key, 11))


def draw_weight_average(key, part):
    return parameter_like(jax.random.fold_in(key, 13))


def draw_first_moment(key, part):
    inner = jax.random.fold_in(key, 17)
    noise_draw = jax.random.normal(inner, (NPAD,), jnp.float32)
    return grad_size() * noise_draw


def draw_second_moment(key, part):
    inner = jax.random.fold_in(key, 19)
    factor = jnp.exp(jax.random.uniform(inner, (NPAD,), jnp.float32, 0.0, 1.3862944))
    return grad_size() * grad_size() * factor


def shard_levels(own_key, extent, split, smallest, largest):
    level, own = 1.0, jax.random.fold_in(own_key, 6)
    for dim, shards_of in split:
        draws = jnp.exp(jax.random.uniform(jax.random.fold_in(own, dim), (shards_of,), jnp.float32, smallest / len(split), largest / len(split)))
        level = level * jnp.repeat(draws, extent[dim] // shards_of).reshape([-1 if axis == dim else 1 for axis in range(len(extent))])
    return level


def centred(rng, shape, scale, bound, shards=(), held_as=jnp.bfloat16):
    array = scale * jax.random.normal(rng, shape, jnp.float32)
    if shards:
        array = array * shard_levels(rng, shape, shards, -0.22, 0.18)
    return jnp.clip(array, -bound, bound).astype(held_as)


def setup_inputs(seed: int = 0) -> dict:
    key_list = jax.random.split(jax.random.key(seed), 8)
    return {
        "tokens": centred(key_list[0], (IMAGES, D, TOK), 1.0, 6.0, ((0, 32),)),
        "image_sides": draw_image_sides(jax.random.fold_in(key_list[7], 71), 0),
        "grad_out": centred(key_list[2], (IMAGES, D, TOK), 1.0, 6.0, ((0, 32),)),
        "master": draw_master(jax.random.fold_in(key_list[7], 71), 0),
        "first_moment": draw_first_moment(jax.random.fold_in(key_list[7], 71), 0),
        "second_moment": draw_second_moment(jax.random.fold_in(key_list[7], 71), 0),
        "weight_average": draw_weight_average(jax.random.fold_in(key_list[7], 71), 0),
    }


@jax.custom_vjp
def low(v):
    return lax.optimization_barrier(v.astype(jnp.bfloat16)).astype(jnp.float32)

@jax.custom_vjp
def low_back(v):
    return v

def low_keep(v):
    return (low(v), None)

def low_pass(kept, grad):
    return (grad,)

def back_keep(v):
    return (v, None)

def back_low(kept, grad):
    return (low(grad),)
low.defvjp(low_keep, low_pass)
low_back.defvjp(back_keep, back_low)
norm_eps = 1e-06
beta_first = 0.5
beta_second = 0.5
adam_eps = 1e-08
weight_decay = 0.05
rate_factor = 0.4
average_decay = 0.8
high = lax.Precision.HIGHEST

def segment_list():
    return [('w_qkv', (3 * D, D), D ** (-0.5)), ('b_qkv', (3 * D,), 0.2), ('pool_q', (D, 9), 1.0 / 3.0), ('pool_k', (D, 9), 1.0 / 3.0), ('pool_v', (D, 9), 1.0 / 3.0), ('rel_h', (REL, D), 0.5 * D ** (-0.5)), ('rel_w', (REL, D), 0.5 * D ** (-0.5)), ('w_proj', (D, D), D ** (-0.5)), ('b_proj', (D,), 0.2), ('w_fc1', (HID, D), D ** (-0.5)), ('b_fc1', (HID,), 0.2), ('w_fc2', (D, HID), HID ** (-0.5)), ('b_fc2', (D,), 0.2), ('ln1_g', (D,), 0.5), ('ln1_b', (D,), 0.2), ('ln2_g', (D,), 0.5), ('ln2_b', (D,), 0.2)]

def unpack_flat(flat):
    pieces = {}
    offset = 0
    for segment_name, piece_shape, spread in segment_list():
        length = math.prod(piece_shape)
        pieces[segment_name] = flat[offset:offset + length].reshape(piece_shape)
        offset += length
    return pieces

def rate_vector(full_len):
    segment_rates = []
    used_len = 0
    for segment_name, piece_shape, spread in segment_list():
        length = math.prod(piece_shape)
        segment_rates.append(jnp.full((length,), rate_factor * spread, jnp.float32))
        used_len += length
    segment_rates.append(jnp.full((full_len - used_len,), rate_factor * D ** (-0.5), jnp.float32))
    return jnp.concatenate(segment_rates)

def layer_norm(values, scale_gain, shift_bias):
    center = values - lax.optimization_barrier(jnp.mean(values, axis=0, keepdims=True))
    spread_sq = lax.optimization_barrier(jnp.mean(center * center, axis=0, keepdims=True))
    return center * lax.rsqrt(spread_sq + norm_eps) * scale_gain[:, None] + shift_bias[:, None]

def depth_pool(field_in, kernel, stride, side_out):
    channels = field_in.shape[0]
    padded = jnp.pad(field_in.reshape(channels, GRID, GRID), ((0, 0), (1, 1), (1, 1)))
    result = jnp.zeros((channels, side_out, side_out), jnp.float32)
    reach = stride * (side_out - 1) + 1
    for row_off in range(3):
        for col_off in range(3):
            window = padded[:, row_off:row_off + reach:stride, col_off:col_off + reach:stride]
            result = result + kernel[:, row_off * 3 + col_off][:, None, None] * window
    return result.reshape(channels, side_out * side_out)

def grid_masks(image_side):
    row_valid = (jnp.arange(GRID, dtype=jnp.int32) < image_side).astype(jnp.float32)
    token_mask = (row_valid[:, None] * row_valid[None, :]).reshape(TOK)
    pooled = (jnp.arange(KG, dtype=jnp.int32) * KSTR < image_side).astype(jnp.float32)
    key_mask = (pooled[:, None] * pooled[None, :]).reshape(KK)
    return (token_mask, key_mask)

def masked_softmax(scores, key_mask):
    return jax.nn.softmax(jnp.where(key_mask[:, None] > 0, scores, -1e+30), axis=0)

def relative_index():
    return (jnp.arange(GRID, dtype=jnp.int32)[:, None] - KSTR * jnp.arange(KG, dtype=jnp.int32)[None, :] + GRID - 1).astype(jnp.int32)

def forward_image(values, flat, image_side):
    weights = unpack_flat(low(flat))
    token_mask, key_mask = grid_masks(image_side)
    normed = layer_norm(values, weights['ln1_g'], weights['ln1_b'])
    mixed_qkv = jnp.dot(weights['w_qkv'], low(normed), precision=high) + weights['b_qkv'][:, None]
    mixed_qkv = low_back(mixed_qkv * token_mask[None, :])
    queries = low(depth_pool(mixed_qkv[:D], weights['pool_q'], 1, GRID) * token_mask[None, :])
    keyset = low(depth_pool(mixed_qkv[D:2 * D], weights['pool_k'], KSTR, KG) * key_mask[None, :])
    valueset = low(depth_pool(mixed_qkv[2 * D:], weights['pool_v'], KSTR, KG) * key_mask[None, :])
    rel_index = relative_index()
    grid_query = queries.reshape(D, GRID, GRID)
    along_rows = jnp.einsum('drc,rad->arc', grid_query, weights['rel_h'][rel_index], precision=high).reshape(KG, 1, TOK)
    along_cols = jnp.einsum('drc,cbd->brc', grid_query, weights['rel_w'][rel_index], precision=high).reshape(1, KG, TOK)
    content = jnp.dot(keyset.T, queries, precision=high).reshape(KG, KG, TOK)
    scores = low_back((D ** (-0.5) * content + along_rows + along_cols).reshape(KK, TOK))
    attention = masked_softmax(scores, key_mask)
    attended = low_back(jnp.dot(valueset, low(attention), precision=high) + queries)
    projected = low_back(jnp.dot(weights['w_proj'], low(attended), precision=high) + weights['b_proj'][:, None])
    middle = values + projected
    normed_two = layer_norm(middle, weights['ln2_g'], weights['ln2_b'])
    hidden = low_back(jnp.dot(weights['w_fc1'], low(normed_two), precision=high) + weights['b_fc1'][:, None])
    active = jax.nn.gelu(hidden, approximate=False)
    mlp_out = low_back(jnp.dot(weights['w_fc2'], low(active), precision=high) + weights['b_fc2'][:, None])
    return (middle + mlp_out) * token_mask[None, :]

def adam_update(gradient, master_part, first_part, second_part, average_part, step_rates):
    moment_one = beta_first * first_part + (1.0 - beta_first) * gradient
    moment_two = beta_second * second_part + (1.0 - beta_second) * gradient * gradient
    fix_one = 1.0 - beta_first ** STEP
    fix_two = 1.0 - beta_second ** STEP
    direction = moment_one / fix_one / (jnp.sqrt(moment_two / fix_two) + adam_eps)
    updated = master_part - step_rates * (direction + weight_decay * master_part)
    blended = average_decay * average_part + (1.0 - average_decay) * updated
    return (updated, moment_one, moment_two, blended)

def reference(tokens, image_sides, grad_out, master, first_moment, second_moment, weight_average):

    def one_image(running, inputs):
        pixels, image_side, cotangent = inputs

        def image_fn(pixel_in, flat_in):
            return forward_image(pixel_in, flat_in, image_side)
        output, pullback = jax.vjp(image_fn, pixels.astype(jnp.float32), master)
        grad_pixels, grad_flat = pullback(cotangent.astype(jnp.float32))
        return (running + grad_flat, (output.astype(jnp.bfloat16), grad_pixels.astype(jnp.bfloat16)))
    summed, outputs = lax.scan(one_image, jnp.zeros_like(master), (tokens, image_sides, grad_out))
    block_out, grad_in = outputs
    gradient = summed / IMAGES
    updated, moment_one, moment_two, blended = adam_update(gradient, master, first_moment, second_moment, weight_average, rate_vector(NPAD))
    return (block_out, grad_in, updated, moment_one, moment_two, blended)
```

```python
import functools
import math

import jax
import jax.numpy as jnp
import numpy as np
from jax import lax
from jax.experimental import pallas as pl
from jax.experimental.pallas import tpu as pltpu
from jax.sharding import PartitionSpec as P

D = 96
HID = 384
KSTR = 4
KG = 20
STEP = 5
GRID = 80
TOK = 6400
KK = 400
REL = 159

norm_eps = 1e-06
beta_first = 0.5
beta_second = 0.5
adam_eps = 1e-08
weight_decay = 0.05
rate_factor = 0.4
average_decay = 0.8

f32 = jnp.float32
bf16 = jnp.bfloat16

HALO = 128
LEAD = 88
FIELD = LEAD + TOK + 8
TILE_ONE = 640
TILE_TWO = 640
TILE_THREE = 640
SCORE_SCALE = D ** (-0.5)
LOG2E = 1.4426950408889634


def segment_list():
    return [
        ("w_qkv", (3 * D, D), D ** (-0.5)),
        ("b_qkv", (3 * D,), 0.2),
        ("pool_q", (D, 9), 1.0 / 3.0),
        ("pool_k", (D, 9), 1.0 / 3.0),
        ("pool_v", (D, 9), 1.0 / 3.0),
        ("rel_h", (REL, D), 0.5 * D ** (-0.5)),
        ("rel_w", (REL, D), 0.5 * D ** (-0.5)),
        ("w_proj", (D, D), D ** (-0.5)),
        ("b_proj", (D,), 0.2),
        ("w_fc1", (HID, D), D ** (-0.5)),
        ("b_fc1", (HID,), 0.2),
        ("w_fc2", (D, HID), HID ** (-0.5)),
        ("b_fc2", (D,), 0.2),
        ("ln1_g", (D,), 0.5),
        ("ln1_b", (D,), 0.2),
        ("ln2_g", (D,), 0.5),
        ("ln2_b", (D,), 0.2),
    ]


def row_bases():
    bases = {}
    offset = 0
    for name, shape, _ in segment_list():
        assert offset % D == 0
        bases[name] = offset // D
        offset += math.prod(shape)
    return bases


ROW = row_bases()


def rate_values(full_len):
    rates = np.full((full_len,), rate_factor * D ** (-0.5), np.float32)
    offset = 0
    for _, shape, spread in segment_list():
        length = math.prod(shape)
        rates[offset : offset + length] = rate_factor * spread
        offset += length
    return rates


def block_rows(shard_len):
    return 16 * (-(-(-(-(shard_len + D - 1) // D)) // 16))


def pool_selectors():
    flat = np.arange(9 * D).reshape(9, D)
    channel = (flat[:, None, :] // 9 == np.arange(D)[None, :, None]).astype(np.float32)
    tap = (flat[:, :, None] % 9 == np.arange(128)[None, None, :]).astype(np.float32)
    return jnp.asarray(channel, bf16), jnp.asarray(tap, bf16)


def lane_index():
    place = np.arange(-HALO, TOK + HALO)
    table = np.zeros((8, TOK + 2 * HALO), np.int32)
    table[0] = place // GRID
    table[1] = place % GRID
    return jnp.asarray(table)


def dot(a, b):
    return lax.dot_general(a, b, (((1,), (0,)), ((), ())), preferred_element_type=f32)


def dot_nt(a, b):
    return lax.dot_general(a, b, (((1,), (1,)), ((), ())), preferred_element_type=f32)


def dot_tn(a, b):
    return lax.dot_general(a, b, (((0,), (0,)), ((), ())), preferred_element_type=f32)


def normalize(values):
    mean = jnp.sum(values, axis=0, keepdims=True) * (1.0 / D)
    center = values - mean
    spread = jnp.sum(center * center, axis=0, keepdims=True) * (1.0 / D)
    inv = lax.rsqrt(spread + norm_eps)
    return center * inv, inv


def normalize_back(grad, unit, inv):
    mean = jnp.sum(grad, axis=0, keepdims=True) * (1.0 / D)
    along = jnp.sum(grad * unit, axis=0, keepdims=True) * (1.0 / D)
    return inv * (grad - mean - unit * along)


def gelu_both(v):
    e = jnp.exp2((v * v) * (-0.5 * LOG2E))
    t = 1.0 / (1.0 + (0.3275911 * math.sqrt(0.5)) * jnp.abs(v))
    series = 0.5 * 1.061405429
    for coef in (-1.453152027, 1.421413741, -0.284496736, 0.254829592):
        series = series * t + 0.5 * coef
    tail = series * t * e
    below = jnp.where(v < 0, tail, 1.0 - tail)
    return v * below, below + (v * (1.0 / math.sqrt(2.0 * math.pi))) * e


def skew_in(rows, place, width):
    where = jnp.broadcast_to(place, (40, width))
    residue = where & 3
    picked = jnp.where(
        residue < 2,
        jnp.where(residue == 0, rows[0:40], rows[40:80]),
        jnp.where(residue == 2, rows[80:120], rows[120:160]),
    )
    shift = where >> 2
    for step in (16, 8, 4, 2, 1):
        picked = jnp.where((shift & step) != 0, pltpu.roll(picked, 40 - step, 0), picked)
    return picked[0:32]


def skew_out(rows, place, width, put):
    where = jnp.broadcast_to(place, (40, width))
    spread = jnp.concatenate([rows, jnp.zeros((8, width), f32)], axis=0)
    shift = where >> 2
    for step in (1, 2, 4, 8, 16):
        spread = jnp.where((shift & step) != 0, pltpu.roll(spread, step, 0), spread)
    residue = where & 3
    for k in range(4):
        put(k, jnp.where(residue == k, spread, 0.0))


def fold_lanes(values):
    width = values.shape[1]
    total = values[:, 0:128]
    for k in range(1, width // 128):
        total = total + values[:, k * 128 : (k + 1) * 128]
    return total


def column_row(column):
    return jnp.transpose(jnp.broadcast_to(column, (D, 128)))[0:1, :]


def image_kernel(
    starts,
    rows_of,
    side_ref,
    chunk_ref,
    x_ref,
    gy_ref,
    idx_ref,
    zsel_ref,
    tsel_ref,
    out_ref,
    gin_ref,
    gchunk_ref,
    wf, wq, wqt, wkt, wvt, wp, wpt, w1, w1t, w2, w2t, rel, relt, cols, kq, kk, kv,
    fq, fk, fv, gfk, gfv, qb, gq, gm,
    a1, a2, vb, vbt, kp, vpool,
    rhs, gse, aaug, n2aug, oaug, n1aug,
    dw2, dw1, dpr, gv, gkr, ln2acc, dwq, dwk, dwv, ln1acc, kqacc, gkt, gvt, gr,
):
    side = side_ref[0]

    wf[...] = jnp.zeros(wf.shape, f32)
    for w, start in enumerate(starts):
        wf[start : start + rows_of, 0:D] += chunk_ref[w].astype(f32)

    def piece(name, count, first=0):
        base = ROW[name] + first
        return wf[base : base + count, :]

    wq[...] = piece("w_qkv", D)[:, :D].astype(bf16)
    wqt[...] = jnp.transpose(piece("w_qkv", D))[:D, :].astype(bf16)
    wkt[...] = jnp.zeros(wkt.shape, bf16)
    wvt[...] = jnp.zeros(wvt.shape, bf16)
    wkt[:, 0:D] = jnp.transpose(piece("w_qkv", D, D))[:D, :].astype(bf16)
    wvt[:, 0:D] = jnp.transpose(piece("w_qkv", D, 2 * D))[:D, :].astype(bf16)
    wp[...] = piece("w_proj", D)[:, :D].astype(bf16)
    wpt[...] = jnp.transpose(piece("w_proj", D))[:D, :].astype(bf16)
    w1[...] = piece("w_fc1", HID)[:, :D].astype(bf16)
    w1t[...] = jnp.transpose(piece("w_fc1", HID))[:D, :].astype(bf16)
    for k in range(4):
        block = wf[pl.ds(ROW["w_fc2"] + k, D, stride=4), :]
        w2t[k * D : (k + 1) * D, :] = jnp.transpose(block)[:D, :].astype(bf16)
    w2[...] = jnp.transpose(w2t[...].astype(f32)).astype(bf16)
    for k in range(4):
        rel[k * 40 : k * 40 + 40, :] = wf[pl.ds(ROW["rel_h"] + 3 + k, 40, stride=4), :][:, :D].astype(bf16)
        rel[160 + k * 40 : 200 + k * 40, :] = wf[pl.ds(ROW["rel_w"] + 3 + k, 40, stride=4), :][:, :D].astype(bf16)
    relt[...] = jnp.transpose(rel[...].astype(f32)).astype(bf16)

    vec_rows = [ROW["b_qkv"], ROW["b_proj"], ROW["b_fc2"], ROW["ln1_g"], ROW["ln1_b"], ROW["ln2_g"], ROW["ln2_b"]]
    vec_rows += [ROW["b_fc1"] + k for k in range(4)]
    stacked = jnp.concatenate([wf[r : r + 1, :] for r in vec_rows] + [jnp.zeros((128 - len(vec_rows), 128), f32)], axis=0)
    cols[...] = jnp.transpose(stacked)[:D, :]

    def pool_columns(name):
        total = jnp.zeros((D, 128), f32)
        for i in range(9):
            row = wf[ROW[name] + i : ROW[name] + i + 1, :][:, :D]
            total = total + dot((zsel_ref[i].astype(f32) * row).astype(bf16), tsel_ref[i])
        return total

    def pool_rows(name):
        full = jnp.concatenate([pool_columns(name), jnp.zeros((32, 128), f32)], axis=0)
        return jnp.transpose(full)[0:16, :]

    kq[...] = pool_columns("pool_q")
    kk[...] = pool_rows("pool_k")
    kv[...] = pool_rows("pool_v")

    b_q, b_proj, b_fc2 = cols[:, 0:1], cols[:, 1:2], cols[:, 2:3]
    ln1_g, ln1_b, ln2_g, ln2_b = cols[:, 3:4], cols[:, 4:5], cols[:, 5:6], cols[:, 6:7]
    b_fc1 = jnp.concatenate([cols[:, 7 + k : 8 + k] for k in range(4)], axis=0)
    b_k = wf[ROW["b_qkv"] + 1 : ROW["b_qkv"] + 2, :]
    b_v = wf[ROW["b_qkv"] + 2 : ROW["b_qkv"] + 3, :]

    for ref in (fq, gq):
        ref[:, 0:HALO] = jnp.zeros((D, HALO), f32)
        ref[:, HALO + TOK :] = jnp.zeros((D, HALO), f32)
    for ref in (fk, fv):
        ref[0:LEAD, :] = jnp.zeros((LEAD, 128), f32)
    for ref in (gfk, gfv, gr, dw2, dw1, dpr, gv, gkr, ln2acc, dwq, dwk, dwv, ln1acc, kqacc):
        ref[...] = jnp.zeros(ref.shape, ref.dtype)

    def first_row_one(width):
        return jnp.where(lax.broadcasted_iota(jnp.int32, (16, width), 0) == 0, 1.0, 0.0).astype(bf16)

    n1aug[D:, :] = first_row_one(TILE_ONE)
    n2aug[D:, :] = first_row_one(TILE_TWO)
    oaug[D:, :] = first_row_one(TILE_TWO)
    aaug[HID:, :] = first_row_one(TILE_TWO)
    rhs[160:176, :] = first_row_one(TILE_TWO)

    def window(i, tile):
        return pl.ds(pl.multiple_of(i * tile, 128), tile + 2 * HALO)

    def inner(i, tile):
        return pl.ds(pl.multiple_of(i * tile + HALO, 128), tile)

    def plain(i, tile):
        return pl.ds(pl.multiple_of(i * tile, 128), tile)

    def token_mask(i, tile):
        place = idx_ref[0:2, inner(i, tile)]
        return jnp.where((place[0:1] < side) & (place[1:2] < side), 1.0, 0.0)

    def project(i, carry):
        unit, _ = normalize(x_ref[:, plain(i, TILE_ONE)].astype(f32))
        low = (unit * ln1_g + ln1_b).astype(bf16)
        fq[:, inner(i, TILE_ONE)] = (dot(wq[...], low) + b_q) * token_mask(i, TILE_ONE)
        field = pl.ds(pl.multiple_of(i * TILE_ONE + LEAD, 8), TILE_ONE)
        fk[field, :] = dot_tn(low, wkt[...]) + b_k
        fv[field, :] = dot_tn(low, wvt[...]) + b_v
        return carry

    lax.fori_loop(0, TOK // TILE_ONE, project, 0)

    def pool_queries(i, carry):
        tile = TILE_ONE
        wide = tile + 2 * HALO
        field = fq[:, window(i, tile)]
        col = jnp.broadcast_to(idx_ref[1:2, window(i, tile)], (D, wide))
        left = jnp.where(col != 0, pltpu.roll(field, 1, 1), 0.0)
        right = jnp.where(col != GRID - 1, pltpu.roll(field, wide - 1, 1), 0.0)

        def row_sum(u):
            return kq[:, 3 * u : 3 * u + 1] * left + kq[:, 3 * u + 1 : 3 * u + 2] * field + kq[:, 3 * u + 2 : 3 * u + 3] * right

        total = pltpu.roll(row_sum(0), GRID, 1) + row_sum(1) + pltpu.roll(row_sum(2), wide - GRID, 1)
        qb[:, plain(i, tile)] = (total[:, HALO : HALO + tile] * token_mask(i, tile)).astype(bf16)
        return carry

    lax.fori_loop(0, TOK // TILE_ONE, pool_queries, 0)

    b_index = lax.broadcasted_iota(jnp.int32, (KG, 128), 0)

    def tap_start(a, u, v):
        return LEAD + GRID * (KSTR * a + u - 1) + v - 1

    for field, kernel_rows, pooled in ((fk, kk, kp), (fv, kv, vpool)):
        for a in range(KG):
            total = jnp.zeros((KG, 128), f32)
            for u in range(3):
                for v in range(3):
                    block = field[pl.ds(tap_start(a, u, v), KG, stride=KSTR), :]
                    if v == 0:
                        block = jnp.where(b_index == 0, 0.0, block)
                    total = total + kernel_rows[3 * u + v : 3 * u + v + 1, :] * block
            keep = (KSTR * b_index < side) & (KSTR * a < side)
            pooled[KG * a : KG * a + KG, :] = jnp.where(keep, total, 0.0)

    key = lax.broadcasted_iota(jnp.int32, (KK, 80), 0)
    key_a = idx_key = lax.div(key, KG)
    key_b = key - KG * idx_key
    place = lax.broadcasted_iota(jnp.int32, (KK, 80), 1)
    one_a = (place < 32) & (KG - 1 - key_a == place)
    one_b = (place >= 32) & (place < 64) & (KG - 1 - key_b == place - 32)
    hot = jnp.where(one_a | one_b, 1.0, 0.0)
    shut = (place == 64) & ((KSTR * key_a >= side) | (KSTR * key_b >= side))
    a1[:, 0:D] = kp[...][:, :D].astype(bf16)
    a1[:, D : D + 80] = jnp.where(shut, -1e30, hot).astype(bf16)
    vbt[...] = vpool[...][:, :D].astype(bf16)
    a2[0:D, :] = jnp.transpose(kp[...])[:D, :].astype(bf16)
    vb[...] = jnp.transpose(vpool[...])[:D, :].astype(bf16)
    key_l = lax.broadcasted_iota(jnp.int32, (64, KK), 1)
    a_l = lax.div(key_l, KG)
    b_l = key_l - KG * a_l
    row_l = lax.broadcasted_iota(jnp.int32, (64, KK), 0)
    hot_l = ((row_l < 32) & (KG - 1 - a_l == row_l)) | ((row_l >= 32) & (KG - 1 - b_l == row_l - 32))
    a2[D : D + 64, :] = jnp.where(hot_l, 1.0, 0.0).astype(bf16)

    def attend(i, carry):
        tile = TILE_TWO
        here = plain(i, tile)
        mask = token_mask(i, tile)
        row, col = idx_ref[0:1, inner(i, tile)], idx_ref[1:2, inner(i, tile)]
        q = qb[:, here]
        seen = dot(rel[...], q)
        rhs[0:D, :] = q
        rhs[D : D + 32, :] = (skew_in(seen[0:160], row, tile) * math.sqrt(D)).astype(bf16)
        rhs[D + 32 : D + 64, :] = (skew_in(seen[160:320], col, tile) * math.sqrt(D)).astype(bf16)
        scores = dot(a1[...], rhs[...])
        top = jnp.max(scores, axis=0, keepdims=True)
        weight = jnp.exp2((scores - top) * (SCORE_SCALE * LOG2E))
        inv_sum = 1.0 / jnp.sum(weight, axis=0, keepdims=True)
        weight_low = weight.astype(bf16)
        mixed = dot(vb[...], weight_low) * inv_sum
        attended = (mixed + q.astype(f32)).astype(bf16)
        oaug[0:D, :] = attended
        middle = x_ref[:, here].astype(f32) + dot(wp[...], attended) + b_proj
        unit, inv = normalize(middle)
        low = (unit * ln2_g + ln2_b).astype(bf16)
        n2aug[0:D, :] = low
        hidden = dot(w1[...], low) + b_fc1
        active, slope = gelu_both(hidden)
        aaug[0:HID, :] = active.astype(bf16)
        out_ref[:, here] = ((middle + dot(w2[...], aaug[0:HID, :]) + b_fc2) * mask).astype(bf16)

        gy = gy_ref[:, here].astype(f32) * mask
        gy_low = gy.astype(bf16)
        dw2[:, 0:KK] += dot_nt(gy_low, aaug[...])
        gh_low = (slope * dot(w2t[...], gy_low)).astype(bf16)
        dw1[...] += dot_nt(n2aug[...], gh_low)
        gn = dot(w1t[...], gh_low)
        ln2acc[0] += fold_lanes(gn * unit)
        ln2acc[1] += fold_lanes(gn)
        gmid = gy + normalize_back(gn * ln2_g, unit, inv)
        gm[:, here] = gmid
        gm_low = gmid.astype(bf16)
        dpr[:, 0:112] += dot_nt(gm_low, oaug[...])
        go = dot(wpt[...], gm_low)
        go_low = (go * inv_sum).astype(bf16)
        delta = jnp.sum(go_low.astype(f32) * mixed, axis=0, keepdims=True)
        gv[:, 0:KK] += dot_nt(go_low, weight_low)
        gs = weight * (dot(vbt[...], go_low) - delta)
        gse[0:KK, :] = gs.astype(bf16)
        back = dot(a2[...], gse[0:KK, :])

        def put(base):
            def write(k, block):
                gse[base + 40 * k : base + 40 * k + 40, :] = block.astype(bf16)

            return write

        skew_out(back[D : D + 32], row, tile, put(KK))
        skew_out(back[D + 32 : D + 64], col, tile, put(KK + 160))
        gkr[:, 0:720] += dot_nt(q, gse[...])
        gq[:, inner(i, tile)] = go + SCORE_SCALE * back[0:D] + dot(relt[...], gse[KK:720, :])
        return carry

    lax.fori_loop(0, TOK // TILE_TWO, attend, 0)

    gkt[...] = jnp.transpose(gkr[:, 0:512])[0:KK, :] * SCORE_SCALE
    gvt[...] = jnp.transpose(gv[...])[0:KK, :]

    def pool_gradient(name, columns):
        low = columns.astype(bf16)
        for i in range(9):
            spread = dot_nt(low, tsel_ref[i]) * zsel_ref[i].astype(f32)
            gr[ROW[name] + i : ROW[name] + i + 1, 0:D] = jnp.sum(spread, axis=0, keepdims=True)

    for field, kernel_rows, pooled, gfield, name in ((fk, kk, gkt, gfk, "pool_k"), (fv, kv, gvt, gfv, "pool_v")):
        sums = []
        for u in range(3):
            for v in range(3):
                total = jnp.zeros((KG, D), f32)
                for a in range(KG):
                    where = pl.ds(tap_start(a, u, v), KG, stride=KSTR)
                    grad = pooled[KG * a : KG * a + KG, :]
                    if v == 0:
                        grad = jnp.where(b_index[:, :D] == 0, 0.0, grad)
                    total = total + grad * field[where, :][:, :D]
                    spread = kernel_rows[3 * u + v : 3 * u + v + 1, :][:, :D] * grad
                    gfield[where, :] = jnp.concatenate([spread, jnp.zeros((KG, 128 - D), f32)], axis=1)
                sums.append(jnp.sum(total, axis=0, keepdims=True))
        rows = jnp.concatenate(sums + [jnp.zeros((128 - 9, D), f32)], axis=0)
        pool_gradient(name, jnp.transpose(rows))

    def finish(i, carry):
        tile = TILE_THREE
        wide = tile + 2 * HALO
        here = plain(i, tile)
        mid = slice(HALO, HALO + tile)
        mask = token_mask(i, tile)
        grad = gq[:, window(i, tile)]
        col = jnp.broadcast_to(idx_ref[1:2, window(i, tile)], (D, wide))
        after = jnp.where(col != GRID - 1, pltpu.roll(grad, wide - 1, 1), 0.0)
        before = jnp.where(col != 0, pltpu.roll(grad, 1, 1), 0.0)

        def row_sum(u):
            return kq[:, 3 * u : 3 * u + 1] * after + kq[:, 3 * u + 1 : 3 * u + 2] * grad + kq[:, 3 * u + 2 : 3 * u + 3] * before

        total = pltpu.roll(row_sum(0), wide - GRID, 1) + row_sum(1) + pltpu.roll(row_sum(2), GRID, 1)
        gq_low = (total[:, mid] * mask).astype(bf16)
        field = fq[:, window(i, tile)]
        for u, rows in enumerate((pltpu.roll(field, GRID, 1), field, pltpu.roll(field, wide - GRID, 1))):
            for v, moved in enumerate((after, grad, before)):
                kqacc[3 * u + v] += fold_lanes(moved[:, mid] * rows[:, mid])

        unit, inv = normalize(x_ref[:, here].astype(f32))
        n1aug[0:D, :] = (unit * ln1_g + ln1_b).astype(bf16)
        flat = pl.ds(pl.multiple_of(i * tile + LEAD, 8), tile)
        gk_low = gfk[flat, :].astype(bf16)
        gv_low = gfv[flat, :].astype(bf16)
        dwq[:, 0:112] += dot_nt(gq_low, n1aug[...])
        dwk[...] += dot(n1aug[...], gk_low)
        dwv[...] += dot(n1aug[...], gv_low)
        gn = dot(wqt[...], gq_low) + dot_nt(wkt[...], gk_low) + dot_nt(wvt[...], gv_low)
        ln1acc[0] += fold_lanes(gn * unit)
        ln1acc[1] += fold_lanes(gn)
        gin_ref[:, here] = (gm[:, here] + normalize_back(gn * ln1_g, unit, inv)).astype(bf16)
        return carry

    lax.fori_loop(0, TOK // TILE_THREE, finish, 0)

    def write(name, rows, first=0):
        base = ROW[name] + first
        gr[base : base + rows.shape[0], 0:D] = rows

    write("w_qkv", dwq[:, 0:D])
    write("b_qkv", jnp.transpose(dwq[...])[D : D + 1, :])
    for k, ref in ((1, dwk), (2, dwv)):
        write("w_qkv", jnp.transpose(ref[0:D, :])[0:D, :], k * D)
        write("b_qkv", ref[D : D + 1, 0:D], k)
    lane = lax.broadcasted_iota(jnp.int32, (D, 128), 1)
    columns = jnp.zeros((D, 128), f32)
    for k in range(9):
        columns = jnp.where(lane == k, jnp.sum(kqacc[k], axis=1, keepdims=True), columns)
    pool_gradient("pool_q", columns)
    rel_rows = jnp.transpose(gkr[:, 384:768])[16:336, :]
    gse_rows = rel_rows
    for k in range(4):
        gr[pl.ds(ROW["rel_h"] + 3 + k, 39, stride=4), :] = jnp.concatenate(
            [gse_rows[40 * k : 40 * k + 39], jnp.zeros((39, 128 - D), f32)], axis=1
        )
        gr[pl.ds(ROW["rel_w"] + 3 + k, 39, stride=4), :] = jnp.concatenate(
            [gse_rows[160 + 40 * k : 160 + 40 * k + 39], jnp.zeros((39, 128 - D), f32)], axis=1
        )
    write("w_proj", dpr[:, 0:D])
    write("b_proj", jnp.transpose(dpr[...])[D : D + 1, :])
    write("w_fc1", jnp.transpose(dw1[0:D, :]))
    for k in range(4):
        write("b_fc1", dw1[D : D + 1, k * D : (k + 1) * D], k)
        gr[pl.ds(ROW["w_fc2"] + k, D, stride=4), :] = jnp.concatenate(
            [dw2[:, k * D : (k + 1) * D], jnp.zeros((D, 128 - D), f32)], axis=1
        )
    write("b_fc2", jnp.transpose(dw2[:, HID:512])[0:1, :])
    write("ln1_g", column_row(jnp.sum(ln1acc[0], axis=1, keepdims=True)))
    write("ln1_b", column_row(jnp.sum(ln1acc[1], axis=1, keepdims=True)))
    write("ln2_g", column_row(jnp.sum(ln2acc[0], axis=1, keepdims=True)))
    write("ln2_b", column_row(jnp.sum(ln2acc[1], axis=1, keepdims=True)))
    for w, start in enumerate(starts):
        gchunk_ref[w] = gr[start : start + rows_of, 0:D].astype(bf16)


def image_step(starts, rows_of, chunks, pixels, image_side, cotangent):
    depth = 8 * (-(-(starts[-1] + rows_of) // 8))
    zsel, tsel = pool_selectors()
    vm = pltpu.VMEM
    scratch = [
        vm((depth, 128), f32),
        vm((D, D), bf16), vm((D, D), bf16), vm((D, 128), bf16), vm((D, 128), bf16),
        vm((D, D), bf16), vm((D, D), bf16),
        vm((HID, D), bf16), vm((D, HID), bf16), vm((D, HID), bf16), vm((HID, D), bf16),
        vm((320, D), bf16), vm((D, 320), bf16), vm((D, 128), f32), vm((D, 128), f32),
        vm((16, 128), f32), vm((16, 128), f32),
        vm((D, TOK + 2 * HALO), f32), vm((FIELD, 128), f32), vm((FIELD, 128), f32),
        vm((FIELD, 128), f32), vm((FIELD, 128), f32),
        vm((D, TOK), bf16), vm((D, TOK + 2 * HALO), f32), vm((D, TOK), f32),
        vm((KK, 176), bf16), vm((160, KK), bf16), vm((D, KK), bf16), vm((KK, D), bf16),
        vm((KK, 128), f32), vm((KK, 128), f32),
        vm((176, TILE_TWO), bf16), vm((720, TILE_TWO), bf16), vm((KK, TILE_TWO), bf16),
        vm((112, TILE_TWO), bf16), vm((112, TILE_TWO), bf16), vm((112, TILE_THREE), bf16),
        vm((D, 512), f32), vm((112, HID), f32), vm((D, 128), f32), vm((D, 512), f32), vm((D, 768), f32),
        vm((2, D, 128), f32), vm((D, 128), f32), vm((112, 128), f32), vm((112, 128), f32),
        vm((2, D, 128), f32), vm((9, D, 128), f32), vm((KK, D), f32), vm((KK, D), f32),
        vm((depth, 128), f32),
    ]
    whole = pl.BlockSpec(memory_space=pltpu.VMEM)
    return pl.pallas_call(
        functools.partial(image_kernel, starts, rows_of),
        out_shape=(
            jax.ShapeDtypeStruct((D, TOK), bf16),
            jax.ShapeDtypeStruct((D, TOK), bf16),
            jax.ShapeDtypeStruct((len(starts), rows_of, D), bf16),
        ),
        in_specs=[pl.BlockSpec(memory_space=pltpu.SMEM)] + [whole] * 6,
        out_specs=(whole, whole, whole),
        scratch_shapes=scratch,
        compiler_params=pltpu.CompilerParams(vmem_limit_bytes=60 * 1024 * 1024),
        name="image_step",
    )(image_side, chunks, pixels, cotangent, lane_index(), zsel, tsel)


def adam_update(gradient, master_part, first_part, second_part, average_part, step_rates):
    moment_one = beta_first * first_part + (1.0 - beta_first) * gradient
    moment_two = beta_second * second_part + (1.0 - beta_second) * gradient * gradient
    fix_one = 1.0 - beta_first**STEP
    fix_two = 1.0 - beta_second**STEP
    direction = moment_one / fix_one / (jnp.sqrt(moment_two / fix_two) + adam_eps)
    updated = master_part - step_rates * (direction + weight_decay * master_part)
    blended = average_decay * average_part + (1.0 - average_decay) * updated
    return (updated, moment_one, moment_two, blended)


def shards(tokens, image_sides, grad_out, master, first_moment, second_moment, weight_average):
    shard_len = master.shape[0]
    owners = lax.axis_size("wide")
    images_all = tokens.shape[0] * owners * lax.axis_size("narrow")
    starts = tuple((shard_len * w) // D for w in range(owners))
    rows_of = block_rows(shard_len)
    inset = lax.rem(lax.axis_index("wide") * shard_len, D)

    own = lax.dynamic_update_slice(jnp.zeros((rows_of * D,), bf16), master.astype(bf16), (inset,))
    own = jnp.broadcast_to(own.reshape(1, rows_of, D), (owners, rows_of, D))
    chunks = lax.all_to_all(own, "wide", 0, 0)

    outs, grads_in, grad_chunks = [], [], None
    for k in range(tokens.shape[0]):
        out, grad_in, chunk = image_step(starts, rows_of, chunks, tokens[k], image_sides[k : k + 1], grad_out[k])
        outs.append(out)
        grads_in.append(grad_in)
        grad_chunks = chunk if k == 0 else (grad_chunks.astype(f32) + chunk.astype(f32)).astype(bf16)
    block_out = jnp.stack(outs)
    grad_in = jnp.stack(grads_in)

    parts = lax.all_to_all(grad_chunks, "wide", 0, 0)
    total = jnp.sum(parts.astype(f32), axis=0)
    total = total + lax.ppermute(total, "narrow", [(0, 1), (1, 0)])
    reduced = lax.dynamic_slice(total.reshape(rows_of * D), (inset,), (shard_len,))
    step_rates = lax.dynamic_slice_in_dim(
        jnp.asarray(rate_values(shard_len * owners)), lax.axis_index("wide") * shard_len, shard_len
    )
    updated, moment_one, moment_two, blended = adam_update(
        reduced / images_all, master, first_moment, second_moment, weight_average, step_rates
    )
    return (block_out, grad_in, updated, moment_one, moment_two, blended)


def solution(mesh):
    return jax.shard_map(
        shards,
        mesh=mesh,
        in_specs=(
            P(("wide", "narrow"), None, None),
            P(("wide", "narrow")),
            P(("wide", "narrow"), None, None),
            P("wide"),
            P("wide"),
            P("wide"),
            P("wide"),
        ),
        out_specs=(
            P(("wide", "narrow"), None, None),
            P(("wide", "narrow"), None, None),
            P("wide"),
            P("wide"),
            P("wide"),
            P("wide"),
        ),
        check_vma=False,
    )
```

```python
import functools
import math

import jax
import jax.numpy as jnp
import numpy as np
from jax import lax
from jax.experimental import pallas as pl
from jax.experimental.pallas import tpu as pltpu
from jax.sharding import PartitionSpec as P

D = 96
HID = 384
KSTR = 4
KG = 20
STEP = 5
GRID = 80
TOK = 6400
KK = 400
REL = 159

norm_eps = 1e-06
beta_first = 0.5
beta_second = 0.5
adam_eps = 1e-08
weight_decay = 0.05
rate_factor = 0.4
average_decay = 0.8

f32 = jnp.float32
bf16 = jnp.bfloat16

HALO = 128
LEAD = 88
FIELD = LEAD + TOK + 8
TILE_ONE = 6400
TILE_TWO = 1280
TILE_THREE = 1280
SCORE_SCALE = D ** (-0.5)
LOG2E = 1.4426950408889634


def segment_list():
    return [
        ("w_qkv", (3 * D, D), D ** (-0.5)),
        ("b_qkv", (3 * D,), 0.2),
        ("pool_q", (D, 9), 1.0 / 3.0),
        ("pool_k", (D, 9), 1.0 / 3.0),
        ("pool_v", (D, 9), 1.0 / 3.0),
        ("rel_h", (REL, D), 0.5 * D ** (-0.5)),
        ("rel_w", (REL, D), 0.5 * D ** (-0.5)),
        ("w_proj", (D, D), D ** (-0.5)),
        ("b_proj", (D,), 0.2),
        ("w_fc1", (HID, D), D ** (-0.5)),
        ("b_fc1", (HID,), 0.2),
        ("w_fc2", (D, HID), HID ** (-0.5)),
        ("b_fc2", (D,), 0.2),
        ("ln1_g", (D,), 0.5),
        ("ln1_b", (D,), 0.2),
        ("ln2_g", (D,), 0.5),
        ("ln2_b", (D,), 0.2),
    ]


def row_bases():
    bases = {}
    offset = 0
    for name, shape, _ in segment_list():
        assert offset % D == 0
        bases[name] = offset // D
        offset += math.prod(shape)
    return bases


ROW = row_bases()


def rate_values(full_len):
    rates = np.full((full_len,), rate_factor * D ** (-0.5), np.float32)
    offset = 0
    for _, shape, spread in segment_list():
        length = math.prod(shape)
        rates[offset : offset + length] = rate_factor * spread
        offset += length
    return rates


def block_rows(shard_len):
    return 16 * (-(-(-(-(shard_len + D - 1) // D)) // 16))


def pool_selectors():
    flat = np.arange(9 * D).reshape(9, D)
    channel = (flat[:, None, :] // 9 == np.arange(D)[None, :, None]).astype(np.float32)
    tap = (flat[:, :, None] % 9 == np.arange(128)[None, None, :]).astype(np.float32)
    return jnp.asarray(channel, bf16), jnp.asarray(tap, bf16)


def lane_index():
    place = np.arange(-HALO, TOK + HALO)
    table = np.zeros((8, TOK + 2 * HALO), np.int32)
    table[0] = place // GRID
    table[1] = place % GRID
    return jnp.asarray(table)


def dot(a, b):
    return lax.dot_general(a, b, (((1,), (0,)), ((), ())), preferred_element_type=f32)


def dot_nt(a, b):
    return lax.dot_general(a, b, (((1,), (1,)), ((), ())), preferred_element_type=f32)


def dot_tn(a, b):
    return lax.dot_general(a, b, (((0,), (0,)), ((), ())), preferred_element_type=f32)


def normalize(values):
    mean = jnp.sum(values, axis=0, keepdims=True) * (1.0 / D)
    center = values - mean
    spread = jnp.sum(center * center, axis=0, keepdims=True) * (1.0 / D)
    inv = lax.rsqrt(spread + norm_eps)
    return center * inv, inv


def skew_rows(rows, place):
    width = rows.shape[1]
    where = jnp.broadcast_to(place, (24, width))
    residue = where & 3
    picked = jnp.where(
        residue < 2,
        jnp.where(residue == 0, rows[0:24], rows[24:48]),
        jnp.where(residue == 2, rows[48:72], rows[72:96]),
    )
    picked = jnp.where((where & 8) != 0, pltpu.roll(picked, 22, 0), picked)
    return jnp.where((where & 4) != 0, pltpu.roll(picked, 23, 0), picked)


def skew_columns(rows, place):
    width = rows.shape[1]
    where = jnp.broadcast_to(place, (40, width))
    residue = where & 3
    x = jnp.where(
        residue < 2,
        jnp.where(residue == 0, rows[0:40], rows[40:80]),
        jnp.where(residue == 2, rows[80:120], rows[120:160]),
    )
    x = jnp.concatenate([jnp.where((where[0:24] & 64) != 0, x[16:40], x[0:24]), x[24:40]], axis=0)
    x = jnp.where((where[0:32] & 32) != 0, x[8:40], x[0:32])
    where = where[0:24]
    x = jnp.where((where & 16) != 0, pltpu.roll(x, 28, 0)[0:24], x[0:24])
    x = jnp.where((where & 8) != 0, pltpu.roll(x, 22, 0), x)
    return jnp.where((where & 4) != 0, pltpu.roll(x, 23, 0), x)


def unskew_rows(x, place):
    where = jnp.broadcast_to(place, x.shape)
    x = jnp.where((where & 4) != 0, pltpu.roll(x, 1, 0), x)
    x = jnp.where((where & 8) != 0, pltpu.roll(x, 2, 0), x)
    residue = where & 3
    return jnp.concatenate([jnp.where(residue == k, x, 0.0) for k in range(4)], axis=0)


def unskew_columns(x, place):
    width = x.shape[1]
    zero = jnp.zeros((8, width), f32)
    where = jnp.broadcast_to(place, (40, width))
    x = jnp.where((where[0:24] & 4) != 0, pltpu.roll(x, 1, 0), x)
    x = jnp.where((where[0:24] & 8) != 0, pltpu.roll(x, 2, 0), x)
    x = jnp.concatenate([x, zero], axis=0)
    x = jnp.where((where[0:32] & 16) != 0, pltpu.roll(x, 4, 0), x)
    x = jnp.where((where & 32) != 0, jnp.concatenate([zero, x], axis=0), jnp.concatenate([x, zero], axis=0))
    far = (where & 64) != 0
    x = jnp.concatenate([jnp.where(far[0:16], 0.0, x[0:16]), jnp.where(far[16:40], x[0:24], x[16:40])], axis=0)
    residue = where & 3
    return jnp.concatenate([jnp.where(residue == k, x, 0.0) for k in range(4)], axis=0)


def column_row(column):
    return jnp.transpose(jnp.broadcast_to(column, (D, 128)))[0:1, :]


def two_columns(column):
    high = column.astype(bf16).astype(f32)
    place = lax.broadcasted_iota(jnp.int32, (column.shape[0], 16), 1)
    return jnp.where(place == 0, high, jnp.where(place == 1, column - high, 0.0)).astype(bf16)


def two_rows(row):
    high = row.astype(bf16).astype(f32)
    place = lax.broadcasted_iota(jnp.int32, (16, row.shape[1]), 0)
    return jnp.where(place == 0, high, jnp.where(place == 1, row - high, 0.0)).astype(bf16)


def two_ones(width):
    return jnp.where(lax.broadcasted_iota(jnp.int32, (16, width), 0) < 2, 1.0, 0.0).astype(bf16)


def image_kernel(
    starts,
    rows_of,
    side_ref,
    chunk_ref,
    x_ref,
    gy_ref,
    idx_ref,
    zsel_ref,
    tsel_ref,
    out_ref,
    gin_ref,
    gchunk_ref,
    wf, wq, wqt, wkt, wvt, wkvg, wp, wpt, w1, w1t, w2, w2t, relh, rel, relt, cols, kq, kk, kv,
    fq, fk, fv, gfk, gfv, qb, gq, gm, un, inv1, fcol,
    a1, a2, vb, vbt, kp, vpool,
    rhs, gse, aaug, n1aug, n2aug, oaug, goaug, gsh, gkv,
    dw2, dw1, dpr, gv, gkr, hacc, dwq, dwkv, kqacc, gkt, gvt, gr,
):
    side = side_ref[0]

    wf[...] = jnp.zeros(wf.shape, f32)
    for w, start in enumerate(starts):
        wf[start : start + rows_of, 0:D] += chunk_ref[w].astype(f32)

    def piece(name, count, first=0):
        base = ROW[name] + first
        return wf[base : base + count, :]

    vec_rows = [ROW["b_qkv"], ROW["b_proj"], ROW["b_fc2"], ROW["ln1_g"], ROW["ln1_b"], ROW["ln2_g"], ROW["ln2_b"]]
    vec_rows += [ROW["b_fc1"] + k for k in range(4)]
    stacked = jnp.concatenate([wf[r : r + 1, :] for r in vec_rows] + [jnp.zeros((128 - len(vec_rows), 128), f32)], axis=0)
    cols[...] = jnp.transpose(stacked)[:D, :]
    cols_low = cols[...].astype(bf16)
    g1_row, b1_row = piece("ln1_g", 1), piece("ln1_b", 1)
    g2_row, b2_row = piece("ln2_g", 1), piece("ln2_b", 1)

    def through(name, count, first, column):
        return dot(piece(name, count, first)[:, :D].astype(bf16), cols_low)[:, column : column + 1]

    wq_gain = piece("w_qkv", D) * g1_row
    wq[:, 0:D] = piece("w_qkv", D)[:, :D].astype(bf16)
    wq[:, D:] = two_columns(cols[:, 0:1])
    wqt[...] = jnp.transpose(wq_gain)[:D, :].astype(bf16)
    for k, ref in ((1, wkt), (2, wvt)):
        ref[...] = jnp.zeros(ref.shape, bf16)
        ref[0:D, 0:D] = jnp.transpose(piece("w_qkv", D, k * D))[:D, :].astype(bf16)
        ref[D:, 0:D] = two_rows(piece("b_qkv", 1, k)[:, :D])
        wkvg[:, 128 * k - 128 : 128 * k] = jnp.zeros((D, 128), bf16)
        wkvg[:, 128 * k - 128 : 128 * k - 128 + D] = jnp.transpose(piece("w_qkv", D, k * D) * g1_row)[:D, :].astype(bf16)
    wp[:, 0:D] = piece("w_proj", D)[:, :D].astype(bf16)
    wp[:, D:] = two_columns(cols[:, 1:2])
    wpt[...] = jnp.transpose(piece("w_proj", D))[:D, :].astype(bf16)
    w1_gain = piece("w_fc1", HID) * g2_row
    b_fc1 = jnp.concatenate([cols[:, 7 + k : 8 + k] for k in range(4)], axis=0)
    w1[:, 0:D] = w1_gain[:, :D].astype(bf16)
    w1[:, D:] = two_columns((b_fc1 + through("w_fc1", HID, 0, 6)) * math.sqrt(0.5))
    w1t[...] = jnp.transpose(w1_gain)[:D, :].astype(bf16)
    for k in range(4):
        block = wf[pl.ds(ROW["w_fc2"] + k, D, stride=4), :]
        w2t[k * D : (k + 1) * D, :] = jnp.transpose(block)[:D, :].astype(bf16)
    w2[:, 0:HID] = jnp.transpose(w2t[...].astype(f32)).astype(bf16)
    w2[:, HID:] = two_columns(cols[:, 2:3] * math.sqrt(0.5 * math.pi))
    for k in range(4):
        relh[k * 40 : k * 40 + 40, :] = wf[pl.ds(ROW["rel_h"] + 3 + k, 40, stride=4), :]
    rel_w = jnp.concatenate([wf[pl.ds(ROW["rel_w"] + 3 + k, 40, stride=4), :] for k in range(4)], axis=0)
    rel[D:256, :] = rel_w[:, :D].astype(bf16)
    relt[:, D:256] = jnp.transpose(rel_w)[:D, :].astype(bf16)

    def pool_columns(name):
        total = jnp.zeros((D, 128), f32)
        for i in range(9):
            row = wf[ROW[name] + i : ROW[name] + i + 1, :][:, :D]
            total = total + dot((zsel_ref[i].astype(f32) * row).astype(bf16), tsel_ref[i])
        return total

    def pool_rows(name):
        full = jnp.concatenate([pool_columns(name), jnp.zeros((32, 128), f32)], axis=0)
        return jnp.transpose(full)[0:16, :]

    pooled_kernel = pool_columns("pool_q")
    for k in range(9):
        kq[k] = jnp.broadcast_to(pooled_kernel[:, k : k + 1], (D, 128))

    def tap(k, ch, width):
        return jnp.concatenate([kq[k, ch, :]] * (width // 128), axis=1)

    kk[...] = pool_rows("pool_k")
    kv[...] = pool_rows("pool_v")

    for ref in (fq, gq):
        ref[:, 0:HALO] = jnp.zeros((D, HALO), f32)
        ref[:, HALO + TOK :] = jnp.zeros((D, HALO), f32)
    for ref in (fk, fv):
        ref[0:LEAD, :] = jnp.zeros((LEAD, 128), f32)
    for ref in (dw2, dw1, dpr, gv, gkr, dwq, dwkv, kqacc):
        ref[...] = jnp.zeros(ref.shape, ref.dtype)
    gr[ROW["rel_h"] : ROW["w_proj"], :] = jnp.zeros((2 * REL, 128), f32)
    tail = ROW["ln2_b"]
    gr[tail:, :] = jnp.zeros((gr.shape[0] - tail, 128), f32)

    un[D:, :] = two_ones(TOK)
    n1aug[D:, :] = two_ones(TILE_ONE)
    n2aug[D:, :] = two_ones(TILE_TWO)
    oaug[D:, :] = two_ones(TILE_TWO)
    aaug[HID:, :] = two_ones(TILE_TWO)
    rhs[192:208, :] = two_ones(TILE_TWO)

    def window(i, tile):
        return pl.ds(pl.multiple_of(i * tile, 128), tile + 2 * HALO)

    def inner(i, tile):
        return pl.ds(pl.multiple_of(i * tile + HALO, 128), tile)

    def plain(i, tile):
        return pl.ds(pl.multiple_of(i * tile, 128), tile)

    def token_mask(i, tile):
        place = idx_ref[0:2, inner(i, tile)]
        return jnp.where((place[0:1] < side) & (place[1:2] < side), 1.0, 0.0)

    def project(i, carry):
        here = plain(i, TILE_ONE)
        unit, inv = normalize(x_ref[:, here].astype(f32))
        un[0:D, here] = unit.astype(bf16)
        inv1[0:1, here] = inv
        n1aug[0:D, :] = (unit * cols[:, 3:4] + cols[:, 4:5]).astype(bf16)
        fq[:, inner(i, TILE_ONE)] = dot(wq[...], n1aug[...]) * token_mask(i, TILE_ONE)
        field = pl.ds(pl.multiple_of(i * TILE_ONE + LEAD, 8), TILE_ONE)
        fk[field, :] = dot_tn(n1aug[...], wkt[...])
        fv[field, :] = dot_tn(n1aug[...], wvt[...])
        return carry

    lax.fori_loop(0, TOK // TILE_ONE, project, 0)

    def pool_queries(i, carry):
        tile = TILE_ONE
        wide = tile + 2 * HALO
        mid = slice(HALO, HALO + tile)
        col = jnp.broadcast_to(idx_ref[1:2, window(i, tile)], (8, wide))
        first, last = col == 0, col == GRID - 1
        mask = token_mask(i, tile)
        for pair in range(D // 16):
            pooled, moved = [], []
            for half in range(2):
                ch = slice(16 * pair + 8 * half, 16 * pair + 8 * half + 8)
                field = fq[ch, window(i, tile)]
                left = jnp.where(first, 0.0, pltpu.roll(field, 1, 1))
                right = jnp.where(last, 0.0, pltpu.roll(field, wide - 1, 1))

                def row_sum(u):
                    return tap(3 * u, ch, wide) * left + tap(3 * u + 1, ch, wide) * field + tap(3 * u + 2, ch, wide) * right

                total = pltpu.roll(row_sum(0), GRID, 1) + row_sum(1) + pltpu.roll(row_sum(2), wide - GRID, 1)
                pooled.append(total[:, mid] * mask)
                moved.append((left[:, mid], field[:, mid], right[:, mid]))
            qb[16 * pair : 16 * pair + 16, plain(i, tile)] = jnp.concatenate(pooled, axis=0).astype(bf16)
            for v in range(3):
                both = jnp.concatenate([moved[0][v], moved[1][v]], axis=0)
                fcol[v * D + 16 * pair : v * D + 16 * pair + 16, plain(i, tile)] = both.astype(bf16)
        return carry

    lax.fori_loop(0, TOK // TILE_ONE, pool_queries, 0)

    b_index = lax.broadcasted_iota(jnp.int32, (KG, 128), 0)

    def tap_start(a, u, v):
        return LEAD + GRID * (KSTR * a + u - 1) + v - 1

    def tap_rows(kernel_rows):
        taps = [jnp.broadcast_to(kernel_rows[k : k + 1, :], (KG, 128)) for k in range(9)]
        return [jnp.where(b_index == 0, 0.0, tap) if k % 3 == 0 else tap for k, tap in enumerate(taps)]

    for field, kernel_rows, pooled in ((fk, kk, kp), (fv, kv, vpool)):
        taps = tap_rows(kernel_rows)
        for a in range(KG):
            total = jnp.zeros((KG, 128), f32)
            for k in range(9):
                total = total + taps[k] * field[pl.ds(tap_start(a, k // 3, k % 3), KG, stride=KSTR), :]
            keep = (KSTR * b_index < side) & (KSTR * a < side)
            pooled[KG * a : KG * a + KG, :] = jnp.where(keep, total, 0.0)

    key = lax.broadcasted_iota(jnp.int32, (KK, 112), 0)
    key_a = lax.div(key, KG)
    key_b = key - KG * key_a
    place = lax.broadcasted_iota(jnp.int32, (KK, 112), 1)
    hot = jnp.zeros((KK, 112), f32)
    for base in (0, 48):
        one_a = (place >= base) & (place < base + 24) & (KG - 1 - key_a == place - base)
        one_b = (place >= base + 24) & (place < base + 48) & (KG - 1 - key_b == place - base - 24)
        hot = jnp.where(one_a | one_b, 1.0, hot)
    shut = (place == 96) & ((KSTR * key_a >= side) | (KSTR * key_b >= side))
    a1[:, 0:D] = kp[...][:, :D].astype(bf16)
    a1[:, D:] = jnp.where(shut, -1e30, hot).astype(bf16)
    vbt[:, 0:D] = vpool[...][:, :D].astype(bf16)
    vbt[:, D:] = jnp.where(lax.broadcasted_iota(jnp.int32, (KK, 16), 1) < 2, -1.0, 0.0).astype(bf16)
    a2[0:D, :] = jnp.transpose(kp[...])[:D, :].astype(bf16)
    vb[0:D, :] = jnp.transpose(vpool[...])[:D, :].astype(bf16)
    vb[D:, :] = jnp.ones((16, KK), bf16)
    key_l = lax.broadcasted_iota(jnp.int32, (48, KK), 1)
    a_l = lax.div(key_l, KG)
    b_l = key_l - KG * a_l
    row_l = lax.broadcasted_iota(jnp.int32, (48, KK), 0)
    hot_l = ((row_l < 24) & (KG - 1 - a_l == row_l)) | ((row_l >= 24) & (KG - 1 - b_l == row_l - 24))
    a2[D:, :] = jnp.where(hot_l, 1.0, 0.0).astype(bf16)

    def attend(i, carry):
        tile = TILE_TWO
        here = plain(i, tile)
        mask = token_mask(i, tile)
        row, col = idx_ref[0:1, inner(i, tile)], idx_ref[1:2, inner(i, tile)]
        near = jnp.concatenate([relh[pl.ds(40 * k + 4 * i, 24), :] for k in range(4)], axis=0)
        rel[0:D, :] = near[:, :D].astype(bf16)
        relt[:, 0:D] = jnp.transpose(near)[:D, :].astype(bf16)
        q = qb[:, here]
        seen = dot(rel[...], q)
        rhs[0:D, :] = q
        sides = jnp.concatenate([skew_rows(seen[0:D], row), skew_columns(seen[D:256], col)], axis=0)
        sides = sides * math.sqrt(D)
        sides_low = sides.astype(bf16)
        rhs[D : D + 48, :] = sides_low
        rhs[D + 48 : D + 96, :] = (sides - sides_low.astype(f32)).astype(bf16)
        scores = dot(a1[...], rhs[...])
        weight = jnp.exp2((scores - jnp.max(scores, axis=0, keepdims=True)) * (SCORE_SCALE * LOG2E))
        weight_low = weight.astype(bf16)
        mixed = dot(vb[...], weight_low)
        inv_sum = 1.0 / mixed[D : D + 1]
        mixed = mixed[0:D] * inv_sum
        oaug[0:D, :] = (mixed + q.astype(f32)).astype(bf16)
        middle = x_ref[:, here].astype(f32) + dot(wp[...], oaug[...])

        center = middle - jnp.sum(middle, axis=0, keepdims=True) * (1.0 / D)
        inv = lax.rsqrt(jnp.sum(center * center, axis=0, keepdims=True) * (1.0 / D) + norm_eps)
        half = center * (inv * math.sqrt(0.5))
        n2aug[0:D, :] = half.astype(bf16)
        z = dot(w1[...], n2aug[...])
        below = lax.erf(z) * (0.5 * math.sqrt(math.pi)) + 0.5 * math.sqrt(math.pi)
        aaug[0:HID, :] = (z * below).astype(bf16)
        slope = below + z * jnp.exp2((z * z) * -LOG2E)
        mlp = dot(w2[...], aaug[...])
        out_ref[:, here] = ((middle + mlp * math.sqrt(2.0 / math.pi)) * mask).astype(bf16)

        gy = gy_ref[:, here].astype(f32) * mask
        gy_low = gy.astype(bf16)
        dw2[:, 0:KK] += dot_nt(gy_low, aaug[...])
        gh_low = (slope * dot(w2t[...], gy_low)).astype(bf16)
        dw1[0:112, :] += dot_nt(n2aug[...], gh_low)
        gn = dot(w1t[...], gh_low)
        mean = jnp.sum(gn, axis=0, keepdims=True) * (1.0 / D)
        along = jnp.sum(gn * half, axis=0, keepdims=True) * (2.0 / D)
        gmid = gy + (gn - mean - half * along) * (inv * math.sqrt(1.0 / math.pi))
        gm[:, here] = gmid
        gm_low = gmid.astype(bf16)
        dpr[:, 0:112] += dot_nt(gm_low, oaug[...])
        go = dot(wpt[...], gm_low)
        go_low = (go * inv_sum).astype(bf16)
        goaug[0:D, :] = go_low
        goaug[D:, :] = two_rows(jnp.sum(go_low.astype(f32) * mixed, axis=0, keepdims=True))
        gv[0:D, 0:KK] += dot_nt(go_low, weight_low)
        gse[0:KK, :] = (weight * dot(vbt[...], goaug[...])).astype(bf16)
        back = dot(a2[...], gse[0:KK, :])
        gse[KK : KK + D, :] = unskew_rows(back[D : D + 24], row).astype(bf16)
        gse[KK + D : KK + 256, :] = unskew_columns(back[D + 24 : D + 48], col).astype(bf16)
        flat = pl.ds(pl.multiple_of(i * tile + LEAD, 8), tile)
        gfk[flat, :] = jnp.zeros((tile, 128), f32)
        gfv[flat, :] = jnp.zeros((tile, 128), f32)
        outer = dot_nt(q, gse[...])
        gkr[0:D, 0 : KK + 256] += outer
        hacc[i] = outer[:, 384:512]
        gq[:, inner(i, tile)] = go + SCORE_SCALE * back[0:D] + dot(relt[...], gse[KK : KK + 256, :])
        return carry

    lax.fori_loop(0, TOK // TILE_TWO, attend, 0)

    gkt[...] = jnp.transpose(gkr[:, 0:512])[0:KK, :] * SCORE_SCALE
    gvt[...] = jnp.transpose(gv[...])[0:KK, :]

    def pool_gradient(name, columns):
        low = columns.astype(bf16)
        for i in range(9):
            spread = dot_nt(low, tsel_ref[i]) * zsel_ref[i].astype(f32)
            gr[ROW[name] + i : ROW[name] + i + 1, 0:D] = jnp.sum(spread, axis=0, keepdims=True)

    for field, kernel_rows, pooled, gfield, name in ((fk, kk, gkt, gfk, "pool_k"), (fv, kv, gvt, gfv, "pool_v")):
        taps = tap_rows(kernel_rows)
        sums = [jnp.zeros((KG, 128), f32) for _ in range(9)]
        for a in range(KG):
            grad = pooled[KG * a : KG * a + KG, :]
            inside = jnp.where(b_index == 0, 0.0, grad)
            for k in range(9):
                where = pl.ds(tap_start(a, k // 3, k % 3), KG, stride=KSTR)
                sums[k] = sums[k] + (inside if k % 3 == 0 else grad) * field[where, :]
                gfield[where, :] = taps[k] * grad
        rows = [jnp.sum(total, axis=0, keepdims=True) for total in sums]
        rows = jnp.concatenate(rows + [jnp.zeros((128 - 9, 128), f32)], axis=0)
        pool_gradient(name, jnp.transpose(rows)[:D, :])

    def finish(i, carry):
        tile = TILE_THREE
        wide = tile + 2 * HALO
        here = plain(i, tile)
        mid = slice(HALO, HALO + tile)
        mask = token_mask(i, tile)
        col = jnp.broadcast_to(idx_ref[1:2, inner(i, tile)], (8, tile))
        first, last = col == 0, col == GRID - 1
        for pair in range(D // 16):
            fields, moved = [], []
            for half in range(2):
                ch = slice(16 * pair + 8 * half, 16 * pair + 8 * half + 8)
                grad = gq[ch, window(i, tile)]
                below, above = pltpu.roll(grad, wide - GRID, 1), pltpu.roll(grad, GRID, 1)

                def col_sum(v):
                    return tap(v, ch, wide) * below + tap(v + 3, ch, wide) * grad + tap(v + 6, ch, wide) * above

                after = jnp.where(last, 0.0, pltpu.roll(col_sum(0), wide - 1, 1)[:, mid])
                before = jnp.where(first, 0.0, pltpu.roll(col_sum(2), 1, 1)[:, mid])
                fields.append((after + col_sum(1)[:, mid] + before) * mask)
                moved.append((below[:, mid], grad[:, mid], above[:, mid]))
            gsh[3 * D + 16 * pair : 3 * D + 16 * pair + 16, :] = jnp.concatenate(fields, axis=0).astype(bf16)
            for u in range(3):
                both = jnp.concatenate([moved[0][u], moved[1][u]], axis=0)
                gsh[u * D + 16 * pair : u * D + 16 * pair + 16, :] = both.astype(bf16)
        kqacc[:, 0 : 3 * D] += dot_nt(gsh[0 : 3 * D, :], fcol[:, here])
        gq_low = gsh[3 * D : 4 * D, :]
        flat = pl.ds(pl.multiple_of(i * tile + LEAD, 8), tile)
        gkv[:, 0:128] = gfk[flat, :].astype(bf16)
        gkv[:, 128:256] = gfv[flat, :].astype(bf16)
        dwq[:, 0:112] += dot_nt(gq_low, un[:, here])
        dwkv[0:112, :] += dot(un[:, here], gkv[...])
        gn = dot(wqt[...], gq_low) + dot_nt(wkvg[...], gkv[...])
        unit = un[0:D, here].astype(f32)
        mean = jnp.sum(gn, axis=0, keepdims=True) * (1.0 / D)
        along = jnp.sum(gn * unit, axis=0, keepdims=True) * (1.0 / D)
        gin_ref[:, here] = (gm[:, here] + (gn - mean - unit * along) * inv1[0:1, here]).astype(bf16)
        return carry

    lax.fori_loop(0, TOK // TILE_THREE, finish, 0)

    def write(name, rows, first=0):
        base = ROW[name] + first
        gr[base : base + rows.shape[0], 0:D] = rows

    def wide_rows(rows):
        return jnp.concatenate([rows, jnp.zeros((rows.shape[0], 128 - D), f32)], axis=1)

    def through_norm(name, first, outer, bias, gain_row, shift_row):
        raw = piece(name, outer.shape[0], first)[:, :D]
        write(name, outer * gain_row[:, :D] + bias * shift_row[:, :D], first)
        return jnp.sum(raw * outer, axis=0, keepdims=True), jnp.sum(raw * bias, axis=0, keepdims=True)

    gain, shift = through_norm("w_qkv", 0, dwq[:, 0:D], dwq[:, D : D + 1], g1_row, b1_row)
    write("b_qkv", jnp.transpose(dwq[...])[D : D + 1, :])
    for k in (1, 2):
        turned = jnp.transpose(dwkv[:, 128 * k - 128 : 128 * k])[0:D, :]
        more_gain, more_shift = through_norm("w_qkv", k * D, turned[:, 0:D], turned[:, D : D + 1], g1_row, b1_row)
        gain, shift = gain + more_gain, shift + more_shift
        write("b_qkv", dwkv[D : D + 1, 128 * k - 128 : 128 * k - 128 + D], k)
    write("ln1_g", gain)
    write("ln1_b", shift)

    lane = lax.broadcasted_iota(jnp.int32, (D, 128), 1)
    wide_lane = lax.broadcasted_iota(jnp.int32, (D, 3 * 128), 1) - lax.broadcasted_iota(jnp.int32, (D, 3 * 128), 0)
    columns = jnp.zeros((D, 128), f32)
    for k in range(9):
        u, v = k // 3, k % 3
        one = jnp.where(wide_lane == v * D, kqacc[u * D : u * D + D, :], 0.0)
        columns = jnp.where(lane == k, jnp.sum(one, axis=1, keepdims=True), columns)
    pool_gradient("pool_q", columns)

    for i in range(TOK // TILE_TWO):
        turned = jnp.transpose(hacc[i])
        for k in range(4):
            where = pl.ds(ROW["rel_h"] + 3 + k + 16 * i, 23, stride=4)
            gr[where, :] = gr[where, :] + wide_rows(turned[16 + 24 * k : 39 + 24 * k])
    turned = jnp.transpose(gkr[0:D, 384:768])
    for k in range(4):
        gr[pl.ds(ROW["rel_w"] + 3 + k, 39, stride=4), :] = wide_rows(turned[112 + 40 * k : 151 + 40 * k])

    write("w_proj", dpr[:, 0:D])
    write("b_proj", jnp.transpose(dpr[...])[D : D + 1, :])
    turned = jnp.transpose(dw1[...])
    gain, shift = through_norm(
        "w_fc1", 0, turned[:, 0:D] * math.sqrt(2.0 / math.pi), turned[:, D : D + 1] * math.sqrt(1.0 / math.pi), g2_row, b2_row
    )
    write("ln2_g", gain)
    write("ln2_b", shift)
    for k in range(4):
        write("b_fc1", dw1[D : D + 1, k * D : (k + 1) * D] * math.sqrt(1.0 / math.pi), k)
        gr[pl.ds(ROW["w_fc2"] + k, D, stride=4), :] = wide_rows(dw2[:, k * D : (k + 1) * D] * math.sqrt(2.0 / math.pi))
    write("b_fc2", jnp.transpose(dw2[:, HID:512])[0:1, :])
    for w, start in enumerate(starts):
        gchunk_ref[w] = gr[start : start + rows_of, 0:D].astype(bf16)


def image_step(starts, rows_of, chunks, pixels, image_side, cotangent):
    depth = 8 * (-(-(starts[-1] + rows_of) // 8))
    zsel, tsel = pool_selectors()
    vm = pltpu.VMEM
    scratch = [
        vm((depth, 128), f32),
        vm((D, 112), bf16), vm((D, D), bf16), vm((112, 128), bf16), vm((112, 128), bf16), vm((D, 256), bf16),
        vm((D, 112), bf16), vm((D, D), bf16),
        vm((HID, 112), bf16), vm((D, HID), bf16), vm((D, KK), bf16), vm((HID, D), bf16),
        vm((160, 128), f32), vm((256, D), bf16), vm((D, 256), bf16),
        vm((D, 128), f32), vm((9, D, 128), f32), vm((16, 128), f32), vm((16, 128), f32),
        vm((D, TOK + 2 * HALO), f32), vm((FIELD, 128), f32), vm((FIELD, 128), f32),
        vm((FIELD, 128), f32), vm((FIELD, 128), f32),
        vm((D, TOK), bf16), vm((D, TOK + 2 * HALO), f32), vm((D, TOK), f32),
        vm((112, TOK), bf16), vm((8, TOK), f32), vm((3 * D, TOK), bf16),
        vm((KK, 208), bf16), vm((144, KK), bf16), vm((112, KK), bf16), vm((KK, 112), bf16),
        vm((KK, 128), f32), vm((KK, 128), f32),
        vm((208, TILE_TWO), bf16), vm((KK + 256, TILE_TWO), bf16), vm((KK, TILE_TWO), bf16),
        vm((112, TILE_ONE), bf16), vm((112, TILE_TWO), bf16), vm((112, TILE_TWO), bf16), vm((112, TILE_TWO), bf16),
        vm((4 * D, TILE_THREE), bf16), vm((TILE_THREE, 256), bf16),
        vm((D, 512), f32), vm((128, HID), f32), vm((D, 128), f32), vm((128, 512), f32), vm((128, 768), f32),
        vm((TOK // TILE_TWO, D, 128), f32),
        vm((D, 128), f32), vm((128, 256), f32), vm((3 * D, 3 * 128), f32), vm((KK, 128), f32), vm((KK, 128), f32),
        vm((depth, 128), f32),
    ]
    whole = pl.BlockSpec(memory_space=pltpu.VMEM)
    return pl.pallas_call(
        functools.partial(image_kernel, starts, rows_of),
        out_shape=(
            jax.ShapeDtypeStruct((D, TOK), bf16),
            jax.ShapeDtypeStruct((D, TOK), bf16),
            jax.ShapeDtypeStruct((len(starts), rows_of, D), bf16),
        ),
        in_specs=[pl.BlockSpec(memory_space=pltpu.SMEM)] + [whole] * 6,
        out_specs=(whole, whole, whole),
        scratch_shapes=scratch,
        compiler_params=pltpu.CompilerParams(vmem_limit_bytes=63 * 1024 * 1024),
        name="image_step",
    )(image_side, chunks, pixels, cotangent, lane_index(), zsel, tsel)


def adam_update(gradient, master_part, first_part, second_part, average_part, step_rates):
    moment_one = beta_first * first_part + (1.0 - beta_first) * gradient
    moment_two = beta_second * second_part + (1.0 - beta_second) * gradient * gradient
    fix_one = 1.0 - beta_first**STEP
    fix_two = 1.0 - beta_second**STEP
    direction = moment_one / fix_one / (jnp.sqrt(moment_two / fix_two) + adam_eps)
    updated = master_part - step_rates * (direction + weight_decay * master_part)
    blended = average_decay * average_part + (1.0 - average_decay) * updated
    return (updated, moment_one, moment_two, blended)


def shards(tokens, image_sides, grad_out, master, first_moment, second_moment, weight_average):
    shard_len = master.shape[0]
    owners = lax.axis_size("wide")
    images_all = tokens.shape[0] * owners * lax.axis_size("narrow")
    starts = tuple((shard_len * w) // D for w in range(owners))
    rows_of = block_rows(shard_len)
    inset = lax.rem(lax.axis_index("wide") * shard_len, D)

    own = lax.dynamic_update_slice(jnp.zeros((rows_of * D,), bf16), master.astype(bf16), (inset,))
    own = jnp.broadcast_to(own.reshape(1, rows_of, D), (owners, rows_of, D))
    chunks = lax.all_to_all(own, "wide", 0, 0)

    outs, grads_in, grad_chunks = [], [], None
    for k in range(tokens.shape[0]):
        out, grad_in, chunk = image_step(starts, rows_of, chunks, tokens[k], image_sides[k : k + 1], grad_out[k])
        outs.append(out)
        grads_in.append(grad_in)
        grad_chunks = chunk if k == 0 else (grad_chunks.astype(f32) + chunk.astype(f32)).astype(bf16)
    block_out = jnp.stack(outs)
    grad_in = jnp.stack(grads_in)

    parts = lax.all_to_all(grad_chunks, "wide", 0, 0)
    total = jnp.sum(parts.astype(f32), axis=0)
    total = total + lax.ppermute(total, "narrow", [(0, 1), (1, 0)])
    reduced = lax.dynamic_slice(total.reshape(rows_of * D), (inset,), (shard_len,))
    step_rates = lax.dynamic_slice_in_dim(
        jnp.asarray(rate_values(shard_len * owners)), lax.axis_index("wide") * shard_len, shard_len
    )
    updated, moment_one, moment_two, blended = adam_update(
        reduced / images_all, master, first_moment, second_moment, weight_average, step_rates
    )
    return (block_out, grad_in, updated, moment_one, moment_two, blended)


def solution(mesh):
    return jax.shard_map(
        shards,
        mesh=mesh,
        in_specs=(
            P(("wide", "narrow"), None, None),
            P(("wide", "narrow")),
            P(("wide", "narrow"), None, None),
            P("wide"),
            P("wide"),
            P("wide"),
            P("wide"),
        ),
        out_specs=(
            P(("wide", "narrow"), None, None),
            P(("wide", "narrow"), None, None),
            P("wide"),
            P("wide"),
            P("wide"),
            P("wide"),
        ),
        check_vma=False,
    )
```

```python
import functools
import math

import jax
import jax.numpy as jnp
import numpy as np
from jax import lax
from jax.experimental import pallas as pl
from jax.experimental.pallas import tpu as pltpu
from jax.sharding import PartitionSpec as P

D = 96
HID = 384
KSTR = 4
KG = 20
STEP = 5
GRID = 80
TOK = 6400
KK = 400
REL = 159

norm_eps = 1e-06
beta_first = 0.5
beta_second = 0.5
adam_eps = 1e-08
weight_decay = 0.05
rate_factor = 0.4
average_decay = 0.8

f32 = jnp.float32
bf16 = jnp.bfloat16

HALO = 128
LEAD = 88
FIELD = LEAD + TOK + 8
TILE_ONE = 6400
TILE_TWO = 1280
TILE_THREE = 1280
TILES = TOK // TILE_TWO
TILE_ROWS = TILE_TWO // GRID
ROW_STEPS = TILE_ROWS // KSTR
SCORE_SCALE = D ** (-0.5)
LOG2E = 1.4426950408889634


def segment_list():
    return [
        ("w_qkv", (3 * D, D), D ** (-0.5)),
        ("b_qkv", (3 * D,), 0.2),
        ("pool_q", (D, 9), 1.0 / 3.0),
        ("pool_k", (D, 9), 1.0 / 3.0),
        ("pool_v", (D, 9), 1.0 / 3.0),
        ("rel_h", (REL, D), 0.5 * D ** (-0.5)),
        ("rel_w", (REL, D), 0.5 * D ** (-0.5)),
        ("w_proj", (D, D), D ** (-0.5)),
        ("b_proj", (D,), 0.2),
        ("w_fc1", (HID, D), D ** (-0.5)),
        ("b_fc1", (HID,), 0.2),
        ("w_fc2", (D, HID), HID ** (-0.5)),
        ("b_fc2", (D,), 0.2),
        ("ln1_g", (D,), 0.5),
        ("ln1_b", (D,), 0.2),
        ("ln2_g", (D,), 0.5),
        ("ln2_b", (D,), 0.2),
    ]


def row_bases():
    bases = {}
    offset = 0
    for name, shape, _ in segment_list():
        assert offset % D == 0
        bases[name] = offset // D
        offset += math.prod(shape)
    return bases


ROW = row_bases()


def rate_values(full_len):
    rates = np.full((full_len,), rate_factor * D ** (-0.5), np.float32)
    offset = 0
    for _, shape, spread in segment_list():
        length = math.prod(shape)
        rates[offset : offset + length] = rate_factor * spread
        offset += length
    return rates


def block_rows(shard_len):
    return 16 * (-(-(-(-(shard_len + D - 1) // D)) // 16))


def pool_selectors():
    flat = np.arange(9 * D).reshape(9, D)
    channel = (flat[:, None, :] // 9 == np.arange(D)[None, :, None]).astype(np.float32)
    tap = (flat[:, :, None] % 9 == np.arange(128)[None, None, :]).astype(np.float32)
    return jnp.asarray(channel, bf16), jnp.asarray(tap, bf16)


def lane_index():
    place = np.arange(-HALO, TOK + HALO)
    table = np.zeros((8, TOK + 2 * HALO), np.int32)
    table[0] = place // GRID
    table[1] = place % GRID
    return jnp.asarray(table)


def dot(a, b):
    return lax.dot_general(a, b, (((1,), (0,)), ((), ())), preferred_element_type=f32)


def dot_nt(a, b):
    return lax.dot_general(a, b, (((1,), (1,)), ((), ())), preferred_element_type=f32)


def dot_tn(a, b):
    return lax.dot_general(a, b, (((0,), (0,)), ((), ())), preferred_element_type=f32)


def normalize(values):
    mean = jnp.sum(values, axis=0, keepdims=True) * (1.0 / D)
    center = values - mean
    spread = jnp.sum(center * center, axis=0, keepdims=True) * (1.0 / D)
    inv = lax.rsqrt(spread + norm_eps)
    return center * inv, inv


def skew_rows(rows, place):
    width = rows.shape[1]
    where = jnp.broadcast_to(place, (24, width))
    residue = where & 3
    x = jnp.where(
        residue < 2,
        jnp.where(residue == 0, rows[0:24], rows[24:48]),
        jnp.where(residue == 2, rows[48:72], rows[72:96]),
    )
    step = ROW_STEPS // 2
    while step >= 1:
        x = jnp.where((where & (4 * step)) != 0, pltpu.roll(x, 24 - step, 0), x)
        step //= 2
    return x


def skew_columns(rows, place):
    width = rows.shape[1]
    where = jnp.broadcast_to(place, (40, width))
    residue = where & 3
    x = jnp.where(
        residue < 2,
        jnp.where(residue == 0, rows[0:40], rows[40:80]),
        jnp.where(residue == 2, rows[80:120], rows[120:160]),
    )
    x = jnp.concatenate([jnp.where((where[0:24] & 64) != 0, x[16:40], x[0:24]), x[24:40]], axis=0)
    x = jnp.where((where[0:32] & 32) != 0, x[8:40], x[0:32])
    where = where[0:24]
    x = jnp.where((where & 16) != 0, pltpu.roll(x, 28, 0)[0:24], x[0:24])
    x = jnp.where((where & 8) != 0, pltpu.roll(x, 22, 0), x)
    return jnp.where((where & 4) != 0, pltpu.roll(x, 23, 0), x)


def unskew_rows(x, place):
    where = jnp.broadcast_to(place, x.shape)
    step = 1
    while step < ROW_STEPS:
        x = jnp.where((where & (4 * step)) != 0, pltpu.roll(x, step, 0), x)
        step *= 2
    residue = where & 3
    return jnp.concatenate([jnp.where(residue == k, x, 0.0) for k in range(4)], axis=0)


def unskew_columns(x, place):
    width = x.shape[1]
    zero = jnp.zeros((8, width), f32)
    where = jnp.broadcast_to(place, (40, width))
    x = jnp.where((where[0:24] & 4) != 0, pltpu.roll(x, 1, 0), x)
    x = jnp.where((where[0:24] & 8) != 0, pltpu.roll(x, 2, 0), x)
    x = jnp.concatenate([x, zero], axis=0)
    x = jnp.where((where[0:32] & 16) != 0, pltpu.roll(x, 4, 0), x)
    x = jnp.where((where & 32) != 0, jnp.concatenate([zero, x], axis=0), jnp.concatenate([x, zero], axis=0))
    far = (where & 64) != 0
    x = jnp.concatenate([jnp.where(far[0:16], 0.0, x[0:16]), jnp.where(far[16:40], x[0:24], x[16:40])], axis=0)
    residue = where & 3
    return jnp.concatenate([jnp.where(residue == k, x, 0.0) for k in range(4)], axis=0)


def aligned(value, step):
    return value if isinstance(value, int) else pl.multiple_of(value, step)


def interleave(*parts):
    live = list(parts)
    while live:
        for part in list(live):
            if next(part, None) is None:
                live.remove(part)


def two_columns(column):
    high = column.astype(bf16).astype(f32)
    place = lax.broadcasted_iota(jnp.int32, (column.shape[0], 16), 1)
    return jnp.where(place == 0, high, jnp.where(place == 1, column - high, 0.0)).astype(bf16)


def two_rows(row):
    high = row.astype(bf16).astype(f32)
    place = lax.broadcasted_iota(jnp.int32, (16, row.shape[1]), 0)
    return jnp.where(place == 0, high, jnp.where(place == 1, row - high, 0.0)).astype(bf16)


def two_ones(width):
    return jnp.where(lax.broadcasted_iota(jnp.int32, (16, width), 0) < 2, 1.0, 0.0).astype(bf16)


def key_columns():
    return lax.broadcasted_iota(jnp.int32, (KG, 128), 0)


def tap_start(a, u, v):
    return LEAD + GRID * (KSTR * a + u - 1) + v - 1


def tap_rows(kernel_rows):
    b_index = key_columns()
    taps = [jnp.broadcast_to(kernel_rows[k : k + 1, :], (KG, 128)) for k in range(9)]
    return [jnp.where(b_index == 0, 0.0, tap) if k % 3 == 0 else tap for k, tap in enumerate(taps)]


def spread_keys(taps, grad, a, gfield):
    idle = LEAD + GRID * (KSTR * a + 2)
    gfield[idle - 8 : idle + GRID, :] = jnp.zeros((GRID + 8, 128), f32)
    for u in range(3):
        gfield[pl.ds(tap_start(a, u, 3), KG, stride=KSTR), :] = jnp.zeros((KG, 128), f32)
    for k in range(9):
        gfield[pl.ds(tap_start(a, k // 3, k % 3), KG, stride=KSTR), :] = taps[k] * grad
    if a == KG - 1:
        gfield[LEAD + TOK - GRID : LEAD + TOK, :] = jnp.zeros((GRID, 128), f32)


def input_kernel(*refs):
    sources, gin_hbm, held = refs[:10], refs[10], refs[11:21]
    field_ref, mid_ref, unit_ref, inv_ref, gkt, gvt, kk, kv, wqt, wkvg = held
    gin_ref, gfk, gfv, gkv, copy_sem = refs[21:]
    copies = [pltpu.make_async_copy(a, b, copy_sem.at[k]) for k, (a, b) in enumerate(zip(sources, held))]
    for copy in copies[::-1]:
        copy.start()
    for copy in copies[4:]:
        copy.wait()
    for kernel_rows, pooled, gfield in ((kk, gkt, gfk), (kv, gvt, gfv)):
        taps = tap_rows(kernel_rows)
        for a in range(KG):
            spread_keys(taps, pooled[KG * a : KG * a + KG, :], a, gfield)
    for copy in copies[:4]:
        copy.wait()

    def gin_copy(i):
        here = pl.ds(aligned(i * TILE_THREE, 128), TILE_THREE)
        return pltpu.make_async_copy(gin_ref.at[:, here], gin_hbm.at[:, here], copy_sem.at[10 + i])

    def finish(i, carry):
        tile = TILE_THREE
        here = pl.ds(aligned(i * tile, 128), tile)
        flat = pl.ds(aligned(i * tile + LEAD, 8), tile)
        gkv[:, 0:128] = gfk[flat, :].astype(bf16)
        gkv[:, 128:256] = gfv[flat, :].astype(bf16)
        gn = dot(wqt[...], field_ref[:, here]) + dot_nt(wkvg[...], gkv[...])
        unit = unit_ref[:, here].astype(f32)
        mean = jnp.sum(gn, axis=0, keepdims=True) * (1.0 / D)
        along = jnp.sum(gn * unit, axis=0, keepdims=True) * (1.0 / D)
        total = mid_ref[:, here].astype(f32) + (gn - mean - unit * along) * inv_ref[0:1, here]
        gin_ref[:, here] = total.astype(bf16)
        gin_copy(i).start()
        return carry

    lax.fori_loop(0, TOK // TILE_THREE, finish, 0)
    for i in range(TOK // TILE_THREE):
        gin_copy(i).wait()


def image_kernel(
    starts,
    rows_of,
    side_ref,
    chunk_ref,
    x_hbm,
    gy_hbm,
    idx_ref,
    zsel_ref,
    tsel_ref,
    out_hbm,
    gchunk_ref,
    field_hbm,
    mid_hbm,
    unit_hbm,
    inv_ref,
    gkt,
    gvt,
    kk,
    kv,
    wqt,
    wkvg,
    wf, wq, wkt, wvt, wp, wpt, w1, w1t, w2, w2t, relh, rel, relt, cols, kq,
    fq, fk, fv, gfk, gfv, qb, gq, gm, un, fcol,
    a1, a2, vb, vbt, kp, vpool,
    rhs, gse, n1aug, goaug, gsh, gkv,
    dw2, dw1, dpr, gv, gkr, hacc, dwq, dwkv, kqacc, gr, x_ref, gy_ref, out_ref, gfield, copy_sem,
    *slot_refs,
):
    slots = (slot_refs[: len(slot_refs) // 2], slot_refs[len(slot_refs) // 2 :])
    side = side_ref[0]
    x_copy = pltpu.make_async_copy(x_hbm, x_ref, copy_sem.at[0])
    gy_copy = pltpu.make_async_copy(gy_hbm, gy_ref, copy_sem.at[1])
    x_copy.start()
    gy_copy.start()

    wf[...] = jnp.zeros(wf.shape, f32)
    for w, start in enumerate(starts):
        wf[start : start + rows_of, 0:D] += chunk_ref[w].astype(f32)

    def piece(name, count, first=0):
        base = ROW[name] + first
        return wf[base : base + count, :]

    vec_rows = [ROW["b_qkv"], ROW["b_proj"], ROW["b_fc2"], ROW["ln1_g"], ROW["ln1_b"], ROW["ln2_g"], ROW["ln2_b"]]
    vec_rows += [ROW["b_fc1"] + k for k in range(4)]
    stacked = jnp.concatenate([wf[r : r + 1, :] for r in vec_rows] + [jnp.zeros((128 - len(vec_rows), 128), f32)], axis=0)
    cols[...] = jnp.transpose(stacked)[:D, :]
    cols_low = cols[...].astype(bf16)
    g1_row, b1_row = piece("ln1_g", 1), piece("ln1_b", 1)
    g2_row, b2_row = piece("ln2_g", 1), piece("ln2_b", 1)

    def through(name, count, first, column):
        return dot(piece(name, count, first)[:, :D].astype(bf16), cols_low)[:, column : column + 1]

    wq_gain = piece("w_qkv", D) * g1_row
    wq[:, 0:D] = piece("w_qkv", D)[:, :D].astype(bf16)
    wq[:, D:] = two_columns(cols[:, 0:1])
    wqt[...] = jnp.transpose(wq_gain)[:D, :].astype(bf16)
    for k, ref in ((1, wkt), (2, wvt)):
        ref[...] = jnp.zeros(ref.shape, bf16)
        ref[0:D, 0:D] = jnp.transpose(piece("w_qkv", D, k * D))[:D, :].astype(bf16)
        ref[D:, 0:D] = two_rows(piece("b_qkv", 1, k)[:, :D])
        wkvg[:, 128 * k - 128 : 128 * k] = jnp.zeros((D, 128), bf16)
        wkvg[:, 128 * k - 128 : 128 * k - 128 + D] = jnp.transpose(piece("w_qkv", D, k * D) * g1_row)[:D, :].astype(bf16)
    wp[:, 0:D] = piece("w_proj", D)[:, :D].astype(bf16)
    wp[:, D:] = two_columns(cols[:, 1:2])
    wpt[...] = jnp.transpose(piece("w_proj", D))[:D, :].astype(bf16)
    w1_gain = piece("w_fc1", HID) * g2_row
    b_fc1 = jnp.concatenate([cols[:, 7 + k : 8 + k] for k in range(4)], axis=0)
    w1[:, 0:D] = w1_gain[:, :D].astype(bf16)
    w1[:, D:] = two_columns((b_fc1 + through("w_fc1", HID, 0, 6)) * math.sqrt(0.5))
    w1t[...] = jnp.transpose(w1_gain)[:D, :].astype(bf16)
    for k in range(4):
        block = wf[pl.ds(ROW["w_fc2"] + k, D, stride=4), :]
        w2t[k * D : (k + 1) * D, :] = jnp.transpose(block)[:D, :].astype(bf16)
    w2[:, 0:HID] = jnp.transpose(w2t[...].astype(f32)).astype(bf16)
    w2[:, HID:] = two_columns(cols[:, 2:3] * math.sqrt(0.5 * math.pi))
    relh[160:, :] = jnp.zeros((8, 128), f32)
    for k in range(4):
        relh[k * 40 : k * 40 + 40, :] = wf[pl.ds(ROW["rel_h"] + 3 + k, 40, stride=4), :]
    rel_w = jnp.concatenate([wf[pl.ds(ROW["rel_w"] + 3 + k, 40, stride=4), :] for k in range(4)], axis=0)
    rel[D:256, :] = rel_w[:, :D].astype(bf16)
    relt[:, D:256] = jnp.transpose(rel_w)[:D, :].astype(bf16)

    def pool_columns(name):
        total = jnp.zeros((D, 128), f32)
        for i in range(9):
            row = wf[ROW[name] + i : ROW[name] + i + 1, :][:, :D]
            total = total + dot((zsel_ref[i].astype(f32) * row).astype(bf16), tsel_ref[i])
        return total

    def pool_rows(name):
        full = jnp.concatenate([pool_columns(name), jnp.zeros((32, 128), f32)], axis=0)
        return jnp.transpose(full)[0:16, :]

    pooled_kernel = pool_columns("pool_q")
    for k in range(9):
        kq[k] = jnp.broadcast_to(pooled_kernel[:, k : k + 1], (D, 128))

    def tap(k, ch, width):
        return jnp.concatenate([kq[k, ch, :]] * (width // 128), axis=1)

    kk[...] = pool_rows("pool_k")
    kv[...] = pool_rows("pool_v")

    for ref in (fq, gq):
        ref[:, 0:HALO] = jnp.zeros((D, HALO), f32)
        ref[:, HALO + TOK :] = jnp.zeros((D, HALO), f32)
    for ref in (fk, fv):
        ref[0:LEAD, :] = jnp.zeros((LEAD, 128), f32)
    for ref in (dw2, dw1, dpr, gv, gkr, dwq, dwkv, kqacc):
        ref[...] = jnp.zeros(ref.shape, ref.dtype)
    gr[ROW["rel_h"] : ROW["w_proj"], :] = jnp.zeros((2 * REL, 128), f32)
    tail = ROW["ln2_b"]
    gr[tail:, :] = jnp.zeros((gr.shape[0] - tail, 128), f32)

    un[D:, :] = two_ones(TOK)
    n1aug[D:, :] = two_ones(TILE_ONE)
    for slot in slots:
        slot[5][HID:, :] = two_ones(TILE_TWO)
        slot[6][D:, :] = two_ones(TILE_TWO)
        slot[7][D:, :] = two_ones(TILE_TWO)
    rhs[192:208, :] = two_ones(TILE_TWO)

    def window(i, tile):
        return pl.ds(aligned(i * tile, 128), tile + 2 * HALO)

    def inner(i, tile):
        return pl.ds(aligned(i * tile + HALO, 128), tile)

    def plain(i, tile):
        return pl.ds(aligned(i * tile, 128), tile)

    def token_mask(i, tile):
        place = idx_ref[0:2, inner(i, tile)]
        return jnp.where((place[0:1] < side) & (place[1:2] < side), 1.0, 0.0)

    x_copy.wait()

    def project(i, carry):
        here = plain(i, TILE_ONE)
        unit, inv = normalize(x_ref[:, here].astype(f32))
        un[0:D, here] = unit.astype(bf16)
        inv_ref[0:1, here] = inv
        n1aug[0:D, :] = (unit * cols[:, 3:4] + cols[:, 4:5]).astype(bf16)
        fq[:, inner(i, TILE_ONE)] = dot(wq[...], n1aug[...]) * token_mask(i, TILE_ONE)
        field = pl.ds(pl.multiple_of(i * TILE_ONE + LEAD, 8), TILE_ONE)
        fk[field, :] = dot_tn(n1aug[...], wkt[...])
        fv[field, :] = dot_tn(n1aug[...], wvt[...])
        return carry

    lax.fori_loop(0, TOK // TILE_ONE, project, 0)

    unit_copy = pltpu.make_async_copy(un.at[0:D, :], unit_hbm, copy_sem.at[4])
    unit_copy.start()

    def pool_queries(i, carry):
        tile = TILE_ONE
        wide = tile + 2 * HALO
        mid = slice(HALO, HALO + tile)
        col = jnp.broadcast_to(idx_ref[1:2, window(i, tile)], (8, wide))
        first, last = col == 0, col == GRID - 1
        mask = token_mask(i, tile)
        for pair in range(D // 16):
            pooled, moved = [], []
            for half in range(2):
                ch = slice(16 * pair + 8 * half, 16 * pair + 8 * half + 8)
                field = fq[ch, window(i, tile)]
                left = jnp.where(first, 0.0, pltpu.roll(field, 1, 1))
                right = jnp.where(last, 0.0, pltpu.roll(field, wide - 1, 1))

                def row_sum(u):
                    return tap(3 * u, ch, wide) * left + tap(3 * u + 1, ch, wide) * field + tap(3 * u + 2, ch, wide) * right

                total = pltpu.roll(row_sum(0), GRID, 1) + row_sum(1) + pltpu.roll(row_sum(2), wide - GRID, 1)
                pooled.append(total[:, mid] * mask)
                moved.append((left[:, mid], field[:, mid], right[:, mid]))
            qb[16 * pair : 16 * pair + 16, plain(i, tile)] = jnp.concatenate(pooled, axis=0).astype(bf16)
            for v in range(3):
                both = jnp.concatenate([moved[0][v], moved[1][v]], axis=0)
                fcol[v * D + 16 * pair : v * D + 16 * pair + 16, plain(i, tile)] = both.astype(bf16)
        return carry

    lax.fori_loop(0, TOK // TILE_ONE, pool_queries, 0)

    b_index = key_columns()

    for field, kernel_rows, pooled in ((fk, kk, kp), (fv, kv, vpool)):
        taps = tap_rows(kernel_rows)
        for a in range(KG):
            total = jnp.zeros((KG, 128), f32)
            for k in range(9):
                total = total + taps[k] * field[pl.ds(tap_start(a, k // 3, k % 3), KG, stride=KSTR), :]
            keep = (KSTR * b_index < side) & (KSTR * a < side)
            pooled[KG * a : KG * a + KG, :] = jnp.where(keep, total, 0.0)

    key = lax.broadcasted_iota(jnp.int32, (KK, 112), 0)
    key_a = lax.div(key, KG)
    key_b = key - KG * key_a
    place = lax.broadcasted_iota(jnp.int32, (KK, 112), 1)
    hot = jnp.zeros((KK, 112), f32)
    for base in (0, 48):
        one_a = (place >= base) & (place < base + 24) & (KG - 1 - key_a == place - base)
        one_b = (place >= base + 24) & (place < base + 48) & (KG - 1 - key_b == place - base - 24)
        hot = jnp.where(one_a | one_b, 1.0, hot)
    shut = (place == 96) & ((KSTR * key_a >= side) | (KSTR * key_b >= side))
    a1[:, 0:D] = kp[...][:, :D].astype(bf16)
    a1[:, D:] = jnp.where(shut, -1e30, hot).astype(bf16)
    vbt[:, 0:D] = vpool[...][:, :D].astype(bf16)
    vbt[:, D:] = jnp.where(lax.broadcasted_iota(jnp.int32, (KK, 16), 1) < 2, -1.0, 0.0).astype(bf16)
    a2[0:D, :] = jnp.transpose(kp[...])[:D, :].astype(bf16)
    vb[0:D, :] = jnp.transpose(vpool[...])[:D, :].astype(bf16)
    vb[D:, :] = jnp.ones((16, KK), bf16)
    key_l = lax.broadcasted_iota(jnp.int32, (48, KK), 1)
    a_l = lax.div(key_l, KG)
    b_l = key_l - KG * a_l
    row_l = lax.broadcasted_iota(jnp.int32, (48, KK), 0)
    hot_l = ((row_l < 24) & (KG - 1 - a_l == row_l)) | ((row_l >= 24) & (KG - 1 - b_l == row_l - 24))
    a2[D:, :] = jnp.where(hot_l, 1.0, 0.0).astype(bf16)

    def ahead(i, slot):
        weight_ref, low_ref, mixed_ref, half_ref, slope_ref, aaug, n2aug, oaug, scale_ref = slot
        tile = TILE_TWO
        here = plain(i, tile)
        row, col = idx_ref[0:1, inner(i, tile)] - i * TILE_ROWS, idx_ref[1:2, inner(i, tile)]
        near = [relh[pl.ds(40 * k + ROW_STEPS * i, 24), :] for k in range(4)]
        rel[0:D, :] = jnp.concatenate(near, axis=0)[:, :D].astype(bf16)
        q = qb[:, here]
        seen = dot(rel[...], q)
        rhs[0:D, :] = q
        yield True
        sides = jnp.concatenate([skew_rows(seen[0:D], row), skew_columns(seen[D:256], col)], axis=0)
        sides = sides * math.sqrt(D)
        sides_low = sides.astype(bf16)
        rhs[D : D + 48, :] = sides_low
        rhs[D + 48 : D + 96, :] = (sides - sides_low.astype(f32)).astype(bf16)
        scores = dot(a1[...], rhs[...])
        yield True
        weight = jnp.exp2((scores - jnp.max(scores, axis=0, keepdims=True)) * (SCORE_SCALE * LOG2E))
        weight_ref[...] = weight
        low_ref[...] = weight.astype(bf16)
        yield True
        mixed = dot(vb[...], low_ref[...])
        inv_sum = 1.0 / mixed[D : D + 1]
        scale_ref[0:1, :] = inv_sum
        mixed = mixed[0:D] * inv_sum
        mixed_ref[...] = mixed
        oaug[0:D, :] = (mixed + q.astype(f32)).astype(bf16)
        middle = x_ref[:, here].astype(f32) + dot(wp[...], oaug[...])
        yield True
        center = middle - jnp.sum(middle, axis=0, keepdims=True) * (1.0 / D)
        inv = lax.rsqrt(jnp.sum(center * center, axis=0, keepdims=True) * (1.0 / D) + norm_eps)
        half = center * (inv * math.sqrt(0.5))
        half_ref[...] = half
        scale_ref[1:2, :] = inv
        n2aug[0:D, :] = half.astype(bf16)
        z = dot(w1[...], n2aug[...])
        yield True
        below = lax.erf(z) * (0.5 * math.sqrt(math.pi)) + 0.5 * math.sqrt(math.pi)
        aaug[0:HID, :] = (z * below).astype(bf16)
        slope_ref[...] = below + z * jnp.exp2((z * z) * -LOG2E)
        yield True
        mlp = dot(w2[...], aaug[...])
        out_ref[:, here] = ((middle + mlp * math.sqrt(2.0 / math.pi)) * token_mask(i, tile)).astype(bf16)

    def behind(i, slot):
        weight_ref, low_ref, mixed_ref, half_ref, slope_ref, aaug, n2aug, oaug, scale_ref = slot
        tile = TILE_TWO
        here = plain(i, tile)
        row, col = idx_ref[0:1, inner(i, tile)] - i * TILE_ROWS, idx_ref[1:2, inner(i, tile)]
        near = [relh[pl.ds(40 * k + ROW_STEPS * i, 24), :] for k in range(4)]
        relt[:, 0:D] = jnp.transpose(jnp.concatenate(near, axis=0))[:D, :].astype(bf16)
        inv_sum, inv = scale_ref[0:1, :], scale_ref[1:2, :]
        gy = gy_ref[:, here].astype(f32) * token_mask(i, tile)
        gy_low = gy.astype(bf16)
        pushed = dot(w2t[...], gy_low)
        yield True
        gh_low = (slope_ref[...] * pushed).astype(bf16)
        dw2[:, 0:KK] += dot_nt(gy_low, aaug[...])
        gn = dot(w1t[...], gh_low)
        yield True
        dw1[0:112, :] += dot_nt(n2aug[...], gh_low)
        half = half_ref[...]
        mean = jnp.sum(gn, axis=0, keepdims=True) * (1.0 / D)
        along = jnp.sum(gn * half, axis=0, keepdims=True) * (2.0 / D)
        gmid = gy + (gn - mean - half * along) * (inv * math.sqrt(1.0 / math.pi))
        gm_low = gmid.astype(bf16)
        gm[:, here] = gm_low
        go = dot(wpt[...], gm_low)
        yield True
        dpr[:, 0:112] += dot_nt(gm_low, oaug[...])
        go_low = (go * inv_sum).astype(bf16)
        goaug[0:D, :] = go_low
        goaug[D:, :] = two_rows(jnp.sum(go_low.astype(f32) * mixed_ref[...], axis=0, keepdims=True))
        spread = dot(vbt[...], goaug[...])
        yield True
        gv[0:D, 0:KK] += dot_nt(go_low, low_ref[...])
        gse[0:KK, :] = (weight_ref[...] * spread).astype(bf16)
        back = dot(a2[...], gse[0:KK, :])
        yield True
        gse[KK : KK + D, :] = unskew_rows(back[D : D + 24], row).astype(bf16)
        gse[KK + D : KK + 256, :] = unskew_columns(back[D + 24 : D + 48], col).astype(bf16)
        yield True
        outer = dot_nt(qb[:, here], gse[...])
        gkr[0:D, 0 : KK + 256] += outer
        hacc[i] = outer[:, 384:512]
        gq[:, inner(i, tile)] = go + SCORE_SCALE * back[0:D] + dot(relt[...], gse[KK : KK + 256, :])

    one, two = slots
    gy_copy.wait()

    def attend(k, carry):
        interleave(ahead(2 * k + 1, two), behind(2 * k, one))
        interleave(ahead(2 * k + 2, one), behind(2 * k + 1, two))
        return carry

    interleave(ahead(0, one))
    lax.fori_loop(0, (TILES - 1) // 2, attend, 0)
    if TILES % 2 == 0:
        interleave(ahead(TILES - 1, two), behind(TILES - 2, one))
        interleave(behind(TILES - 1, two))
    else:
        interleave(behind(TILES - 1, one))

    out_copy = pltpu.make_async_copy(out_ref, out_hbm, copy_sem.at[2])
    out_copy.start()
    mid_copy = pltpu.make_async_copy(gm, mid_hbm, copy_sem.at[3])
    mid_copy.start()

    gkt[...] = jnp.transpose(gkr[:, 0:512])[0:KK, :] * SCORE_SCALE
    gvt[...] = jnp.transpose(gv[...])[0:KK, :]

    def pool_gradient(name, columns):
        low = columns.astype(bf16)
        for i in range(9):
            spread = dot_nt(low, tsel_ref[i]) * zsel_ref[i].astype(f32)
            gr[ROW[name] + i : ROW[name] + i + 1, 0:D] = jnp.sum(spread, axis=0, keepdims=True)

    for field, kernel_rows, pooled, gspread, name in ((fk, kk, gkt, gfk, "pool_k"), (fv, kv, gvt, gfv, "pool_v")):
        taps = tap_rows(kernel_rows)
        sums = [jnp.zeros((KG, 128), f32) for _ in range(9)]
        for a in range(KG):
            grad = pooled[KG * a : KG * a + KG, :]
            inside = jnp.where(b_index == 0, 0.0, grad)
            spread_keys(taps, grad, a, gspread)
            for k in range(9):
                where = pl.ds(tap_start(a, k // 3, k % 3), KG, stride=KSTR)
                sums[k] = sums[k] + (inside if k % 3 == 0 else grad) * field[where, :]
        rows = [jnp.sum(total, axis=0, keepdims=True) for total in sums]
        rows = jnp.concatenate(rows + [jnp.zeros((128 - 9, 128), f32)], axis=0)
        pool_gradient(name, jnp.transpose(rows)[:D, :])

    def finish(i, carry):
        tile = TILE_THREE
        wide = tile + 2 * HALO
        here = plain(i, tile)
        mid = slice(HALO, HALO + tile)
        mask = token_mask(i, tile)
        col = jnp.broadcast_to(idx_ref[1:2, inner(i, tile)], (8, tile))
        first, last = col == 0, col == GRID - 1
        for pair in range(D // 16):
            fields, moved = [], []
            for half in range(2):
                ch = slice(16 * pair + 8 * half, 16 * pair + 8 * half + 8)
                grad = gq[ch, window(i, tile)]
                below, above = pltpu.roll(grad, wide - GRID, 1), pltpu.roll(grad, GRID, 1)

                def col_sum(v):
                    return tap(v, ch, wide) * below + tap(v + 3, ch, wide) * grad + tap(v + 6, ch, wide) * above

                after = jnp.where(last, 0.0, pltpu.roll(col_sum(0), wide - 1, 1)[:, mid])
                before = jnp.where(first, 0.0, pltpu.roll(col_sum(2), 1, 1)[:, mid])
                fields.append((after + col_sum(1)[:, mid] + before) * mask)
                moved.append((below[:, mid], grad[:, mid], above[:, mid]))
            gfield[16 * pair : 16 * pair + 16, here] = jnp.concatenate(fields, axis=0).astype(bf16)
            for u in range(3):
                both = jnp.concatenate([moved[0][u], moved[1][u]], axis=0)
                gsh[u * D + 16 * pair : u * D + 16 * pair + 16, :] = both.astype(bf16)
        kqacc[:, 0 : 3 * D] += dot_nt(gsh[...], fcol[:, here])
        flat = pl.ds(pl.multiple_of(i * tile + LEAD, 8), tile)
        gkv[:, 0:128] = gfk[flat, :].astype(bf16)
        gkv[:, 128:256] = gfv[flat, :].astype(bf16)
        dwq[:, 0:112] += dot_nt(gfield[:, here], un[:, here])
        dwkv[0:112, :] += dot(un[:, here], gkv[...])
        field_copy(i).start()
        return carry

    def field_copy(i):
        here = plain(i, TILE_THREE)
        return pltpu.make_async_copy(gfield.at[:, here], field_hbm.at[:, here], copy_sem.at[5 + i])

    lax.fori_loop(0, TOK // TILE_THREE, finish, 0)
    out_copy.wait()
    mid_copy.wait()
    unit_copy.wait()

    def write(name, rows, first=0):
        base = ROW[name] + first
        gr[base : base + rows.shape[0], 0:D] = rows

    def wide_rows(rows):
        return jnp.concatenate([rows, jnp.zeros((rows.shape[0], 128 - D), f32)], axis=1)

    def through_norm(name, first, outer, bias, gain_row, shift_row):
        raw = piece(name, outer.shape[0], first)[:, :D]
        write(name, outer * gain_row[:, :D] + bias * shift_row[:, :D], first)
        return jnp.sum(raw * outer, axis=0, keepdims=True), jnp.sum(raw * bias, axis=0, keepdims=True)

    gain, shift = through_norm("w_qkv", 0, dwq[:, 0:D], dwq[:, D : D + 1], g1_row, b1_row)
    write("b_qkv", jnp.transpose(dwq[...])[D : D + 1, :])
    for k in (1, 2):
        turned = jnp.transpose(dwkv[:, 128 * k - 128 : 128 * k])[0:D, :]
        more_gain, more_shift = through_norm("w_qkv", k * D, turned[:, 0:D], turned[:, D : D + 1], g1_row, b1_row)
        gain, shift = gain + more_gain, shift + more_shift
        write("b_qkv", dwkv[D : D + 1, 128 * k - 128 : 128 * k - 128 + D], k)
    write("ln1_g", gain)
    write("ln1_b", shift)

    lane = lax.broadcasted_iota(jnp.int32, (D, 128), 1)
    wide_lane = lax.broadcasted_iota(jnp.int32, (D, 3 * 128), 1) - lax.broadcasted_iota(jnp.int32, (D, 3 * 128), 0)
    columns = jnp.zeros((D, 128), f32)
    for k in range(9):
        u, v = k // 3, k % 3
        one = jnp.where(wide_lane == v * D, kqacc[u * D : u * D + D, :], 0.0)
        columns = jnp.where(lane == k, jnp.sum(one, axis=1, keepdims=True), columns)
    pool_gradient("pool_q", columns)

    for i in range(TILES):
        turned = jnp.transpose(hacc[i])
        for k in range(4):
            count = KG + ROW_STEPS - 1
            where = pl.ds(ROW["rel_h"] + 3 + k + TILE_ROWS * i, count, stride=4)
            gr[where, :] = gr[where, :] + wide_rows(turned[16 + 24 * k : 16 + 24 * k + count])
    turned = jnp.transpose(gkr[0:D, 384:768])
    for k in range(4):
        gr[pl.ds(ROW["rel_w"] + 3 + k, 39, stride=4), :] = wide_rows(turned[112 + 40 * k : 151 + 40 * k])

    write("w_proj", dpr[:, 0:D])
    write("b_proj", jnp.transpose(dpr[...])[D : D + 1, :])
    turned = jnp.transpose(dw1[...])
    gain, shift = through_norm(
        "w_fc1", 0, turned[:, 0:D] * math.sqrt(2.0 / math.pi), turned[:, D : D + 1] * math.sqrt(1.0 / math.pi), g2_row, b2_row
    )
    write("ln2_g", gain)
    write("ln2_b", shift)
    for k in range(4):
        write("b_fc1", dw1[D : D + 1, k * D : (k + 1) * D] * math.sqrt(1.0 / math.pi), k)
        gr[pl.ds(ROW["w_fc2"] + k, D, stride=4), :] = wide_rows(dw2[:, k * D : (k + 1) * D] * math.sqrt(2.0 / math.pi))
    write("b_fc2", jnp.transpose(dw2[:, HID:512])[0:1, :])
    for i in range(TOK // TILE_THREE):
        field_copy(i).wait()
    for w, start in enumerate(starts):
        gchunk_ref[w] = gr[start : start + rows_of, 0:D].astype(bf16)


def image_step(starts, rows_of, chunks, pixels, image_side, cotangent):
    depth = 8 * (-(-(starts[-1] + rows_of) // 8))
    zsel, tsel = pool_selectors()
    vm = pltpu.VMEM
    scratch = [
        vm((depth, 128), f32),
        vm((D, 112), bf16), vm((112, 128), bf16), vm((112, 128), bf16),
        vm((D, 112), bf16), vm((D, D), bf16),
        vm((HID, 112), bf16), vm((D, HID), bf16), vm((D, KK), bf16), vm((HID, D), bf16),
        vm((168, 128), f32), vm((256, D), bf16), vm((D, 256), bf16),
        vm((D, 128), f32), vm((9, D, 128), f32),
        vm((D, TOK + 2 * HALO), f32), vm((FIELD, 128), f32), vm((FIELD, 128), f32),
        vm((FIELD, 128), f32), vm((FIELD, 128), f32),
        vm((D, TOK), bf16), vm((D, TOK + 2 * HALO), f32), vm((D, TOK), bf16),
        vm((112, TOK), bf16), vm((3 * D, TOK), bf16),
        vm((KK, 208), bf16), vm((144, KK), bf16), vm((112, KK), bf16), vm((KK, 112), bf16),
        vm((KK, 128), f32), vm((KK, 128), f32),
        vm((208, TILE_TWO), bf16), vm((KK + 256, TILE_TWO), bf16), vm((112, TILE_ONE), bf16), vm((112, TILE_TWO), bf16),
        vm((3 * D, TILE_THREE), bf16), vm((TILE_THREE, 256), bf16),
        vm((D, 512), f32), vm((128, HID), f32), vm((D, 128), f32), vm((128, 512), f32), vm((128, 768), f32),
        vm((TILES, D, 128), f32),
        vm((D, 128), f32), vm((128, 256), f32), vm((3 * D, 3 * 128), f32),
        vm((depth, 128), f32),
        vm((D, TOK), bf16), vm((D, TOK), bf16), vm((D, TOK), bf16), vm((D, TOK), bf16),
        pltpu.SemaphoreType.DMA((5 + TOK // TILE_THREE,)),
    ]
    slot = [
        vm((KK, TILE_TWO), f32), vm((KK, TILE_TWO), bf16), vm((D, TILE_TWO), f32), vm((D, TILE_TWO), f32), vm((HID, TILE_TWO), f32),
        vm((KK, TILE_TWO), bf16), vm((112, TILE_TWO), bf16), vm((112, TILE_TWO), bf16), vm((8, TILE_TWO), f32),
    ]
    whole = pl.BlockSpec(memory_space=pltpu.VMEM)
    far = pl.BlockSpec(memory_space=pl.ANY)
    shape = jax.ShapeDtypeStruct
    out, grad_chunks, *rest = pl.pallas_call(
        functools.partial(image_kernel, starts, rows_of),
        out_shape=(
            shape((D, TOK), bf16), shape((len(starts), rows_of, D), bf16),
            shape((D, TOK), bf16), shape((D, TOK), bf16), shape((D, TOK), bf16), shape((8, TOK), f32),
            shape((KK, 128), f32), shape((KK, 128), f32), shape((16, 128), f32), shape((16, 128), f32),
            shape((D, D), bf16), shape((D, 256), bf16),
        ),
        in_specs=[pl.BlockSpec(memory_space=pltpu.SMEM), whole, far, far, whole, whole, whole],
        out_specs=(far, whole, far, far, far) + (whole,) * 7,
        scratch_shapes=scratch + slot + slot,
        compiler_params=pltpu.CompilerParams(vmem_limit_bytes=63 * 1024 * 1024),
        name="image_step",
    )(image_side, chunks, pixels, cotangent, lane_index(), zsel, tsel)
    return out, grad_chunks, rest


def input_step(rest):
    far = pl.BlockSpec(memory_space=pl.ANY)
    vm = pltpu.VMEM
    scratch = [vm(part.shape, part.dtype) for part in rest]
    scratch += [vm((D, TOK), bf16), vm((FIELD, 128), f32), vm((FIELD, 128), f32), vm((TILE_THREE, 256), bf16)]
    return pl.pallas_call(
        input_kernel,
        out_shape=jax.ShapeDtypeStruct((D, TOK), bf16),
        in_specs=[far] * len(rest),
        out_specs=far,
        scratch_shapes=scratch + [pltpu.SemaphoreType.DMA((10 + TOK // TILE_THREE,))],
        compiler_params=pltpu.CompilerParams(vmem_limit_bytes=60 * 1024 * 1024),
        cost_estimate=pl.CostEstimate(flops=2 * D * 3 * D * TOK, bytes_accessed=16 * 1024 * 1024, transcendentals=0),
        name="input_step",
    )(*rest)


def adam_update(gradient, master_part, first_part, second_part, average_part, step_rates):
    moment_one = beta_first * first_part + (1.0 - beta_first) * gradient
    moment_two = beta_second * second_part + (1.0 - beta_second) * gradient * gradient
    fix_one = 1.0 - beta_first**STEP
    fix_two = 1.0 - beta_second**STEP
    direction = moment_one / fix_one / (jnp.sqrt(moment_two / fix_two) + adam_eps)
    updated = master_part - step_rates * (direction + weight_decay * master_part)
    blended = average_decay * average_part + (1.0 - average_decay) * updated
    return (updated, moment_one, moment_two, blended)


def shards(tokens, image_sides, grad_out, master, first_moment, second_moment, weight_average):
    shard_len = master.shape[0]
    owners = lax.axis_size("wide")
    images_all = tokens.shape[0] * owners * lax.axis_size("narrow")
    starts = tuple((shard_len * w) // D for w in range(owners))
    rows_of = block_rows(shard_len)
    inset = lax.rem(lax.axis_index("wide") * shard_len, D)

    own = lax.dynamic_update_slice(jnp.zeros((rows_of * D,), bf16), master.astype(bf16), (inset,))
    own = jnp.broadcast_to(own.reshape(1, rows_of, D), (owners, rows_of, D))
    chunks = lax.all_to_all(own, "wide", 0, 0)

    outs, grads_in, grad_chunks = [], [], None
    for k in range(tokens.shape[0]):
        out, chunk, rest = image_step(starts, rows_of, chunks, tokens[k], image_sides[k : k + 1], grad_out[k])
        outs.append(out)
        grads_in.append(input_step(rest))
        grad_chunks = chunk if k == 0 else (grad_chunks.astype(f32) + chunk.astype(f32)).astype(bf16)
    block_out = jnp.stack(outs)
    grad_in = jnp.stack(grads_in)

    parts = lax.all_to_all(grad_chunks, "wide", 0, 0)
    parts, grad_in = lax.optimization_barrier((parts, grad_in))
    total = jnp.sum(parts.astype(f32), axis=0)
    total = total + lax.ppermute(total, "narrow", [(0, 1), (1, 0)])
    reduced = lax.dynamic_slice(total.reshape(rows_of * D), (inset,), (shard_len,))
    step_rates = lax.dynamic_slice_in_dim(
        jnp.asarray(rate_values(shard_len * owners)), lax.axis_index("wide") * shard_len, shard_len
    )
    updated, moment_one, moment_two, blended = adam_update(
        reduced / images_all, master, first_moment, second_moment, weight_average, step_rates
    )
    return (block_out, grad_in, updated, moment_one, moment_two, blended)


def solution(mesh):
    return jax.shard_map(
        shards,
        mesh=mesh,
        in_specs=(
            P(("wide", "narrow"), None, None),
            P(("wide", "narrow")),
            P(("wide", "narrow"), None, None),
            P("wide"),
            P("wide"),
            P("wide"),
            P("wide"),
        ),
        out_specs=(
            P(("wide", "narrow"), None, None),
            P(("wide", "narrow"), None, None),
            P("wide"),
            P("wide"),
            P("wide"),
            P("wide"),
        ),
        check_vma=False,
    )
```

```python
import functools
import math

import jax
import jax.numpy as jnp
import numpy as np
from jax import lax
from jax.experimental import pallas as pl
from jax.experimental.pallas import tpu as pltpu
from jax.sharding import PartitionSpec as P

D = 96
HID = 384
KSTR = 4
KG = 20
STEP = 5
GRID = 80
TOK = 6400
KK = 400
REL = 159

norm_eps = 1e-06
beta_first = 0.5
beta_second = 0.5
adam_eps = 1e-08
weight_decay = 0.05
rate_factor = 0.4
average_decay = 0.8

f32 = jnp.float32
bf16 = jnp.bfloat16

HALO = 128
LEAD = 88
FIELD = LEAD + TOK + 8
TILE_PROJECT = 3200
TILE_ONE = 6400
TILE_TWO = 1280
TILE_THREE = 1280
TILES = TOK // TILE_TWO
TILE_ROWS = TILE_TWO // GRID
ROW_STEPS = TILE_ROWS // KSTR
SCORE_SCALE = D ** (-0.5)
LOG2E = 1.4426950408889634


def segment_list():
    return [
        ("w_qkv", (3 * D, D), D ** (-0.5)),
        ("b_qkv", (3 * D,), 0.2),
        ("pool_q", (D, 9), 1.0 / 3.0),
        ("pool_k", (D, 9), 1.0 / 3.0),
        ("pool_v", (D, 9), 1.0 / 3.0),
        ("rel_h", (REL, D), 0.5 * D ** (-0.5)),
        ("rel_w", (REL, D), 0.5 * D ** (-0.5)),
        ("w_proj", (D, D), D ** (-0.5)),
        ("b_proj", (D,), 0.2),
        ("w_fc1", (HID, D), D ** (-0.5)),
        ("b_fc1", (HID,), 0.2),
        ("w_fc2", (D, HID), HID ** (-0.5)),
        ("b_fc2", (D,), 0.2),
        ("ln1_g", (D,), 0.5),
        ("ln1_b", (D,), 0.2),
        ("ln2_g", (D,), 0.5),
        ("ln2_b", (D,), 0.2),
    ]


def row_bases():
    bases = {}
    offset = 0
    for name, shape, _ in segment_list():
        assert offset % D == 0
        bases[name] = offset // D
        offset += math.prod(shape)
    return bases


ROW = row_bases()


def rate_values(full_len):
    rates = np.full((full_len,), rate_factor * D ** (-0.5), np.float32)
    offset = 0
    for _, shape, spread in segment_list():
        length = math.prod(shape)
        rates[offset : offset + length] = rate_factor * spread
        offset += length
    return rates


def block_rows(shard_len):
    return 16 * (-(-(-(-(shard_len + D - 1) // D)) // 16))


def pool_selectors():
    flat = np.arange(9 * D).reshape(9, D)
    channel = (flat[:, None, :] // 9 == np.arange(D)[None, :, None]).astype(np.float32)
    tap = (flat[:, :, None] % 9 == np.arange(128)[None, None, :]).astype(np.float32)
    return jnp.asarray(channel, bf16), jnp.asarray(tap, bf16)


def lane_index():
    place = np.arange(-HALO, TOK + HALO)
    table = np.zeros((8, TOK + 2 * HALO), np.int32)
    table[0] = place // GRID
    table[1] = place % GRID
    return jnp.asarray(table)


def dot(a, b):
    return lax.dot_general(a, b, (((1,), (0,)), ((), ())), preferred_element_type=f32)


def dot_nt(a, b):
    return lax.dot_general(a, b, (((1,), (1,)), ((), ())), preferred_element_type=f32)


def dot_tn(a, b):
    return lax.dot_general(a, b, (((0,), (0,)), ((), ())), preferred_element_type=f32)


def normalize(values):
    mean = jnp.sum(values, axis=0, keepdims=True) * (1.0 / D)
    center = values - mean
    spread = jnp.sum(center * center, axis=0, keepdims=True) * (1.0 / D)
    inv = lax.rsqrt(spread + norm_eps)
    return center * inv, inv


def skew_rows(rows, place):
    width = rows.shape[1]
    where = jnp.broadcast_to(place, (24, width))
    residue = where & 3
    x = jnp.where(
        residue < 2,
        jnp.where(residue == 0, rows[0:24], rows[24:48]),
        jnp.where(residue == 2, rows[48:72], rows[72:96]),
    )
    step = ROW_STEPS // 2
    while step >= 1:
        x = jnp.where((where & (4 * step)) != 0, pltpu.roll(x, 24 - step, 0), x)
        step //= 2
    return x


def skew_columns(rows, place):
    width = rows.shape[1]
    where = jnp.broadcast_to(place, (40, width))
    residue = where & 3
    x = jnp.where(
        residue < 2,
        jnp.where(residue == 0, rows[0:40], rows[40:80]),
        jnp.where(residue == 2, rows[80:120], rows[120:160]),
    )
    x = jnp.concatenate([jnp.where((where[0:24] & 64) != 0, x[16:40], x[0:24]), x[24:40]], axis=0)
    x = jnp.where((where[0:32] & 32) != 0, x[8:40], x[0:32])
    where = where[0:24]
    x = jnp.where((where & 16) != 0, pltpu.roll(x, 28, 0)[0:24], x[0:24])
    x = jnp.where((where & 8) != 0, pltpu.roll(x, 22, 0), x)
    return jnp.where((where & 4) != 0, pltpu.roll(x, 23, 0), x)


def unskew_rows(x, place):
    where = jnp.broadcast_to(place, x.shape)
    step = 1
    while step < ROW_STEPS:
        x = jnp.where((where & (4 * step)) != 0, pltpu.roll(x, step, 0), x)
        step *= 2
    residue = where & 3
    return jnp.concatenate([jnp.where(residue == k, x, 0.0) for k in range(4)], axis=0)


def unskew_columns(x, place):
    width = x.shape[1]
    zero = jnp.zeros((8, width), f32)
    where = jnp.broadcast_to(place, (40, width))
    x = jnp.where((where[0:24] & 4) != 0, pltpu.roll(x, 1, 0), x)
    x = jnp.where((where[0:24] & 8) != 0, pltpu.roll(x, 2, 0), x)
    x = jnp.concatenate([x, zero], axis=0)
    x = jnp.where((where[0:32] & 16) != 0, pltpu.roll(x, 4, 0), x)
    x = jnp.where((where & 32) != 0, jnp.concatenate([zero, x], axis=0), jnp.concatenate([x, zero], axis=0))
    far = (where & 64) != 0
    x = jnp.concatenate([jnp.where(far[0:16], 0.0, x[0:16]), jnp.where(far[16:40], x[0:24], x[16:40])], axis=0)
    residue = where & 3
    return jnp.concatenate([jnp.where(residue == k, x, 0.0) for k in range(4)], axis=0)


def aligned(value, step):
    return value if isinstance(value, int) else pl.multiple_of(value, step)


def interleave(*parts):
    live = list(parts)
    while live:
        for part in list(live):
            if next(part, None) is None:
                live.remove(part)


def two_columns(column):
    high = column.astype(bf16).astype(f32)
    place = lax.broadcasted_iota(jnp.int32, (column.shape[0], 16), 1)
    return jnp.where(place == 0, high, jnp.where(place == 1, column - high, 0.0)).astype(bf16)


def two_rows(row):
    high = row.astype(bf16).astype(f32)
    place = lax.broadcasted_iota(jnp.int32, (16, row.shape[1]), 0)
    return jnp.where(place == 0, high, jnp.where(place == 1, row - high, 0.0)).astype(bf16)


def two_ones(width):
    return jnp.where(lax.broadcasted_iota(jnp.int32, (16, width), 0) < 2, 1.0, 0.0).astype(bf16)


def key_columns():
    return lax.broadcasted_iota(jnp.int32, (KG, 128), 0)


def tap_start(a, u, v):
    return LEAD + GRID * (KSTR * a + u - 1) + v - 1


def tap_rows(kernel_rows):
    b_index = key_columns()
    taps = [jnp.broadcast_to(kernel_rows[k : k + 1, :], (KG, 128)) for k in range(9)]
    return [jnp.where(b_index == 0, 0.0, tap) if k % 3 == 0 else tap for k, tap in enumerate(taps)]


def spread_keys(taps, grad, a, gfield):
    idle = LEAD + GRID * (KSTR * a + 2)
    gfield[idle - 8 : idle + GRID, :] = jnp.zeros((GRID + 8, 128), f32)
    for u in range(3):
        gfield[pl.ds(tap_start(a, u, 3), KG, stride=KSTR), :] = jnp.zeros((KG, 128), f32)
    for k in range(9):
        gfield[pl.ds(tap_start(a, k // 3, k % 3), KG, stride=KSTR), :] = taps[k] * grad
    if a == KG - 1:
        gfield[LEAD + TOK - GRID : LEAD + TOK, :] = jnp.zeros((GRID, 128), f32)


def input_kernel(*refs):
    sources, gin_hbm, held = refs[:10], refs[10], refs[11:21]
    field_ref, mid_ref, unit_ref, inv_ref, gkt, gvt, kk, kv, wqt, wkvg = held
    gin_ref, gfk, gfv, gkv, copy_sem = refs[21:]
    copies = [pltpu.make_async_copy(a, b, copy_sem.at[k]) for k, (a, b) in enumerate(zip(sources, held))]
    for copy in copies[::-1]:
        copy.start()
    for copy in copies[4:]:
        copy.wait()
    for kernel_rows, pooled, gfield in ((kk, gkt, gfk), (kv, gvt, gfv)):
        taps = tap_rows(kernel_rows)
        for a in range(KG):
            spread_keys(taps, pooled[KG * a : KG * a + KG, :], a, gfield)
    for copy in copies[:4]:
        copy.wait()

    def gin_copy(i):
        here = pl.ds(aligned(i * TILE_THREE, 128), TILE_THREE)
        return pltpu.make_async_copy(gin_ref.at[:, here], gin_hbm.at[:, here], copy_sem.at[10 + i])

    def finish(i, carry):
        tile = TILE_THREE
        here = pl.ds(aligned(i * tile, 128), tile)
        flat = pl.ds(aligned(i * tile + LEAD, 8), tile)
        gkv[:, 0:128] = gfk[flat, :].astype(bf16)
        gkv[:, 128:256] = gfv[flat, :].astype(bf16)
        gn = dot(wqt[...], field_ref[:, here]) + dot_nt(wkvg[...], gkv[...])
        unit = unit_ref[:, here].astype(f32)
        mean = jnp.sum(gn, axis=0, keepdims=True) * (1.0 / D)
        along = jnp.sum(gn * unit, axis=0, keepdims=True) * (1.0 / D)
        total = mid_ref[:, here].astype(f32) + (gn - mean - unit * along) * inv_ref[0:1, here]
        gin_ref[:, here] = total.astype(bf16)
        gin_copy(i).start()
        return carry

    lax.fori_loop(0, TOK // TILE_THREE, finish, 0)
    for i in range(TOK // TILE_THREE):
        gin_copy(i).wait()


def image_kernel(
    shard_len,
    starts,
    rows_of,
    side_ref,
    chunk_ref,
    x_hbm,
    gy_hbm,
    idx_hbm,
    zsel_hbm,
    tsel_hbm,
    out_hbm,
    gchunk_ref,
    field_hbm,
    mid_hbm,
    unit_hbm,
    inv_ref,
    gkt,
    gvt,
    kk,
    kv,
    wqt,
    wkvg,
    wf, wq, wkt, wvt, wp, wpt, w1, w1t, w2, w2t, relh, rel, relt, cols, kq,
    fq, fk, fv, qb, gm, un, fcol,
    a1, a2, vb, vbt, kp, vpool,
    rhs, gse, n1aug, goaug, gsh, gkv,
    dw2, dw1, dpr, gv, gkr, hacc, dwq, dwkv, kqacc, gr, x_ref, gy_ref, out_ref, gfield, copy_sem, flat, zsel_ref, tsel_ref, idx_ref, table_sem,
    *slot_refs,
):
    gq, gfk, gfv = fq, fk, fv
    slots = (slot_refs[: len(slot_refs) // 2], slot_refs[len(slot_refs) // 2 :])
    side = side_ref[0]
    table_copies = [
        pltpu.make_async_copy(source, target, table_sem.at[k])
        for k, (source, target) in enumerate(((zsel_hbm, zsel_ref), (tsel_hbm, tsel_ref), (idx_hbm, idx_ref)))
    ]
    for copy in table_copies:
        copy.start()
    x_copy = pltpu.make_async_copy(x_hbm, x_ref, copy_sem.at[0])
    gy_copy = pltpu.make_async_copy(gy_hbm, gy_ref, copy_sem.at[1])
    x_copy.start()
    gy_copy.start()

    flat[...] = jnp.zeros(flat.shape, f32)
    lane_of = lax.broadcasted_iota(jnp.int32, chunk_ref.shape[1:], 1)
    for w in range(len(starts)):
        base, inset = (shard_len * w) // 128, (shard_len * w) % 128
        part = chunk_ref[w].astype(f32)
        if inset:
            part = pltpu.roll(part, inset, 1)
            flat[base + 1 : base + 1 + part.shape[0], :] += jnp.where(lane_of < inset, part, 0.0)
            part = jnp.where(lane_of < inset, 0.0, part)
        flat[base : base + part.shape[0], :] += part
    groups = -(-(shard_len * len(starts)) // (4 * D))
    lane_of = lax.broadcasted_iota(jnp.int32, (groups, 128), 1)
    first, second, third = (flat[pl.ds(k, groups, stride=3), :] for k in range(3))
    wf[pl.ds(0, groups, stride=4), :] = first
    wf[pl.ds(1, groups, stride=4), :] = pltpu.roll(jnp.where(lane_of >= 96, first, second), 32, 1)
    wf[pl.ds(2, groups, stride=4), :] = pltpu.roll(jnp.where(lane_of >= 64, second, third), 64, 1)
    wf[pl.ds(3, groups, stride=4), :] = pltpu.roll(third, 96, 1)

    def piece(name, count, first=0):
        base = ROW[name] + first
        return wf[base : base + count, :]

    vec_rows = [ROW["b_qkv"], ROW["b_proj"], ROW["b_fc2"], ROW["ln1_g"], ROW["ln1_b"], ROW["ln2_g"], ROW["ln2_b"]]
    vec_rows += [ROW["b_fc1"] + k for k in range(4)]
    stacked = jnp.concatenate([wf[r : r + 1, :] for r in vec_rows] + [jnp.zeros((128 - len(vec_rows), 128), f32)], axis=0)
    cols[...] = jnp.transpose(stacked)[:D, :]
    cols_low = cols[...].astype(bf16)
    g1_row, b1_row = piece("ln1_g", 1), piece("ln1_b", 1)
    g2_row, b2_row = piece("ln2_g", 1), piece("ln2_b", 1)

    def through(name, count, first, column):
        return dot(piece(name, count, first)[:, :D].astype(bf16), cols_low)[:, column : column + 1]

    wq_gain = piece("w_qkv", D) * g1_row
    wq[:, 0:D] = piece("w_qkv", D)[:, :D].astype(bf16)
    wq[:, D:] = two_columns(cols[:, 0:1])
    wqt[...] = jnp.transpose(wq_gain)[:D, :].astype(bf16)
    for k, ref in ((1, wkt), (2, wvt)):
        ref[...] = jnp.zeros(ref.shape, bf16)
        ref[0:D, 0:D] = jnp.transpose(piece("w_qkv", D, k * D))[:D, :].astype(bf16)
        ref[D:, 0:D] = two_rows(piece("b_qkv", 1, k)[:, :D])
        wkvg[:, 128 * k - 128 : 128 * k] = jnp.zeros((D, 128), bf16)
        wkvg[:, 128 * k - 128 : 128 * k - 128 + D] = jnp.transpose(piece("w_qkv", D, k * D) * g1_row)[:D, :].astype(bf16)
    wp[:, 0:D] = piece("w_proj", D)[:, :D].astype(bf16)
    wp[:, D:] = two_columns(cols[:, 1:2])
    wpt[...] = jnp.transpose(piece("w_proj", D))[:D, :].astype(bf16)
    w1_gain = piece("w_fc1", HID) * g2_row
    b_fc1 = jnp.concatenate([cols[:, 7 + k : 8 + k] for k in range(4)], axis=0)
    w1[:, 0:D] = w1_gain[:, :D].astype(bf16)
    w1[:, D:] = two_columns((b_fc1 + through("w_fc1", HID, 0, 6)) * math.sqrt(0.5))
    w1t[...] = jnp.transpose(w1_gain)[:D, :].astype(bf16)
    for k in range(4):
        block = wf[pl.ds(ROW["w_fc2"] + k, D, stride=4), :]
        w2t[k * D : (k + 1) * D, :] = jnp.transpose(block)[:D, :].astype(bf16)
    w2[:, 0:HID] = jnp.transpose(w2t[...].astype(f32)).astype(bf16)
    w2[:, HID:] = two_columns(cols[:, 2:3] * math.sqrt(0.5 * math.pi))
    relh[160:, :] = jnp.zeros((8, 128), f32)
    for k in range(4):
        relh[k * 40 : k * 40 + 40, :] = wf[pl.ds(ROW["rel_h"] + 3 + k, 40, stride=4), :]
    rel_w = jnp.concatenate([wf[pl.ds(ROW["rel_w"] + 3 + k, 40, stride=4), :] for k in range(4)], axis=0)
    rel[D:256, :] = rel_w[:, :D].astype(bf16)
    relt[:, D:256] = jnp.transpose(rel_w)[:D, :].astype(bf16)

    def pool_columns(name):
        total = jnp.zeros((D, 128), f32)
        for i in range(9):
            row = wf[ROW[name] + i : ROW[name] + i + 1, :][:, :D]
            total = total + dot((zsel_ref[i].astype(f32) * row).astype(bf16), tsel_ref[i])
        return total

    def pool_rows(name):
        full = jnp.concatenate([pool_columns(name), jnp.zeros((32, 128), f32)], axis=0)
        return jnp.transpose(full)[0:16, :]

    for copy in table_copies:
        copy.wait()
    pooled_kernel = pool_columns("pool_q")
    for k in range(9):
        kq[k] = jnp.broadcast_to(pooled_kernel[:, k : k + 1], (D, 128))

    def tap(k, ch, width):
        return jnp.concatenate([kq[k, ch, :]] * (width // 128), axis=1)

    kk[...] = pool_rows("pool_k")
    kv[...] = pool_rows("pool_v")

    for ref in (fq,):
        ref[:, 0:HALO] = jnp.zeros((D, HALO), f32)
        ref[:, HALO + TOK :] = jnp.zeros((D, HALO), f32)
    for ref in (fk, fv):
        ref[0:LEAD, :] = jnp.zeros((LEAD, 128), f32)
    for ref in (dw2, dw1, dpr, gv, gkr, dwq, dwkv, kqacc):
        ref[...] = jnp.zeros(ref.shape, ref.dtype)
    gr[ROW["rel_h"] : ROW["w_proj"], :] = jnp.zeros((2 * REL, 128), f32)
    tail = ROW["ln2_b"]
    gr[tail:, :] = jnp.zeros((gr.shape[0] - tail, 128), f32)

    un[D:, :] = two_ones(TOK)
    n1aug[D:, :] = two_ones(TILE_PROJECT)
    for slot in slots:
        slot[5][HID:, :] = two_ones(TILE_TWO)
        slot[6][D:, :] = two_ones(TILE_TWO)
        slot[7][D:, :] = two_ones(TILE_TWO)
    rhs[192:208, :] = two_ones(TILE_TWO)

    def window(i, tile):
        return pl.ds(aligned(i * tile, 128), tile + 2 * HALO)

    def inner(i, tile):
        return pl.ds(aligned(i * tile + HALO, 128), tile)

    def plain(i, tile):
        return pl.ds(aligned(i * tile, 128), tile)

    def token_mask(i, tile):
        place = idx_ref[0:2, inner(i, tile)]
        return jnp.where((place[0:1] < side) & (place[1:2] < side), 1.0, 0.0)

    x_copy.wait()

    def project(i, carry):
        here = plain(i, TILE_PROJECT)
        unit, inv = normalize(x_ref[:, here].astype(f32))
        un[0:D, here] = unit.astype(bf16)
        inv_ref[0:1, here] = inv
        n1aug[0:D, :] = (unit * cols[:, 3:4] + cols[:, 4:5]).astype(bf16)
        fq[:, inner(i, TILE_PROJECT)] = dot(wq[...], n1aug[...]) * token_mask(i, TILE_PROJECT)
        field = pl.ds(pl.multiple_of(i * TILE_PROJECT + LEAD, 8), TILE_PROJECT)
        fk[field, :] = dot_tn(n1aug[...], wkt[...])
        fv[field, :] = dot_tn(n1aug[...], wvt[...])
        return carry

    lax.fori_loop(0, TOK // TILE_PROJECT, project, 0)

    unit_copy = pltpu.make_async_copy(un.at[0:D, :], unit_hbm, copy_sem.at[4])
    unit_copy.start()

    def pool_queries(i, carry):
        tile = TILE_ONE
        wide = tile + 2 * HALO
        mid = slice(HALO, HALO + tile)
        col = jnp.broadcast_to(idx_ref[1:2, window(i, tile)], (8, wide))
        first, last = col == 0, col == GRID - 1
        mask = token_mask(i, tile)
        for pair in range(D // 16):
            pooled, moved = [], []
            for half in range(2):
                ch = slice(16 * pair + 8 * half, 16 * pair + 8 * half + 8)
                field = fq[ch, window(i, tile)]
                left = jnp.where(first, 0.0, pltpu.roll(field, 1, 1))
                right = jnp.where(last, 0.0, pltpu.roll(field, wide - 1, 1))

                def row_sum(u):
                    return tap(3 * u, ch, wide) * left + tap(3 * u + 1, ch, wide) * field + tap(3 * u + 2, ch, wide) * right

                total = pltpu.roll(row_sum(0), GRID, 1) + row_sum(1) + pltpu.roll(row_sum(2), wide - GRID, 1)
                pooled.append(total[:, mid] * mask)
                moved.append((left[:, mid], field[:, mid], right[:, mid]))
            qb[16 * pair : 16 * pair + 16, plain(i, tile)] = jnp.concatenate(pooled, axis=0).astype(bf16)
            for v in range(3):
                both = jnp.concatenate([moved[0][v], moved[1][v]], axis=0)
                fcol[v * D + 16 * pair : v * D + 16 * pair + 16, plain(i, tile)] = both.astype(bf16)
        return carry

    lax.fori_loop(0, TOK // TILE_ONE, pool_queries, 0)

    b_index = key_columns()

    for field, kernel_rows, pooled in ((fk, kk, kp), (fv, kv, vpool)):
        taps = tap_rows(kernel_rows)
        for a in range(KG):
            total = jnp.zeros((KG, 128), f32)
            for k in range(9):
                total = total + taps[k] * field[pl.ds(tap_start(a, k // 3, k % 3), KG, stride=KSTR), :]
            keep = (KSTR * b_index < side) & (KSTR * a < side)
            pooled[KG * a : KG * a + KG, :] = jnp.where(keep, total, 0.0)

    key = lax.broadcasted_iota(jnp.int32, (KK, 112), 0)
    key_a = lax.div(key, KG)
    key_b = key - KG * key_a
    place = lax.broadcasted_iota(jnp.int32, (KK, 112), 1)
    hot = jnp.zeros((KK, 112), f32)
    for base in (0, 48):
        one_a = (place >= base) & (place < base + 24) & (KG - 1 - key_a == place - base)
        one_b = (place >= base + 24) & (place < base + 48) & (KG - 1 - key_b == place - base - 24)
        hot = jnp.where(one_a | one_b, 1.0, hot)
    shut = (place == 96) & ((KSTR * key_a >= side) | (KSTR * key_b >= side))
    a1[:, 0:D] = kp[...][:, :D].astype(bf16)
    a1[:, D:] = jnp.where(shut, -1e30, hot).astype(bf16)
    vbt[:, 0:D] = vpool[...][:, :D].astype(bf16)
    vbt[:, D:] = jnp.where(lax.broadcasted_iota(jnp.int32, (KK, 16), 1) < 2, -1.0, 0.0).astype(bf16)
    a2[0:D, :] = jnp.transpose(kp[...])[:D, :].astype(bf16)
    vb[0:D, :] = jnp.transpose(vpool[...])[:D, :].astype(bf16)
    vb[D:, :] = jnp.ones((16, KK), bf16)
    key_l = lax.broadcasted_iota(jnp.int32, (48, KK), 1)
    a_l = lax.div(key_l, KG)
    b_l = key_l - KG * a_l
    row_l = lax.broadcasted_iota(jnp.int32, (48, KK), 0)
    hot_l = ((row_l < 24) & (KG - 1 - a_l == row_l)) | ((row_l >= 24) & (KG - 1 - b_l == row_l - 24))
    a2[D:, :] = jnp.where(hot_l, 1.0, 0.0).astype(bf16)

    def ahead(i, slot):
        weight_ref, low_ref, mixed_ref, half_ref, slope_ref, aaug, n2aug, oaug, scale_ref = slot
        tile = TILE_TWO
        here = plain(i, tile)
        row, col = idx_ref[0:1, inner(i, tile)] - i * TILE_ROWS, idx_ref[1:2, inner(i, tile)]
        near = [relh[pl.ds(40 * k + ROW_STEPS * i, 24), :] for k in range(4)]
        rel[0:D, :] = jnp.concatenate(near, axis=0)[:, :D].astype(bf16)
        q = qb[:, here]
        seen = dot(rel[...], q)
        rhs[0:D, :] = q
        yield True
        sides = jnp.concatenate([skew_rows(seen[0:D], row), skew_columns(seen[D:256], col)], axis=0)
        sides = sides * math.sqrt(D)
        sides_low = sides.astype(bf16)
        rhs[D : D + 48, :] = sides_low
        rhs[D + 48 : D + 96, :] = (sides - sides_low.astype(f32)).astype(bf16)
        scores = dot(a1[...], rhs[...])
        yield True
        weight = jnp.exp2((scores - jnp.max(scores, axis=0, keepdims=True)) * (SCORE_SCALE * LOG2E))
        weight_ref[...] = weight
        low_ref[...] = weight.astype(bf16)
        yield True
        mixed = dot(vb[...], low_ref[...])
        inv_sum = 1.0 / mixed[D : D + 1]
        scale_ref[0:1, :] = inv_sum
        mixed = mixed[0:D] * inv_sum
        mixed_ref[...] = mixed
        oaug[0:D, :] = (mixed + q.astype(f32)).astype(bf16)
        middle = x_ref[:, here].astype(f32) + dot(wp[...], oaug[...])
        yield True
        center = middle - jnp.sum(middle, axis=0, keepdims=True) * (1.0 / D)
        inv = lax.rsqrt(jnp.sum(center * center, axis=0, keepdims=True) * (1.0 / D) + norm_eps)
        half = center * (inv * math.sqrt(0.5))
        half_ref[...] = half
        scale_ref[1:2, :] = inv
        n2aug[0:D, :] = half.astype(bf16)
        z = dot(w1[...], n2aug[...])
        yield True
        below = lax.erf(z) * (0.5 * math.sqrt(math.pi)) + 0.5 * math.sqrt(math.pi)
        aaug[0:HID, :] = (z * below).astype(bf16)
        slope_ref[...] = below + z * jnp.exp2((z * z) * -LOG2E)
        yield True
        mlp = dot(w2[...], aaug[...])
        out_ref[:, here] = ((middle + mlp * math.sqrt(2.0 / math.pi)) * token_mask(i, tile)).astype(bf16)

    def behind(i, slot):
        weight_ref, low_ref, mixed_ref, half_ref, slope_ref, aaug, n2aug, oaug, scale_ref = slot
        tile = TILE_TWO
        here = plain(i, tile)
        row, col = idx_ref[0:1, inner(i, tile)] - i * TILE_ROWS, idx_ref[1:2, inner(i, tile)]
        near = [relh[pl.ds(40 * k + ROW_STEPS * i, 24), :] for k in range(4)]
        relt[:, 0:D] = jnp.transpose(jnp.concatenate(near, axis=0))[:D, :].astype(bf16)
        inv_sum, inv = scale_ref[0:1, :], scale_ref[1:2, :]
        gy = gy_ref[:, here].astype(f32) * token_mask(i, tile)
        gy_low = gy.astype(bf16)
        pushed = dot(w2t[...], gy_low)
        yield True
        gh_low = (slope_ref[...] * pushed).astype(bf16)
        dw2[:, 0:KK] += dot_nt(gy_low, aaug[...])
        gn = dot(w1t[...], gh_low)
        yield True
        dw1[0:112, :] += dot_nt(n2aug[...], gh_low)
        half = half_ref[...]
        mean = jnp.sum(gn, axis=0, keepdims=True) * (1.0 / D)
        along = jnp.sum(gn * half, axis=0, keepdims=True) * (2.0 / D)
        gmid = gy + (gn - mean - half * along) * (inv * math.sqrt(1.0 / math.pi))
        gm_low = gmid.astype(bf16)
        gm[:, here] = gm_low
        go = dot(wpt[...], gm_low)
        yield True
        dpr[:, 0:112] += dot_nt(gm_low, oaug[...])
        go_low = (go * inv_sum).astype(bf16)
        goaug[0:D, :] = go_low
        goaug[D:, :] = two_rows(jnp.sum(go_low.astype(f32) * mixed_ref[...], axis=0, keepdims=True))
        spread = dot(vbt[...], goaug[...])
        yield True
        gv[0:D, 0:KK] += dot_nt(go_low, low_ref[...])
        gse[0:KK, :] = (weight_ref[...] * spread).astype(bf16)
        back = dot(a2[...], gse[0:KK, :])
        yield True
        gse[KK : KK + D, :] = unskew_rows(back[D : D + 24], row).astype(bf16)
        gse[KK + D : KK + 256, :] = unskew_columns(back[D + 24 : D + 48], col).astype(bf16)
        yield True
        outer = dot_nt(qb[:, here], gse[...])
        gkr[0:D, 0 : KK + 256] += outer
        hacc[i] = outer[:, 384:512]
        gq[:, inner(i, tile)] = go + SCORE_SCALE * back[0:D] + dot(relt[...], gse[KK : KK + 256, :])

    one, two = slots
    gy_copy.wait()

    def attend(k, carry):
        interleave(ahead(2 * k + 1, two), behind(2 * k, one))
        interleave(ahead(2 * k + 2, one), behind(2 * k + 1, two))
        return carry

    interleave(ahead(0, one))
    lax.fori_loop(0, (TILES - 1) // 2, attend, 0)
    if TILES % 2 == 0:
        interleave(ahead(TILES - 1, two), behind(TILES - 2, one))
        interleave(behind(TILES - 1, two))
    else:
        interleave(behind(TILES - 1, one))

    out_copy = pltpu.make_async_copy(out_ref, out_hbm, copy_sem.at[2])
    out_copy.start()
    mid_copy = pltpu.make_async_copy(gm, mid_hbm, copy_sem.at[3])
    mid_copy.start()

    gkt[...] = jnp.transpose(gkr[:, 0:512])[0:KK, :] * SCORE_SCALE
    gvt[...] = jnp.transpose(gv[...])[0:KK, :]

    def pool_gradient(name, columns):
        low = columns.astype(bf16)
        for i in range(9):
            spread = dot_nt(low, tsel_ref[i]) * zsel_ref[i].astype(f32)
            gr[ROW[name] + i : ROW[name] + i + 1, 0:D] = jnp.sum(spread, axis=0, keepdims=True)

    for field, kernel_rows, pooled, gspread, name in ((fk, kk, gkt, gfk, "pool_k"), (fv, kv, gvt, gfv, "pool_v")):
        taps = tap_rows(kernel_rows)
        sums = [jnp.zeros((KG, 128), f32) for _ in range(9)]
        for a in range(KG):
            grad = pooled[KG * a : KG * a + KG, :]
            inside = jnp.where(b_index == 0, 0.0, grad)
            for k in range(9):
                where = pl.ds(tap_start(a, k // 3, k % 3), KG, stride=KSTR)
                sums[k] = sums[k] + (inside if k % 3 == 0 else grad) * field[where, :]
            spread_keys(taps, grad, a, gspread)
        rows = [jnp.sum(total, axis=0, keepdims=True) for total in sums]
        rows = jnp.concatenate(rows + [jnp.zeros((128 - 9, 128), f32)], axis=0)
        pool_gradient(name, jnp.transpose(rows)[:D, :])

    def finish(i, carry):
        tile = TILE_THREE
        wide = tile + 2 * HALO
        here = plain(i, tile)
        mid = slice(HALO, HALO + tile)
        mask = token_mask(i, tile)
        col = jnp.broadcast_to(idx_ref[1:2, inner(i, tile)], (8, tile))
        first, last = col == 0, col == GRID - 1
        for pair in range(D // 16):
            fields, moved = [], []
            for half in range(2):
                ch = slice(16 * pair + 8 * half, 16 * pair + 8 * half + 8)
                grad = gq[ch, window(i, tile)]
                below, above = pltpu.roll(grad, wide - GRID, 1), pltpu.roll(grad, GRID, 1)

                def col_sum(v):
                    return tap(v, ch, wide) * below + tap(v + 3, ch, wide) * grad + tap(v + 6, ch, wide) * above

                after = jnp.where(last, 0.0, pltpu.roll(col_sum(0), wide - 1, 1)[:, mid])
                before = jnp.where(first, 0.0, pltpu.roll(col_sum(2), 1, 1)[:, mid])
                fields.append((after + col_sum(1)[:, mid] + before) * mask)
                moved.append((below[:, mid], grad[:, mid], above[:, mid]))
            gfield[16 * pair : 16 * pair + 16, here] = jnp.concatenate(fields, axis=0).astype(bf16)
            for u in range(3):
                both = jnp.concatenate([moved[0][u], moved[1][u]], axis=0)
                gsh[u * D + 16 * pair : u * D + 16 * pair + 16, :] = both.astype(bf16)
        kqacc[:, 0 : 3 * D] += dot_nt(gsh[...], fcol[:, here])
        flat = pl.ds(pl.multiple_of(i * tile + LEAD, 8), tile)
        gkv[:, 0:128] = gfk[flat, :].astype(bf16)
        gkv[:, 128:256] = gfv[flat, :].astype(bf16)
        dwq[:, 0:112] += dot_nt(gfield[:, here], un[:, here])
        dwkv[0:112, :] += dot(un[:, here], gkv[...])
        field_copy(i).start()
        return carry

    def field_copy(i):
        here = plain(i, TILE_THREE)
        return pltpu.make_async_copy(gfield.at[:, here], field_hbm.at[:, here], copy_sem.at[5 + i])

    lax.fori_loop(0, TOK // TILE_THREE, finish, 0)
    out_copy.wait()
    mid_copy.wait()
    unit_copy.wait()

    def write(name, rows, first=0):
        base = ROW[name] + first
        gr[base : base + rows.shape[0], 0:D] = rows

    def wide_rows(rows):
        return jnp.concatenate([rows, jnp.zeros((rows.shape[0], 128 - D), f32)], axis=1)

    def through_norm(name, first, outer, bias, gain_row, shift_row):
        raw = piece(name, outer.shape[0], first)[:, :D]
        write(name, outer * gain_row[:, :D] + bias * shift_row[:, :D], first)
        return jnp.sum(raw * outer, axis=0, keepdims=True), jnp.sum(raw * bias, axis=0, keepdims=True)

    gain, shift = through_norm("w_qkv", 0, dwq[:, 0:D], dwq[:, D : D + 1], g1_row, b1_row)
    write("b_qkv", jnp.transpose(dwq[...])[D : D + 1, :])
    for k in (1, 2):
        turned = jnp.transpose(dwkv[:, 128 * k - 128 : 128 * k])[0:D, :]
        more_gain, more_shift = through_norm("w_qkv", k * D, turned[:, 0:D], turned[:, D : D + 1], g1_row, b1_row)
        gain, shift = gain + more_gain, shift + more_shift
        write("b_qkv", dwkv[D : D + 1, 128 * k - 128 : 128 * k - 128 + D], k)
    write("ln1_g", gain)
    write("ln1_b", shift)

    lane = lax.broadcasted_iota(jnp.int32, (D, 128), 1)
    wide_lane = lax.broadcasted_iota(jnp.int32, (D, 3 * 128), 1) - lax.broadcasted_iota(jnp.int32, (D, 3 * 128), 0)
    columns = jnp.zeros((D, 128), f32)
    for k in range(9):
        u, v = k // 3, k % 3
        one = jnp.where(wide_lane == v * D, kqacc[u * D : u * D + D, :], 0.0)
        columns = jnp.where(lane == k, jnp.sum(one, axis=1, keepdims=True), columns)
    pool_gradient("pool_q", columns)

    for i in range(TILES):
        turned = jnp.transpose(hacc[i])
        for k in range(4):
            count = KG + ROW_STEPS - 1
            where = pl.ds(ROW["rel_h"] + 3 + k + TILE_ROWS * i, count, stride=4)
            gr[where, :] = gr[where, :] + wide_rows(turned[16 + 24 * k : 16 + 24 * k + count])
    turned = jnp.transpose(gkr[0:D, 384:768])
    for k in range(4):
        gr[pl.ds(ROW["rel_w"] + 3 + k, 39, stride=4), :] = wide_rows(turned[112 + 40 * k : 151 + 40 * k])

    write("w_proj", dpr[:, 0:D])
    write("b_proj", jnp.transpose(dpr[...])[D : D + 1, :])
    turned = jnp.transpose(dw1[...])
    gain, shift = through_norm(
        "w_fc1", 0, turned[:, 0:D] * math.sqrt(2.0 / math.pi), turned[:, D : D + 1] * math.sqrt(1.0 / math.pi), g2_row, b2_row
    )
    write("ln2_g", gain)
    write("ln2_b", shift)
    for k in range(4):
        write("b_fc1", dw1[D : D + 1, k * D : (k + 1) * D] * math.sqrt(1.0 / math.pi), k)
        gr[pl.ds(ROW["w_fc2"] + k, D, stride=4), :] = wide_rows(dw2[:, k * D : (k + 1) * D] * math.sqrt(2.0 / math.pi))
    write("b_fc2", jnp.transpose(dw2[:, HID:512])[0:1, :])
    for i in range(TOK // TILE_THREE):
        field_copy(i).wait()
    for w, start in enumerate(starts):
        gchunk_ref[w] = gr[start : start + rows_of, 0:D].astype(bf16)


def image_step(shard_len, chunks, pixels, image_side, cotangent):
    starts = tuple((shard_len * w) // D for w in range(chunks.shape[0]))
    rows_of = block_rows(shard_len)
    groups = -(-(shard_len * len(starts)) // (4 * D))
    depth = max(8 * (-(-(starts[-1] + rows_of) // 8)), 4 * groups)
    flat_rows = max(3 * groups, (shard_len * (len(starts) - 1)) // 128 + chunks.shape[1] + 1)
    flat_rows = 8 * (-(-flat_rows // 8))
    zsel, tsel = pool_selectors()
    vm = pltpu.VMEM
    scratch = [
        vm((depth, 128), f32),
        vm((D, 112), bf16), vm((112, 128), bf16), vm((112, 128), bf16),
        vm((D, 112), bf16), vm((D, D), bf16),
        vm((HID, 112), bf16), vm((D, HID), bf16), vm((D, KK), bf16), vm((HID, D), bf16),
        vm((168, 128), f32), vm((256, D), bf16), vm((D, 256), bf16),
        vm((D, 128), f32), vm((9, D, 128), f32),
        vm((D, TOK + 2 * HALO), f32), vm((FIELD, 128), f32), vm((FIELD, 128), f32),
        vm((D, TOK), bf16), vm((D, TOK), bf16),
        vm((112, TOK), bf16), vm((3 * D, TOK), bf16),
        vm((KK, 208), bf16), vm((144, KK), bf16), vm((112, KK), bf16), vm((KK, 112), bf16),
        vm((KK, 128), f32), vm((KK, 128), f32),
        vm((208, TILE_TWO), bf16), vm((KK + 256, TILE_TWO), bf16), vm((112, TILE_PROJECT), bf16), vm((112, TILE_TWO), bf16),
        vm((3 * D, TILE_THREE), bf16), vm((TILE_THREE, 256), bf16),
        vm((D, 512), f32), vm((128, HID), f32), vm((D, 128), f32), vm((128, 512), f32), vm((128, 768), f32),
        vm((TILES, D, 128), f32),
        vm((D, 128), f32), vm((128, 256), f32), vm((3 * D, 3 * 128), f32),
        vm((depth, 128), f32),
        vm((D, TOK), bf16), vm((D, TOK), bf16), vm((D, TOK), bf16), vm((D, TOK), bf16),
        pltpu.SemaphoreType.DMA((5 + TOK // TILE_THREE,)),
        vm((flat_rows, 128), f32),
        vm(zsel.shape, bf16), vm(tsel.shape, bf16), vm((8, TOK + 2 * HALO), jnp.int32), pltpu.SemaphoreType.DMA((3,)),
    ]
    slot = [
        vm((KK, TILE_TWO), f32), vm((KK, TILE_TWO), bf16), vm((D, TILE_TWO), f32), vm((D, TILE_TWO), f32), vm((HID, TILE_TWO), f32),
        vm((KK, TILE_TWO), bf16), vm((112, TILE_TWO), bf16), vm((112, TILE_TWO), bf16), vm((8, TILE_TWO), f32),
    ]
    whole = pl.BlockSpec(memory_space=pltpu.VMEM)
    far = pl.BlockSpec(memory_space=pl.ANY)
    shape = jax.ShapeDtypeStruct
    out, grad_chunks, *rest = pl.pallas_call(
        functools.partial(image_kernel, shard_len, starts, rows_of),
        out_shape=(
            shape((D, TOK), bf16), shape((len(starts), rows_of, D), bf16),
            shape((D, TOK), bf16), shape((D, TOK), bf16), shape((D, TOK), bf16), shape((8, TOK), f32),
            shape((KK, 128), f32), shape((KK, 128), f32), shape((16, 128), f32), shape((16, 128), f32),
            shape((D, D), bf16), shape((D, 256), bf16),
        ),
        in_specs=[pl.BlockSpec(memory_space=pltpu.SMEM), whole, far, far, far, far, far],
        out_specs=(far, whole, far, far, far) + (whole,) * 7,
        scratch_shapes=scratch + slot + slot,
        compiler_params=pltpu.CompilerParams(vmem_limit_bytes=54 * 1024 * 1024),
        name="image_step",
    )(image_side, chunks, pixels, cotangent, lane_index(), zsel, tsel)
    return out, grad_chunks, rest


def input_step(rest):
    far = pl.BlockSpec(memory_space=pl.ANY)
    vm = pltpu.VMEM
    scratch = [vm(part.shape, part.dtype) for part in rest]
    scratch += [vm((D, TOK), bf16), vm((FIELD, 128), f32), vm((FIELD, 128), f32), vm((TILE_THREE, 256), bf16)]
    return pl.pallas_call(
        input_kernel,
        out_shape=jax.ShapeDtypeStruct((D, TOK), bf16),
        in_specs=[far] * len(rest),
        out_specs=far,
        scratch_shapes=scratch + [pltpu.SemaphoreType.DMA((10 + TOK // TILE_THREE,))],
        compiler_params=pltpu.CompilerParams(vmem_limit_bytes=60 * 1024 * 1024),
        cost_estimate=pl.CostEstimate(flops=2 * D * 3 * D * TOK, bytes_accessed=16 * 1024 * 1024, transcendentals=0),
        name="input_step",
    )(*rest)


def adam_update(gradient, master_part, first_part, second_part, average_part, step_rates):
    moment_one = beta_first * first_part + (1.0 - beta_first) * gradient
    moment_two = beta_second * second_part + (1.0 - beta_second) * gradient * gradient
    fix_one = 1.0 - beta_first**STEP
    fix_two = 1.0 - beta_second**STEP
    direction = moment_one / fix_one / (jnp.sqrt(moment_two / fix_two) + adam_eps)
    updated = master_part - step_rates * (direction + weight_decay * master_part)
    blended = average_decay * average_part + (1.0 - average_decay) * updated
    return (updated, moment_one, moment_two, blended)


def shards(tokens, image_sides, grad_out, master, first_moment, second_moment, weight_average):
    shard_len = master.shape[0]
    owners = lax.axis_size("wide")
    images_all = tokens.shape[0] * owners * lax.axis_size("narrow")
    rows_of = block_rows(shard_len)
    inset = lax.rem(lax.axis_index("wide") * shard_len, D)

    filled = 1024 * (-(-shard_len // 1024))
    own = jnp.pad(master, (0, filled - shard_len)).reshape(1, filled // 128, 128).astype(bf16)
    chunks = lax.all_to_all(jnp.broadcast_to(own, (owners, filled // 128, 128)), "wide", 0, 0)

    outs, grads_in, grad_chunks = [], [], None
    for k in range(tokens.shape[0]):
        out, chunk, rest = image_step(shard_len, chunks, tokens[k], image_sides[k : k + 1], grad_out[k])
        outs.append(out)
        grads_in.append(input_step(rest))
        grad_chunks = chunk if k == 0 else (grad_chunks.astype(f32) + chunk.astype(f32)).astype(bf16)
    block_out = jnp.stack(outs)
    grad_in = jnp.stack(grads_in)

    parts = lax.all_to_all(grad_chunks, "wide", 0, 0)
    parts, grad_in = lax.optimization_barrier((parts, grad_in))
    total = jnp.sum(parts.astype(f32), axis=0)
    total = total + lax.ppermute(total, "narrow", [(0, 1), (1, 0)])
    reduced = lax.dynamic_slice(total.reshape(rows_of * D), (inset,), (shard_len,))
    step_rates = lax.dynamic_slice_in_dim(
        jnp.asarray(rate_values(shard_len * owners)), lax.axis_index("wide") * shard_len, shard_len
    )
    updated, moment_one, moment_two, blended = adam_update(
        reduced / images_all, master, first_moment, second_moment, weight_average, step_rates
    )
    return (block_out, grad_in, updated, moment_one, moment_two, blended)


def solution(mesh):
    return jax.shard_map(
        shards,
        mesh=mesh,
        in_specs=(
            P(("wide", "narrow"), None, None),
            P(("wide", "narrow")),
            P(("wide", "narrow"), None, None),
            P("wide"),
            P("wide"),
            P("wide"),
            P("wide"),
        ),
        out_specs=(
            P(("wide", "narrow"), None, None),
            P(("wide", "narrow"), None, None),
            P("wide"),
            P("wide"),
            P("wide"),
            P("wide"),
        ),
        check_vma=False,
    )
```

```python
import functools
import math

import jax
import jax.numpy as jnp
import numpy as np
from jax import lax
from jax.experimental import pallas as pl
from jax.experimental.pallas import tpu as pltpu
from jax.sharding import PartitionSpec as P

D = 96
HID = 384
KSTR = 4
KG = 20
STEP = 5
GRID = 80
TOK = 6400
KK = 400
REL = 159

norm_eps = 1e-06
beta_first = 0.5
beta_second = 0.5
adam_eps = 1e-08
weight_decay = 0.05
rate_factor = 0.4
average_decay = 0.8

f32 = jnp.float32
bf16 = jnp.bfloat16

HALO = 128
LEAD = 88
FIELD = LEAD + TOK + 8
TILE_PROJECT = 6400
TILE_ONE = 6400
TILE_TWO = 1280
TILE_THREE = 1280
TILES = TOK // TILE_TWO
TILE_ROWS = TILE_TWO // GRID
ROW_STEPS = TILE_ROWS // KSTR
SCORE_SCALE = D ** (-0.5)
LOG2E = 1.4426950408889634


def segment_list():
    return [
        ("w_qkv", (3 * D, D), D ** (-0.5)),
        ("b_qkv", (3 * D,), 0.2),
        ("pool_q", (D, 9), 1.0 / 3.0),
        ("pool_k", (D, 9), 1.0 / 3.0),
        ("pool_v", (D, 9), 1.0 / 3.0),
        ("rel_h", (REL, D), 0.5 * D ** (-0.5)),
        ("rel_w", (REL, D), 0.5 * D ** (-0.5)),
        ("w_proj", (D, D), D ** (-0.5)),
        ("b_proj", (D,), 0.2),
        ("w_fc1", (HID, D), D ** (-0.5)),
        ("b_fc1", (HID,), 0.2),
        ("w_fc2", (D, HID), HID ** (-0.5)),
        ("b_fc2", (D,), 0.2),
        ("ln1_g", (D,), 0.5),
        ("ln1_b", (D,), 0.2),
        ("ln2_g", (D,), 0.5),
        ("ln2_b", (D,), 0.2),
    ]


def row_bases():
    bases = {}
    offset = 0
    for name, shape, _ in segment_list():
        assert offset % D == 0
        bases[name] = offset // D
        offset += math.prod(shape)
    return bases


ROW = row_bases()


def rate_values(full_len):
    rates = np.full((full_len,), rate_factor * D ** (-0.5), np.float32)
    offset = 0
    for _, shape, spread in segment_list():
        length = math.prod(shape)
        rates[offset : offset + length] = rate_factor * spread
        offset += length
    return rates


def block_rows(shard_len):
    return 16 * (-(-(-(-(shard_len + D - 1) // D)) // 16))


def pool_selectors():
    flat = np.arange(9 * D).reshape(9, D)
    channel = (flat[:, None, :] // 9 == np.arange(D)[None, :, None]).astype(np.float32)
    tap = (flat[:, :, None] % 9 == np.arange(128)[None, None, :]).astype(np.float32)
    return jnp.asarray(channel, bf16), jnp.asarray(tap, bf16)


def lane_index():
    place = np.arange(-HALO, TOK + HALO)
    table = np.zeros((8, TOK + 2 * HALO), np.int32)
    table[0] = place // GRID
    table[1] = place % GRID
    return jnp.asarray(table)


def dot(a, b):
    return lax.dot_general(a, b, (((1,), (0,)), ((), ())), preferred_element_type=f32)


def dot_nt(a, b):
    return lax.dot_general(a, b, (((1,), (1,)), ((), ())), preferred_element_type=f32)


def dot_tn(a, b):
    return lax.dot_general(a, b, (((0,), (0,)), ((), ())), preferred_element_type=f32)


def normalize(values):
    mean = jnp.sum(values, axis=0, keepdims=True) * (1.0 / D)
    center = values - mean
    spread = jnp.sum(center * center, axis=0, keepdims=True) * (1.0 / D)
    inv = lax.rsqrt(spread + norm_eps)
    return center * inv, inv


def skew_rows(rows, place):
    width = rows.shape[1]
    where = jnp.broadcast_to(place, (24, width))
    residue = where & 3
    x = jnp.where(
        residue < 2,
        jnp.where(residue == 0, rows[0:24], rows[24:48]),
        jnp.where(residue == 2, rows[48:72], rows[72:96]),
    )
    step = ROW_STEPS // 2
    while step >= 1:
        x = jnp.where((where & (4 * step)) != 0, pltpu.roll(x, 24 - step, 0), x)
        step //= 2
    return x


def skew_columns(rows, place):
    width = rows.shape[1]
    where = jnp.broadcast_to(place, (40, width))
    residue = where & 3
    x = jnp.where(
        residue < 2,
        jnp.where(residue == 0, rows[0:40], rows[40:80]),
        jnp.where(residue == 2, rows[80:120], rows[120:160]),
    )
    x = jnp.concatenate([jnp.where((where[0:24] & 64) != 0, x[16:40], x[0:24]), x[24:40]], axis=0)
    x = jnp.where((where[0:32] & 32) != 0, x[8:40], x[0:32])
    where = where[0:24]
    x = jnp.where((where & 16) != 0, pltpu.roll(x, 28, 0)[0:24], x[0:24])
    x = jnp.where((where & 8) != 0, pltpu.roll(x, 22, 0), x)
    return jnp.where((where & 4) != 0, pltpu.roll(x, 23, 0), x)


def unskew_rows(x, place):
    where = jnp.broadcast_to(place, x.shape)
    step = 1
    while step < ROW_STEPS:
        x = jnp.where((where & (4 * step)) != 0, pltpu.roll(x, step, 0), x)
        step *= 2
    residue = where & 3
    return jnp.concatenate([jnp.where(residue == k, x, 0.0) for k in range(4)], axis=0)


def unskew_columns(x, place):
    width = x.shape[1]
    zero = jnp.zeros((8, width), f32)
    where = jnp.broadcast_to(place, (40, width))
    x = jnp.where((where[0:24] & 4) != 0, pltpu.roll(x, 1, 0), x)
    x = jnp.where((where[0:24] & 8) != 0, pltpu.roll(x, 2, 0), x)
    x = jnp.concatenate([x, zero], axis=0)
    x = jnp.where((where[0:32] & 16) != 0, pltpu.roll(x, 4, 0), x)
    x = jnp.where((where & 32) != 0, jnp.concatenate([zero, x], axis=0), jnp.concatenate([x, zero], axis=0))
    far = (where & 64) != 0
    x = jnp.concatenate([jnp.where(far[0:16], 0.0, x[0:16]), jnp.where(far[16:40], x[0:24], x[16:40])], axis=0)
    residue = where & 3
    return jnp.concatenate([jnp.where(residue == k, x, 0.0) for k in range(4)], axis=0)


def aligned(value, step):
    return value if isinstance(value, int) else pl.multiple_of(value, step)


def interleave(*parts):
    live = list(parts)
    while live:
        for part in list(live):
            if next(part, None) is None:
                live.remove(part)


def two_columns(column):
    high = column.astype(bf16).astype(f32)
    place = lax.broadcasted_iota(jnp.int32, (column.shape[0], 16), 1)
    return jnp.where(place == 0, high, jnp.where(place == 1, column - high, 0.0)).astype(bf16)


def two_rows(row):
    high = row.astype(bf16).astype(f32)
    place = lax.broadcasted_iota(jnp.int32, (16, row.shape[1]), 0)
    return jnp.where(place == 0, high, jnp.where(place == 1, row - high, 0.0)).astype(bf16)


def two_ones(width):
    return jnp.where(lax.broadcasted_iota(jnp.int32, (16, width), 0) < 2, 1.0, 0.0).astype(bf16)


def key_columns():
    return lax.broadcasted_iota(jnp.int32, (KG, 128), 0)


def tap_start(a, u, v):
    return LEAD + GRID * (KSTR * a + u - 1) + v - 1


def tap_rows(kernel_rows):
    b_index = key_columns()
    taps = [jnp.broadcast_to(kernel_rows[k : k + 1, :], (KG, 128)) for k in range(9)]
    return [jnp.where(b_index == 0, 0.0, tap) if k % 3 == 0 else tap for k, tap in enumerate(taps)]


def spread_keys(taps, grad, a, gfield):
    idle = LEAD + GRID * (KSTR * a + 2)
    gfield[pl.ds(aligned(idle - 8, 8), GRID + 8), :] = jnp.zeros((GRID + 8, 128), f32)
    for u in range(3):
        gfield[pl.ds(tap_start(a, u, 3), KG, stride=KSTR), :] = jnp.zeros((KG, 128), f32)
    for k in range(9):
        gfield[pl.ds(tap_start(a, k // 3, k % 3), KG, stride=KSTR), :] = taps[k] * grad


def input_kernel(*refs):
    sources, gin_hbm, held = refs[:10], refs[10], refs[11:21]
    field_ref, mid_ref, unit_ref, inv_ref, gkt, gvt, kk, kv, wqt, wkvg = held
    gin_ref, gfk, gfv, gkv, copy_sem = refs[21:]
    copies = [pltpu.make_async_copy(a, b, copy_sem.at[k]) for k, (a, b) in enumerate(zip(sources, held))]
    for copy in copies[::-1]:
        copy.start()
    for copy in copies[4:]:
        copy.wait()
    for kernel_rows, pooled, gfield in ((kk, gkt, gfk), (kv, gvt, gfv)):
        taps = tap_rows(kernel_rows)

        def spread(a, carry):
            spread_keys(taps, pooled[pl.ds(KG * a, KG), :], a, gfield)
            return carry

        lax.fori_loop(0, KG, spread, 0)
        gfield[LEAD + TOK - GRID : LEAD + TOK, :] = jnp.zeros((GRID, 128), f32)
    for copy in copies[:4]:
        copy.wait()

    def gin_copy(i):
        here = pl.ds(aligned(i * TILE_THREE, 128), TILE_THREE)
        return pltpu.make_async_copy(gin_ref.at[:, here], gin_hbm.at[:, here], copy_sem.at[10 + i])

    def finish(i, carry):
        tile = TILE_THREE
        here = pl.ds(aligned(i * tile, 128), tile)
        flat = pl.ds(aligned(i * tile + LEAD, 8), tile)
        gkv[:, 0:128] = gfk[flat, :].astype(bf16)
        gkv[:, 128:256] = gfv[flat, :].astype(bf16)
        gn = dot(wqt[...], field_ref[:, here]) + dot_nt(wkvg[...], gkv[...])
        unit = unit_ref[:, here].astype(f32)
        mean = jnp.sum(gn, axis=0, keepdims=True) * (1.0 / D)
        along = jnp.sum(gn * unit, axis=0, keepdims=True) * (1.0 / D)
        total = mid_ref[:, here].astype(f32) + (gn - mean - unit * along) * inv_ref[0:1, here]
        gin_ref[:, here] = total.astype(bf16)
        gin_copy(i).start()
        return carry

    lax.fori_loop(0, TOK // TILE_THREE, finish, 0)
    for i in range(TOK // TILE_THREE):
        gin_copy(i).wait()


def image_kernel(
    shard_len,
    starts,
    rows_of,
    side_ref,
    chunk_ref,
    x_hbm,
    gy_hbm,
    idx_hbm,
    zsel_hbm,
    tsel_hbm,
    out_hbm,
    gchunk_ref,
    field_hbm,
    mid_hbm,
    unit_hbm,
    inv_ref,
    gkt,
    gvt,
    kk,
    kv,
    wqt,
    wkvg,
    wf, wq, wkt, wvt, wp, wpt, w1, w1t, w2, w2t, relh, rel, relt, cols, kq,
    fq, fk, fv, qb, gm, un, fcol,
    a1, a2, vb, vbt, kp, vpool,
    rhs, gse, n1aug, goaug, gsh, gkv,
    dw2, dw1, dpr, gv, gkr, hacc, dwq, dwkv, kqacc, gr, x_ref, gy_ref, out_ref, gfield, copy_sem, flat, zsel_ref, tsel_ref, idx_ref, table_sem,
    *slot_refs,
):
    gq, gfk, gfv = fq, fk, fv
    slots = (slot_refs[: len(slot_refs) // 2], slot_refs[len(slot_refs) // 2 :])
    side = side_ref[0]
    table_copies = [
        pltpu.make_async_copy(source, target, table_sem.at[k])
        for k, (source, target) in enumerate(((zsel_hbm, zsel_ref), (tsel_hbm, tsel_ref), (idx_hbm, idx_ref)))
    ]
    for copy in table_copies:
        copy.start()
    x_copy = pltpu.make_async_copy(x_hbm, x_ref, copy_sem.at[0])
    gy_copy = pltpu.make_async_copy(gy_hbm, gy_ref, copy_sem.at[1])
    x_copy.start()
    gy_copy.start()

    flat[...] = jnp.zeros(flat.shape, f32)
    lane_of = lax.broadcasted_iota(jnp.int32, chunk_ref.shape[1:], 1)
    for w in range(len(starts)):
        base, inset = (shard_len * w) // 128, (shard_len * w) % 128
        part = chunk_ref[w].astype(f32)
        if inset:
            part = pltpu.roll(part, inset, 1)
            flat[base + 1 : base + 1 + part.shape[0], :] += jnp.where(lane_of < inset, part, 0.0)
            part = jnp.where(lane_of < inset, 0.0, part)
        flat[base : base + part.shape[0], :] += part
    groups = -(-(shard_len * len(starts)) // (4 * D))
    lane_of = lax.broadcasted_iota(jnp.int32, (groups, 128), 1)
    first, second, third = (flat[pl.ds(k, groups, stride=3), :] for k in range(3))
    wf[pl.ds(0, groups, stride=4), :] = first
    wf[pl.ds(1, groups, stride=4), :] = pltpu.roll(jnp.where(lane_of >= 96, first, second), 32, 1)
    wf[pl.ds(2, groups, stride=4), :] = pltpu.roll(jnp.where(lane_of >= 64, second, third), 64, 1)
    wf[pl.ds(3, groups, stride=4), :] = pltpu.roll(third, 96, 1)

    def piece(name, count, first=0):
        base = ROW[name] + first
        return wf[base : base + count, :]

    vec_rows = [ROW["b_qkv"], ROW["b_proj"], ROW["b_fc2"], ROW["ln1_g"], ROW["ln1_b"], ROW["ln2_g"], ROW["ln2_b"]]
    vec_rows += [ROW["b_fc1"] + k for k in range(4)]
    stacked = jnp.concatenate([wf[r : r + 1, :] for r in vec_rows] + [jnp.zeros((128 - len(vec_rows), 128), f32)], axis=0)
    cols[...] = jnp.transpose(stacked)[:D, :]
    cols_low = cols[...].astype(bf16)
    g1_row, b1_row = piece("ln1_g", 1), piece("ln1_b", 1)
    g2_row, b2_row = piece("ln2_g", 1), piece("ln2_b", 1)

    def through(name, count, first, column):
        return dot(piece(name, count, first)[:, :D].astype(bf16), cols_low)[:, column : column + 1]

    wq_gain = piece("w_qkv", D) * g1_row
    wq[:, 0:D] = piece("w_qkv", D)[:, :D].astype(bf16)
    wq[:, D:] = two_columns(cols[:, 0:1])
    wqt[...] = jnp.transpose(wq_gain)[:D, :].astype(bf16)
    for k, ref in ((1, wkt), (2, wvt)):
        ref[...] = jnp.zeros(ref.shape, bf16)
        ref[0:D, 0:D] = jnp.transpose(piece("w_qkv", D, k * D))[:D, :].astype(bf16)
        ref[D:, 0:D] = two_rows(piece("b_qkv", 1, k)[:, :D])
        wkvg[:, 128 * k - 128 : 128 * k] = jnp.zeros((D, 128), bf16)
        wkvg[:, 128 * k - 128 : 128 * k - 128 + D] = jnp.transpose(piece("w_qkv", D, k * D) * g1_row)[:D, :].astype(bf16)
    wp[:, 0:D] = piece("w_proj", D)[:, :D].astype(bf16)
    wp[:, D:] = two_columns(cols[:, 1:2])
    wpt[...] = jnp.transpose(piece("w_proj", D))[:D, :].astype(bf16)
    w1_gain = piece("w_fc1", HID) * g2_row
    b_fc1 = jnp.concatenate([cols[:, 7 + k : 8 + k] for k in range(4)], axis=0)
    w1[:, 0:D] = w1_gain[:, :D].astype(bf16)
    w1[:, D:] = two_columns((b_fc1 + through("w_fc1", HID, 0, 6)) * math.sqrt(0.5))
    w1t[...] = jnp.transpose(w1_gain)[:D, :].astype(bf16)
    for k in range(4):
        block = wf[pl.ds(ROW["w_fc2"] + k, D, stride=4), :]
        w2t[k * D : (k + 1) * D, :] = jnp.transpose(block)[:D, :].astype(bf16)
    w2[:, 0:HID] = jnp.transpose(w2t[...].astype(f32)).astype(bf16)
    w2[:, HID:] = two_columns(cols[:, 2:3] * math.sqrt(0.5 * math.pi))
    relh[160:, :] = jnp.zeros((8, 128), f32)
    for k in range(4):
        relh[k * 40 : k * 40 + 40, :] = wf[pl.ds(ROW["rel_h"] + 3 + k, 40, stride=4), :]
    rel_w = jnp.concatenate([wf[pl.ds(ROW["rel_w"] + 3 + k, 40, stride=4), :] for k in range(4)], axis=0)
    rel[D:256, :] = rel_w[:, :D].astype(bf16)
    relt[:, D:256] = jnp.transpose(rel_w)[:D, :].astype(bf16)

    def pool_columns(name):
        total = jnp.zeros((D, 128), f32)
        for i in range(9):
            row = wf[ROW[name] + i : ROW[name] + i + 1, :][:, :D]
            total = total + dot((zsel_ref[i].astype(f32) * row).astype(bf16), tsel_ref[i])
        return total

    def pool_rows(name):
        full = jnp.concatenate([pool_columns(name), jnp.zeros((32, 128), f32)], axis=0)
        return jnp.transpose(full)[0:16, :]

    for copy in table_copies:
        copy.wait()
    pooled_kernel = pool_columns("pool_q")
    for k in range(9):
        kq[k] = jnp.broadcast_to(pooled_kernel[:, k : k + 1], (D, 128))

    def tap(k, ch, width):
        return jnp.concatenate([kq[k, ch, :]] * (width // 128), axis=1)

    kk[...] = pool_rows("pool_k")
    kv[...] = pool_rows("pool_v")

    for ref in (fq,):
        ref[:, 0:HALO] = jnp.zeros((D, HALO), f32)
        ref[:, HALO + TOK :] = jnp.zeros((D, HALO), f32)
    for ref in (fk, fv):
        ref[0:LEAD, :] = jnp.zeros((LEAD, 128), f32)
    for ref in (dw2, dw1, dpr, gv, gkr, dwq, dwkv, kqacc):
        ref[...] = jnp.zeros(ref.shape, ref.dtype)
    gr[ROW["rel_h"] : ROW["w_proj"], :] = jnp.zeros((2 * REL, 128), f32)
    tail = ROW["ln2_b"]
    gr[tail:, :] = jnp.zeros((gr.shape[0] - tail, 128), f32)

    un[D:, :] = two_ones(TOK)
    n1aug[D:, :] = two_ones(TILE_PROJECT)
    for slot in slots:
        slot[5][HID:, :] = two_ones(TILE_TWO)
        slot[6][D:, :] = two_ones(TILE_TWO)
        slot[7][D:, :] = two_ones(TILE_TWO)
    rhs[192:208, :] = two_ones(TILE_TWO)

    def window(i, tile):
        return pl.ds(aligned(i * tile, 128), tile + 2 * HALO)

    def inner(i, tile):
        return pl.ds(aligned(i * tile + HALO, 128), tile)

    def plain(i, tile):
        return pl.ds(aligned(i * tile, 128), tile)

    def token_mask(i, tile):
        place = idx_ref[0:2, inner(i, tile)]
        return jnp.where((place[0:1] < side) & (place[1:2] < side), 1.0, 0.0)

    x_copy.wait()

    def project(i, carry):
        here = plain(i, TILE_PROJECT)
        unit, inv = normalize(x_ref[:, here].astype(f32))
        un[0:D, here] = unit.astype(bf16)
        inv_ref[0:1, here] = inv
        n1aug[0:D, :] = (unit * cols[:, 3:4] + cols[:, 4:5]).astype(bf16)
        fq[:, inner(i, TILE_PROJECT)] = dot(wq[...], n1aug[...]) * token_mask(i, TILE_PROJECT)
        field = pl.ds(pl.multiple_of(i * TILE_PROJECT + LEAD, 8), TILE_PROJECT)
        fk[field, :] = dot_tn(n1aug[...], wkt[...])
        fv[field, :] = dot_tn(n1aug[...], wvt[...])
        return carry

    lax.fori_loop(0, TOK // TILE_PROJECT, project, 0)

    unit_copy = pltpu.make_async_copy(un.at[0:D, :], unit_hbm, copy_sem.at[4])
    unit_copy.start()

    def pool_queries(i, carry):
        tile = TILE_ONE
        wide = tile + 2 * HALO
        mid = slice(HALO, HALO + tile)
        col = jnp.broadcast_to(idx_ref[1:2, window(i, tile)], (8, wide))
        first, last = col == 0, col == GRID - 1
        mask = token_mask(i, tile)
        for pair in range(D // 16):
            pooled, moved = [], []
            for half in range(2):
                ch = slice(16 * pair + 8 * half, 16 * pair + 8 * half + 8)
                field = fq[ch, window(i, tile)]
                left = jnp.where(first, 0.0, pltpu.roll(field, 1, 1))
                right = jnp.where(last, 0.0, pltpu.roll(field, wide - 1, 1))

                def row_sum(u):
                    return tap(3 * u, ch, wide) * left + tap(3 * u + 1, ch, wide) * field + tap(3 * u + 2, ch, wide) * right

                total = pltpu.roll(row_sum(0), GRID, 1) + row_sum(1) + pltpu.roll(row_sum(2), wide - GRID, 1)
                pooled.append(total[:, mid] * mask)
                moved.append((left[:, mid], field[:, mid], right[:, mid]))
            qb[16 * pair : 16 * pair + 16, plain(i, tile)] = jnp.concatenate(pooled, axis=0).astype(bf16)
            for v in range(3):
                both = jnp.concatenate([moved[0][v], moved[1][v]], axis=0)
                fcol[v * D + 16 * pair : v * D + 16 * pair + 16, plain(i, tile)] = both.astype(bf16)
        return carry

    lax.fori_loop(0, TOK // TILE_ONE, pool_queries, 0)

    b_index = key_columns()

    for field, kernel_rows, pooled in ((fk, kk, kp), (fv, kv, vpool)):
        taps = tap_rows(kernel_rows)
        for a in range(KG):
            total = jnp.zeros((KG, 128), f32)
            for k in range(9):
                total = total + taps[k] * field[pl.ds(tap_start(a, k // 3, k % 3), KG, stride=KSTR), :]
            keep = (KSTR * b_index < side) & (KSTR * a < side)
            pooled[KG * a : KG * a + KG, :] = jnp.where(keep, total, 0.0)

    key = lax.broadcasted_iota(jnp.int32, (KK, 112), 0)
    key_a = lax.div(key, KG)
    key_b = key - KG * key_a
    place = lax.broadcasted_iota(jnp.int32, (KK, 112), 1)
    hot = jnp.zeros((KK, 112), f32)
    for base in (0, 48):
        one_a = (place >= base) & (place < base + 24) & (KG - 1 - key_a == place - base)
        one_b = (place >= base + 24) & (place < base + 48) & (KG - 1 - key_b == place - base - 24)
        hot = jnp.where(one_a | one_b, 1.0, hot)
    shut = (place == 96) & ((KSTR * key_a >= side) | (KSTR * key_b >= side))
    a1[:, 0:D] = kp[...][:, :D].astype(bf16)
    a1[:, D:] = jnp.where(shut, -1e30, hot).astype(bf16)
    vbt[:, 0:D] = vpool[...][:, :D].astype(bf16)
    vbt[:, D:] = jnp.where(lax.broadcasted_iota(jnp.int32, (KK, 16), 1) < 2, -1.0, 0.0).astype(bf16)
    a2[0:D, :] = jnp.transpose(kp[...])[:D, :].astype(bf16)
    vb[0:D, :] = jnp.transpose(vpool[...])[:D, :].astype(bf16)
    vb[D:, :] = jnp.ones((16, KK), bf16)
    key_l = lax.broadcasted_iota(jnp.int32, (48, KK), 1)
    a_l = lax.div(key_l, KG)
    b_l = key_l - KG * a_l
    row_l = lax.broadcasted_iota(jnp.int32, (48, KK), 0)
    hot_l = ((row_l < 24) & (KG - 1 - a_l == row_l)) | ((row_l >= 24) & (KG - 1 - b_l == row_l - 24))
    a2[D:, :] = jnp.where(hot_l, 1.0, 0.0).astype(bf16)

    def ahead(i, slot):
        weight_ref, low_ref, mixed_ref, half_ref, slope_ref, aaug, n2aug, oaug, scale_ref = slot
        tile = TILE_TWO
        here = plain(i, tile)
        row, col = idx_ref[0:1, inner(i, tile)] - i * TILE_ROWS, idx_ref[1:2, inner(i, tile)]
        near = [relh[pl.ds(40 * k + ROW_STEPS * i, 24), :] for k in range(4)]
        rel[0:D, :] = jnp.concatenate(near, axis=0)[:, :D].astype(bf16)
        q = qb[:, here]
        seen = dot(rel[...], q)
        rhs[0:D, :] = q
        yield True
        sides = jnp.concatenate([skew_rows(seen[0:D], row), skew_columns(seen[D:256], col)], axis=0)
        sides = sides * math.sqrt(D)
        sides_low = sides.astype(bf16)
        rhs[D : D + 48, :] = sides_low
        rhs[D + 48 : D + 96, :] = (sides - sides_low.astype(f32)).astype(bf16)
        scores = dot(a1[...], rhs[...])
        yield True
        weight = jnp.exp2((scores - jnp.max(scores, axis=0, keepdims=True)) * (SCORE_SCALE * LOG2E))
        weight_ref[...] = weight
        low_ref[...] = weight.astype(bf16)
        yield True
        mixed = dot(vb[...], low_ref[...])
        inv_sum = 1.0 / mixed[D : D + 1]
        scale_ref[0:1, :] = inv_sum
        mixed = mixed[0:D] * inv_sum
        mixed_ref[...] = mixed
        oaug[0:D, :] = (mixed + q.astype(f32)).astype(bf16)
        middle = x_ref[:, here].astype(f32) + dot(wp[...], oaug[...])
        yield True
        center = middle - jnp.sum(middle, axis=0, keepdims=True) * (1.0 / D)
        inv = lax.rsqrt(jnp.sum(center * center, axis=0, keepdims=True) * (1.0 / D) + norm_eps)
        half = center * (inv * math.sqrt(0.5))
        half_ref[...] = half
        scale_ref[1:2, :] = inv
        n2aug[0:D, :] = half.astype(bf16)
        z = dot(w1[...], n2aug[...])
        yield True
        below = lax.erf(z) * (0.5 * math.sqrt(math.pi)) + 0.5 * math.sqrt(math.pi)
        aaug[0:HID, :] = (z * below).astype(bf16)
        slope_ref[...] = below + z * jnp.exp2((z * z) * -LOG2E)
        yield True
        mlp = dot(w2[...], aaug[...])
        out_ref[:, here] = ((middle + mlp * math.sqrt(2.0 / math.pi)) * token_mask(i, tile)).astype(bf16)

    def behind(i, slot):
        weight_ref, low_ref, mixed_ref, half_ref, slope_ref, aaug, n2aug, oaug, scale_ref = slot
        tile = TILE_TWO
        here = plain(i, tile)
        row, col = idx_ref[0:1, inner(i, tile)] - i * TILE_ROWS, idx_ref[1:2, inner(i, tile)]
        near = [relh[pl.ds(40 * k + ROW_STEPS * i, 24), :] for k in range(4)]
        relt[:, 0:D] = jnp.transpose(jnp.concatenate(near, axis=0))[:D, :].astype(bf16)
        inv_sum, inv = scale_ref[0:1, :], scale_ref[1:2, :]
        gy = gy_ref[:, here].astype(f32) * token_mask(i, tile)
        gy_low = gy.astype(bf16)
        pushed = dot(w2t[...], gy_low)
        yield True
        gh_low = (slope_ref[...] * pushed).astype(bf16)
        dw2[:, 0:KK] += dot_nt(gy_low, aaug[...])
        gn = dot(w1t[...], gh_low)
        yield True
        dw1[0:112, :] += dot_nt(n2aug[...], gh_low)
        half = half_ref[...]
        mean = jnp.sum(gn, axis=0, keepdims=True) * (1.0 / D)
        along = jnp.sum(gn * half, axis=0, keepdims=True) * (2.0 / D)
        gmid = gy + (gn - mean - half * along) * (inv * math.sqrt(1.0 / math.pi))
        gm_low = gmid.astype(bf16)
        gm[:, here] = gm_low
        go = dot(wpt[...], gm_low)
        yield True
        dpr[:, 0:112] += dot_nt(gm_low, oaug[...])
        go_low = (go * inv_sum).astype(bf16)
        goaug[0:D, :] = go_low
        goaug[D:, :] = two_rows(jnp.sum(go_low.astype(f32) * mixed_ref[...], axis=0, keepdims=True))
        spread = dot(vbt[...], goaug[...])
        yield True
        gv[0:D, 0:KK] += dot_nt(go_low, low_ref[...])
        gse[0:KK, :] = (weight_ref[...] * spread).astype(bf16)
        back = dot(a2[...], gse[0:KK, :])
        yield True
        gse[KK : KK + D, :] = unskew_rows(back[D : D + 24], row).astype(bf16)
        gse[KK + D : KK + 256, :] = unskew_columns(back[D + 24 : D + 48], col).astype(bf16)
        yield True
        outer = dot_nt(qb[:, here], gse[...])
        gkr[0:D, 0 : KK + 256] += outer
        hacc[i] = outer[:, 384:512]
        gq[:, inner(i, tile)] = go + SCORE_SCALE * back[0:D] + dot(relt[...], gse[KK : KK + 256, :])

    one, two = slots
    gy_copy.wait()

    def attend(k, carry):
        interleave(ahead(2 * k + 1, two), behind(2 * k, one))
        interleave(ahead(2 * k + 2, one), behind(2 * k + 1, two))
        return carry

    interleave(ahead(0, one))
    lax.fori_loop(0, (TILES - 1) // 2, attend, 0)
    if TILES % 2 == 0:
        interleave(ahead(TILES - 1, two), behind(TILES - 2, one))
        interleave(behind(TILES - 1, two))
    else:
        interleave(behind(TILES - 1, one))

    out_copy = pltpu.make_async_copy(out_ref, out_hbm, copy_sem.at[2])
    out_copy.start()
    mid_copy = pltpu.make_async_copy(gm, mid_hbm, copy_sem.at[3])
    mid_copy.start()

    gkt[...] = jnp.transpose(gkr[:, 0:512])[0:KK, :] * SCORE_SCALE
    gvt[...] = jnp.transpose(gv[...])[0:KK, :]

    def pool_gradient(name, columns):
        low = columns.astype(bf16)
        for i in range(9):
            spread = dot_nt(low, tsel_ref[i]) * zsel_ref[i].astype(f32)
            gr[ROW[name] + i : ROW[name] + i + 1, 0:D] = jnp.sum(spread, axis=0, keepdims=True)

    for field, kernel_rows, pooled, gspread, name in ((fk, kk, gkt, gfk, "pool_k"), (fv, kv, gvt, gfv, "pool_v")):
        taps = tap_rows(kernel_rows)
        sums = [jnp.zeros((KG, 128), f32) for _ in range(9)]
        for a in range(KG):
            grad = pooled[KG * a : KG * a + KG, :]
            inside = jnp.where(b_index == 0, 0.0, grad)
            for k in range(9):
                where = pl.ds(tap_start(a, k // 3, k % 3), KG, stride=KSTR)
                sums[k] = sums[k] + (inside if k % 3 == 0 else grad) * field[where, :]
            spread_keys(taps, grad, a, gspread)
            if a == KG - 1:
                gspread[LEAD + TOK - GRID : LEAD + TOK, :] = jnp.zeros((GRID, 128), f32)
        rows = [jnp.sum(total, axis=0, keepdims=True) for total in sums]
        rows = jnp.concatenate(rows + [jnp.zeros((128 - 9, 128), f32)], axis=0)
        pool_gradient(name, jnp.transpose(rows)[:D, :])

    def finish(i, carry):
        tile = TILE_THREE
        wide = tile + 2 * HALO
        here = plain(i, tile)
        mid = slice(HALO, HALO + tile)
        mask = token_mask(i, tile)
        col = jnp.broadcast_to(idx_ref[1:2, inner(i, tile)], (8, tile))
        first, last = col == 0, col == GRID - 1
        for pair in range(D // 16):
            fields, moved = [], []
            for half in range(2):
                ch = slice(16 * pair + 8 * half, 16 * pair + 8 * half + 8)
                grad = gq[ch, window(i, tile)]
                below, above = pltpu.roll(grad, wide - GRID, 1), pltpu.roll(grad, GRID, 1)

                def col_sum(v):
                    return tap(v, ch, wide) * below + tap(v + 3, ch, wide) * grad + tap(v + 6, ch, wide) * above

                after = jnp.where(last, 0.0, pltpu.roll(col_sum(0), wide - 1, 1)[:, mid])
                before = jnp.where(first, 0.0, pltpu.roll(col_sum(2), 1, 1)[:, mid])
                fields.append((after + col_sum(1)[:, mid] + before) * mask)
                moved.append((below[:, mid], grad[:, mid], above[:, mid]))
            gfield[16 * pair : 16 * pair + 16, here] = jnp.concatenate(fields, axis=0).astype(bf16)
            for u in range(3):
                both = jnp.concatenate([moved[0][u], moved[1][u]], axis=0)
                gsh[u * D + 16 * pair : u * D + 16 * pair + 16, :] = both.astype(bf16)
        kqacc[:, 0 : 3 * D] += dot_nt(gsh[...], fcol[:, here])
        flat = pl.ds(pl.multiple_of(i * tile + LEAD, 8), tile)
        gkv[:, 0:128] = gfk[flat, :].astype(bf16)
        gkv[:, 128:256] = gfv[flat, :].astype(bf16)
        dwq[:, 0:112] += dot_nt(gfield[:, here], un[:, here])
        dwkv[0:112, :] += dot(un[:, here], gkv[...])
        field_copy(i).start()
        return carry

    def field_copy(i):
        here = plain(i, TILE_THREE)
        return pltpu.make_async_copy(gfield.at[:, here], field_hbm.at[:, here], copy_sem.at[5 + i])

    lax.fori_loop(0, TOK // TILE_THREE, finish, 0)
    out_copy.wait()
    mid_copy.wait()
    unit_copy.wait()

    def write(name, rows, first=0):
        base = ROW[name] + first
        gr[base : base + rows.shape[0], 0:D] = rows

    def wide_rows(rows):
        return jnp.concatenate([rows, jnp.zeros((rows.shape[0], 128 - D), f32)], axis=1)

    def through_norm(name, first, outer, bias, gain_row, shift_row):
        raw = piece(name, outer.shape[0], first)[:, :D]
        write(name, outer * gain_row[:, :D] + bias * shift_row[:, :D], first)
        return jnp.sum(raw * outer, axis=0, keepdims=True), jnp.sum(raw * bias, axis=0, keepdims=True)

    gain, shift = through_norm("w_qkv", 0, dwq[:, 0:D], dwq[:, D : D + 1], g1_row, b1_row)
    write("b_qkv", jnp.transpose(dwq[...])[D : D + 1, :])
    for k in (1, 2):
        turned = jnp.transpose(dwkv[:, 128 * k - 128 : 128 * k])[0:D, :]
        more_gain, more_shift = through_norm("w_qkv", k * D, turned[:, 0:D], turned[:, D : D + 1], g1_row, b1_row)
        gain, shift = gain + more_gain, shift + more_shift
        write("b_qkv", dwkv[D : D + 1, 128 * k - 128 : 128 * k - 128 + D], k)
    write("ln1_g", gain)
    write("ln1_b", shift)

    lane = lax.broadcasted_iota(jnp.int32, (D, 128), 1)
    wide_lane = lax.broadcasted_iota(jnp.int32, (D, 3 * 128), 1) - lax.broadcasted_iota(jnp.int32, (D, 3 * 128), 0)
    columns = jnp.zeros((D, 128), f32)
    for k in range(9):
        u, v = k // 3, k % 3
        one = jnp.where(wide_lane == v * D, kqacc[u * D : u * D + D, :], 0.0)
        columns = jnp.where(lane == k, jnp.sum(one, axis=1, keepdims=True), columns)
    pool_gradient("pool_q", columns)

    for i in range(TILES):
        turned = jnp.transpose(hacc[i])
        for k in range(4):
            count = KG + ROW_STEPS - 1
            where = pl.ds(ROW["rel_h"] + 3 + k + TILE_ROWS * i, count, stride=4)
            gr[where, :] = gr[where, :] + wide_rows(turned[16 + 24 * k : 16 + 24 * k + count])
    turned = jnp.transpose(gkr[0:D, 384:768])
    for k in range(4):
        gr[pl.ds(ROW["rel_w"] + 3 + k, 39, stride=4), :] = wide_rows(turned[112 + 40 * k : 151 + 40 * k])

    write("w_proj", dpr[:, 0:D])
    write("b_proj", jnp.transpose(dpr[...])[D : D + 1, :])
    turned = jnp.transpose(dw1[...])
    gain, shift = through_norm(
        "w_fc1", 0, turned[:, 0:D] * math.sqrt(2.0 / math.pi), turned[:, D : D + 1] * math.sqrt(1.0 / math.pi), g2_row, b2_row
    )
    write("ln2_g", gain)
    write("ln2_b", shift)
    for k in range(4):
        write("b_fc1", dw1[D : D + 1, k * D : (k + 1) * D] * math.sqrt(1.0 / math.pi), k)
        gr[pl.ds(ROW["w_fc2"] + k, D, stride=4), :] = wide_rows(dw2[:, k * D : (k + 1) * D] * math.sqrt(2.0 / math.pi))
    write("b_fc2", jnp.transpose(dw2[:, HID:512])[0:1, :])
    for i in range(TOK // TILE_THREE):
        field_copy(i).wait()
    for w, start in enumerate(starts):
        gchunk_ref[w] = gr[start : start + rows_of, 0:D].astype(bf16)


def image_step(shard_len, chunks, pixels, image_side, cotangent):
    starts = tuple((shard_len * w) // D for w in range(chunks.shape[0]))
    rows_of = block_rows(shard_len)
    groups = -(-(shard_len * len(starts)) // (4 * D))
    depth = max(8 * (-(-(starts[-1] + rows_of) // 8)), 4 * groups)
    flat_rows = max(3 * groups, (shard_len * (len(starts) - 1)) // 128 + chunks.shape[1] + 1)
    flat_rows = 8 * (-(-flat_rows // 8))
    zsel, tsel = pool_selectors()
    vm = pltpu.VMEM
    scratch = [
        vm((depth, 128), f32),
        vm((D, 112), bf16), vm((112, 128), bf16), vm((112, 128), bf16),
        vm((D, 112), bf16), vm((D, D), bf16),
        vm((HID, 112), bf16), vm((D, HID), bf16), vm((D, KK), bf16), vm((HID, D), bf16),
        vm((168, 128), f32), vm((256, D), bf16), vm((D, 256), bf16),
        vm((D, 128), f32), vm((9, D, 128), f32),
        vm((D, TOK + 2 * HALO), f32), vm((FIELD, 128), f32), vm((FIELD, 128), f32),
        vm((D, TOK), bf16), vm((D, TOK), bf16),
        vm((112, TOK), bf16), vm((3 * D, TOK), bf16),
        vm((KK, 208), bf16), vm((144, KK), bf16), vm((112, KK), bf16), vm((KK, 112), bf16),
        vm((KK, 128), f32), vm((KK, 128), f32),
        vm((208, TILE_TWO), bf16), vm((KK + 256, TILE_TWO), bf16), vm((112, TILE_PROJECT), bf16), vm((112, TILE_TWO), bf16),
        vm((3 * D, TILE_THREE), bf16), vm((TILE_THREE, 256), bf16),
        vm((D, 512), f32), vm((128, HID), f32), vm((D, 128), f32), vm((128, 512), f32), vm((128, 768), f32),
        vm((TILES, D, 128), f32),
        vm((D, 128), f32), vm((128, 256), f32), vm((3 * D, 3 * 128), f32),
        vm((depth, 128), f32),
        vm((D, TOK), bf16), vm((D, TOK), bf16), vm((D, TOK), bf16), vm((D, TOK), bf16),
        pltpu.SemaphoreType.DMA((5 + TOK // TILE_THREE,)),
        vm((flat_rows, 128), f32),
        vm(zsel.shape, bf16), vm(tsel.shape, bf16), vm((8, TOK + 2 * HALO), jnp.int32), pltpu.SemaphoreType.DMA((3,)),
    ]
    slot = [
        vm((KK, TILE_TWO), f32), vm((KK, TILE_TWO), bf16), vm((D, TILE_TWO), f32), vm((D, TILE_TWO), f32), vm((HID, TILE_TWO), f32),
        vm((KK, TILE_TWO), bf16), vm((112, TILE_TWO), bf16), vm((112, TILE_TWO), bf16), vm((8, TILE_TWO), f32),
    ]
    whole = pl.BlockSpec(memory_space=pltpu.VMEM)
    far = pl.BlockSpec(memory_space=pl.ANY)
    shape = jax.ShapeDtypeStruct
    out, grad_chunks, *rest = pl.pallas_call(
        functools.partial(image_kernel, shard_len, starts, rows_of),
        out_shape=(
            shape((D, TOK), bf16), shape((len(starts), rows_of, D), bf16),
            shape((D, TOK), bf16), shape((D, TOK), bf16), shape((D, TOK), bf16), shape((8, TOK), f32),
            shape((KK, 128), f32), shape((KK, 128), f32), shape((16, 128), f32), shape((16, 128), f32),
            shape((D, D), bf16), shape((D, 256), bf16),
        ),
        in_specs=[pl.BlockSpec(memory_space=pltpu.SMEM), whole, far, far, far, far, far],
        out_specs=(far, whole, far, far, far) + (whole,) * 7,
        scratch_shapes=scratch + slot + slot,
        compiler_params=pltpu.CompilerParams(vmem_limit_bytes=54 * 1024 * 1024),
        name="image_step",
    )(image_side, chunks, pixels, cotangent, lane_index(), zsel, tsel)
    return out, grad_chunks, rest


def input_step(rest):
    far = pl.BlockSpec(memory_space=pl.ANY)
    vm = pltpu.VMEM
    scratch = [vm(part.shape, part.dtype) for part in rest]
    scratch += [vm((D, TOK), bf16), vm((FIELD, 128), f32), vm((FIELD, 128), f32), vm((TILE_THREE, 256), bf16)]
    return pl.pallas_call(
        input_kernel,
        out_shape=jax.ShapeDtypeStruct((D, TOK), bf16),
        in_specs=[far] * len(rest),
        out_specs=far,
        scratch_shapes=scratch + [pltpu.SemaphoreType.DMA((10 + TOK // TILE_THREE,))],
        compiler_params=pltpu.CompilerParams(vmem_limit_bytes=60 * 1024 * 1024),
        cost_estimate=pl.CostEstimate(flops=2 * D * 3 * D * TOK, bytes_accessed=16 * 1024 * 1024, transcendentals=0),
        name="input_step",
    )(*rest)


def adam_update(gradient, master_part, first_part, second_part, average_part, step_rates):
    moment_one = beta_first * first_part + (1.0 - beta_first) * gradient
    moment_two = beta_second * second_part + (1.0 - beta_second) * gradient * gradient
    fix_one = 1.0 - beta_first**STEP
    fix_two = 1.0 - beta_second**STEP
    direction = moment_one / fix_one / (jnp.sqrt(moment_two / fix_two) + adam_eps)
    updated = master_part - step_rates * (direction + weight_decay * master_part)
    blended = average_decay * average_part + (1.0 - average_decay) * updated
    return (updated, moment_one, moment_two, blended)


def shards(tokens, image_sides, grad_out, master, first_moment, second_moment, weight_average):
    shard_len = master.shape[0]
    owners = lax.axis_size("wide")
    images_all = tokens.shape[0] * owners * lax.axis_size("narrow")
    rows_of = block_rows(shard_len)
    inset = lax.rem(lax.axis_index("wide") * shard_len, D)

    filled = 1024 * (-(-shard_len // 1024))
    own = jnp.pad(master, (0, filled - shard_len)).reshape(1, filled // 128, 128).astype(bf16)
    chunks = lax.all_to_all(jnp.broadcast_to(own, (owners, filled // 128, 128)), "wide", 0, 0)

    outs, grads_in, grad_chunks = [], [], None
    for k in range(tokens.shape[0]):
        out, chunk, rest = image_step(shard_len, chunks, tokens[k], image_sides[k : k + 1], grad_out[k])
        outs.append(out)
        grads_in.append(input_step(rest))
        grad_chunks = chunk if k == 0 else (grad_chunks.astype(f32) + chunk.astype(f32)).astype(bf16)
    block_out = jnp.stack(outs)
    grad_in = jnp.stack(grads_in)

    parts = lax.all_to_all(grad_chunks, "wide", 0, 0)
    step_rates = lax.dynamic_slice_in_dim(
        jnp.asarray(rate_values(shard_len * owners)), lax.axis_index("wide") * shard_len, shard_len
    )
    parts, grad_in, step_rates = lax.optimization_barrier((parts, grad_in, step_rates))
    total = jnp.sum(parts.astype(f32), axis=0)
    total = total + lax.ppermute(total, "narrow", [(0, 1), (1, 0)])
    reduced = lax.dynamic_slice(total.reshape(rows_of * D), (inset,), (shard_len,))
    updated, moment_one, moment_two, blended = adam_update(
        reduced / images_all, master, first_moment, second_moment, weight_average, step_rates
    )
    return (block_out, grad_in, updated, moment_one, moment_two, blended)


def solution(mesh):
    return jax.shard_map(
        shards,
        mesh=mesh,
        in_specs=(
            P(("wide", "narrow"), None, None),
            P(("wide", "narrow")),
            P(("wide", "narrow"), None, None),
            P("wide"),
            P("wide"),
            P("wide"),
            P("wide"),
        ),
        out_specs=(
            P(("wide", "narrow"), None, None),
            P(("wide", "narrow"), None, None),
            P("wide"),
            P("wide"),
            P("wide"),
            P("wide"),
        ),
        check_vma=False,
    )
```

```python
import functools
import math

import jax
import jax.numpy as jnp
import numpy as np
from jax import lax
from jax.experimental import pallas as pl
from jax.experimental.pallas import tpu as pltpu
from jax.sharding import PartitionSpec as P

D = 96
HID = 384
KSTR = 4
KG = 20
STEP = 5
GRID = 80
TOK = 6400
KK = 400
REL = 159

norm_eps = 1e-06
beta_first = 0.5
beta_second = 0.5
adam_eps = 1e-08
weight_decay = 0.05
rate_factor = 0.4
average_decay = 0.8

f32 = jnp.float32
bf16 = jnp.bfloat16

HALO = 128
LEAD = 88
FIELD = LEAD + TOK + 8
TILE_PROJECT = 6400
TILE_ONE = 6400
TILE_TWO = 1280
TILE_THREE = 1280
TILES = TOK // TILE_TWO
TILE_ROWS = TILE_TWO // GRID
ROW_STEPS = TILE_ROWS // KSTR
SCORE_SCALE = D ** (-0.5)
LOG2E = 1.4426950408889634


def segment_list():
    return [
        ("w_qkv", (3 * D, D), D ** (-0.5)),
        ("b_qkv", (3 * D,), 0.2),
        ("pool_q", (D, 9), 1.0 / 3.0),
        ("pool_k", (D, 9), 1.0 / 3.0),
        ("pool_v", (D, 9), 1.0 / 3.0),
        ("rel_h", (REL, D), 0.5 * D ** (-0.5)),
        ("rel_w", (REL, D), 0.5 * D ** (-0.5)),
        ("w_proj", (D, D), D ** (-0.5)),
        ("b_proj", (D,), 0.2),
        ("w_fc1", (HID, D), D ** (-0.5)),
        ("b_fc1", (HID,), 0.2),
        ("w_fc2", (D, HID), HID ** (-0.5)),
        ("b_fc2", (D,), 0.2),
        ("ln1_g", (D,), 0.5),
        ("ln1_b", (D,), 0.2),
        ("ln2_g", (D,), 0.5),
        ("ln2_b", (D,), 0.2),
    ]


def row_bases():
    bases = {}
    offset = 0
    for name, shape, _ in segment_list():
        assert offset % D == 0
        bases[name] = offset // D
        offset += math.prod(shape)
    return bases


ROW = row_bases()


def rate_values(full_len):
    rates = np.full((full_len,), rate_factor * D ** (-0.5), np.float32)
    offset = 0
    for _, shape, spread in segment_list():
        length = math.prod(shape)
        rates[offset : offset + length] = rate_factor * spread
        offset += length
    return rates


def block_rows(shard_len):
    return 16 * (-(-(-(-(shard_len + D - 1) // D)) // 16))


def pool_selectors():
    flat = np.arange(9 * D).reshape(9, D)
    channel = (flat[:, None, :] // 9 == np.arange(D)[None, :, None]).astype(np.float32)
    tap = (flat[:, :, None] % 9 == np.arange(128)[None, None, :]).astype(np.float32)
    return jnp.asarray(channel, bf16), jnp.asarray(tap, bf16)


def lane_index():
    place = np.arange(-HALO, TOK + HALO)
    table = np.zeros((8, TOK + 2 * HALO), np.int32)
    table[0] = place // GRID
    table[1] = place % GRID
    return jnp.asarray(table)


def dot(a, b):
    return lax.dot_general(a, b, (((1,), (0,)), ((), ())), preferred_element_type=f32)


def dot_nt(a, b):
    return lax.dot_general(a, b, (((1,), (1,)), ((), ())), preferred_element_type=f32)


def dot_tn(a, b):
    return lax.dot_general(a, b, (((0,), (0,)), ((), ())), preferred_element_type=f32)


def normalize(values):
    mean = jnp.sum(values, axis=0, keepdims=True) * (1.0 / D)
    center = values - mean
    spread = jnp.sum(center * center, axis=0, keepdims=True) * (1.0 / D)
    inv = lax.rsqrt(spread + norm_eps)
    return center * inv, inv


def skew_rows(rows, place):
    width = rows.shape[1]
    where = jnp.broadcast_to(place, (24, width))
    residue = where & 3
    x = jnp.where(
        residue < 2,
        jnp.where(residue == 0, rows[0:24], rows[24:48]),
        jnp.where(residue == 2, rows[48:72], rows[72:96]),
    )
    step = ROW_STEPS // 2
    while step >= 1:
        x = jnp.where((where & (4 * step)) != 0, pltpu.roll(x, 24 - step, 0), x)
        step //= 2
    return x


def skew_columns(rows, place):
    width = rows.shape[1]
    where = jnp.broadcast_to(place, (40, width))
    residue = where & 3
    x = jnp.where(
        residue < 2,
        jnp.where(residue == 0, rows[0:40], rows[40:80]),
        jnp.where(residue == 2, rows[80:120], rows[120:160]),
    )
    x = jnp.concatenate([jnp.where((where[0:24] & 64) != 0, x[16:40], x[0:24]), x[24:40]], axis=0)
    x = jnp.where((where[0:32] & 32) != 0, x[8:40], x[0:32])
    where = where[0:24]
    x = jnp.where((where & 16) != 0, pltpu.roll(x, 28, 0)[0:24], x[0:24])
    x = jnp.where((where & 8) != 0, pltpu.roll(x, 22, 0), x)
    return jnp.where((where & 4) != 0, pltpu.roll(x, 23, 0), x)


def unskew_rows(x, place):
    where = jnp.broadcast_to(place, x.shape)
    step = 1
    while step < ROW_STEPS:
        x = jnp.where((where & (4 * step)) != 0, pltpu.roll(x, step, 0), x)
        step *= 2
    residue = where & 3
    return jnp.concatenate([jnp.where(residue == k, x, 0.0) for k in range(4)], axis=0)


def unskew_columns(x, place):
    width = x.shape[1]
    zero = jnp.zeros((8, width), f32)
    where = jnp.broadcast_to(place, (40, width))
    x = jnp.where((where[0:24] & 4) != 0, pltpu.roll(x, 1, 0), x)
    x = jnp.where((where[0:24] & 8) != 0, pltpu.roll(x, 2, 0), x)
    x = jnp.concatenate([x, zero], axis=0)
    x = jnp.where((where[0:32] & 16) != 0, pltpu.roll(x, 4, 0), x)
    x = jnp.where((where & 32) != 0, jnp.concatenate([zero, x], axis=0), jnp.concatenate([x, zero], axis=0))
    far = (where & 64) != 0
    x = jnp.concatenate([jnp.where(far[0:16], 0.0, x[0:16]), jnp.where(far[16:40], x[0:24], x[16:40])], axis=0)
    residue = where & 3
    return jnp.concatenate([jnp.where(residue == k, x, 0.0) for k in range(4)], axis=0)


def group_row(pair, shift):
    return D * (pair // 2) + 32 * shift + 16 * (pair % 2)


def aligned(value, step):
    return value if isinstance(value, int) else pl.multiple_of(value, step)


def interleave(*parts):
    live = list(parts)
    while live:
        for part in list(live):
            if next(part, None) is None:
                live.remove(part)


def two_columns(column):
    high = column.astype(bf16).astype(f32)
    place = lax.broadcasted_iota(jnp.int32, (column.shape[0], 16), 1)
    return jnp.where(place == 0, high, jnp.where(place == 1, column - high, 0.0)).astype(bf16)


def two_rows(row):
    high = row.astype(bf16).astype(f32)
    place = lax.broadcasted_iota(jnp.int32, (16, row.shape[1]), 0)
    return jnp.where(place == 0, high, jnp.where(place == 1, row - high, 0.0)).astype(bf16)


def two_ones(width):
    return jnp.where(lax.broadcasted_iota(jnp.int32, (16, width), 0) < 2, 1.0, 0.0).astype(bf16)


def key_columns():
    return lax.broadcasted_iota(jnp.int32, (KG, 128), 0)


def tap_start(a, u, v):
    return LEAD + GRID * (KSTR * a + u - 1) + v - 1


def tap_rows(kernel_rows):
    b_index = key_columns()
    taps = [jnp.broadcast_to(kernel_rows[k : k + 1, :], (KG, 128)) for k in range(9)]
    return [jnp.where(b_index == 0, 0.0, tap) if k % 3 == 0 else tap for k, tap in enumerate(taps)]


def spread_keys(taps, grad, a, gfield):
    idle = LEAD + GRID * (KSTR * a + 2)
    gfield[pl.ds(aligned(idle - 8, 8), GRID + 8), :] = jnp.zeros((GRID + 8, 128), f32)
    for u in range(3):
        gfield[pl.ds(tap_start(a, u, 3), KG, stride=KSTR), :] = jnp.zeros((KG, 128), f32)
    for k in range(9):
        gfield[pl.ds(tap_start(a, k // 3, k % 3), KG, stride=KSTR), :] = taps[k] * grad


def input_kernel(*refs):
    sources, gin_hbm, held = refs[:10], refs[10], refs[11:21]
    field_ref, mid_ref, unit_ref, inv_ref, gkt, gvt, kk, kv, wqt, wkvg = held
    gin_ref, gfk, gfv, gkv, copy_sem = refs[21:]
    copies = [pltpu.make_async_copy(a, b, copy_sem.at[k]) for k, (a, b) in enumerate(zip(sources, held))]
    for copy in copies[::-1]:
        copy.start()
    for copy in copies[4:]:
        copy.wait()
    for kernel_rows, pooled, gfield in ((kk, gkt, gfk), (kv, gvt, gfv)):
        taps = tap_rows(kernel_rows)

        def spread(a, carry):
            spread_keys(taps, pooled[pl.ds(KG * a, KG), :], a, gfield)
            return carry

        lax.fori_loop(0, KG, spread, 0)
        gfield[LEAD + TOK - GRID : LEAD + TOK, :] = jnp.zeros((GRID, 128), f32)
    for copy in copies[:4]:
        copy.wait()

    def gin_copy(i):
        here = pl.ds(aligned(i * TILE_THREE, 128), TILE_THREE)
        return pltpu.make_async_copy(gin_ref.at[:, here], gin_hbm.at[:, here], copy_sem.at[10 + i])

    def finish(i, carry):
        tile = TILE_THREE
        here = pl.ds(aligned(i * tile, 128), tile)
        flat = pl.ds(aligned(i * tile + LEAD, 8), tile)
        gkv[:, 0:128] = gfk[flat, :].astype(bf16)
        gkv[:, 128:256] = gfv[flat, :].astype(bf16)
        gn = dot(wqt[...], field_ref[:, here]) + dot_nt(wkvg[...], gkv[...])
        unit = unit_ref[:, here].astype(f32)
        mean = jnp.sum(gn, axis=0, keepdims=True) * (1.0 / D)
        along = jnp.sum(gn * unit, axis=0, keepdims=True) * (1.0 / D)
        total = mid_ref[:, here].astype(f32) + (gn - mean - unit * along) * inv_ref[0:1, here]
        gin_ref[:, here] = total.astype(bf16)
        gin_copy(i).start()
        return carry

    lax.fori_loop(0, TOK // TILE_THREE, finish, 0)
    for i in range(TOK // TILE_THREE):
        gin_copy(i).wait()


def image_kernel(
    shard_len,
    starts,
    rows_of,
    side_ref,
    chunk_ref,
    x_hbm,
    gy_hbm,
    idx_hbm,
    zsel_hbm,
    tsel_hbm,
    out_hbm,
    gchunk_ref,
    field_hbm,
    mid_hbm,
    unit_hbm,
    inv_ref,
    gkt,
    gvt,
    kk,
    kv,
    wqt,
    wkvg,
    wf, wq, wkt, wvt, wp, wpt, w1, w1t, w2, w2t, relh, rel, relt, cols, kq,
    fq, fk, fv, qb, gm, un, fcol,
    a1, a2, vb, vbt, kp, vpool,
    rhs, gse, n1aug, goaug, gsh, gkv,
    dw2, dw1, dpr, gv, gkr, hacc, dwq, dwkv, kqacc, gr, x_ref, gy_ref, out_ref, gfield, copy_sem, flat, zsel_ref, tsel_ref, idx_ref, table_sem,
    *slot_refs,
):
    gq, gfk, gfv = fq, fk, fv
    slots = (slot_refs[: len(slot_refs) // 2], slot_refs[len(slot_refs) // 2 :])
    side = side_ref[0]
    table_copies = [
        pltpu.make_async_copy(source, target, table_sem.at[k])
        for k, (source, target) in enumerate(((zsel_hbm, zsel_ref), (tsel_hbm, tsel_ref), (idx_hbm, idx_ref)))
    ]
    for copy in table_copies:
        copy.start()
    x_copy = pltpu.make_async_copy(x_hbm, x_ref, copy_sem.at[0])
    gy_copy = pltpu.make_async_copy(gy_hbm, gy_ref, copy_sem.at[1])
    x_copy.start()
    gy_copy.start()

    flat[...] = jnp.zeros(flat.shape, f32)
    lane_of = lax.broadcasted_iota(jnp.int32, chunk_ref.shape[1:], 1)
    for w in range(len(starts)):
        base, inset = (shard_len * w) // 128, (shard_len * w) % 128
        part = chunk_ref[w].astype(f32)
        if inset:
            part = pltpu.roll(part, inset, 1)
            flat[base + 1 : base + 1 + part.shape[0], :] += jnp.where(lane_of < inset, part, 0.0)
            part = jnp.where(lane_of < inset, 0.0, part)
        flat[base : base + part.shape[0], :] += part
    groups = -(-(shard_len * len(starts)) // (4 * D))
    lane_of = lax.broadcasted_iota(jnp.int32, (groups, 128), 1)
    first, second, third = (flat[pl.ds(k, groups, stride=3), :] for k in range(3))
    wf[pl.ds(0, groups, stride=4), :] = first
    wf[pl.ds(1, groups, stride=4), :] = pltpu.roll(jnp.where(lane_of >= 96, first, second), 32, 1)
    wf[pl.ds(2, groups, stride=4), :] = pltpu.roll(jnp.where(lane_of >= 64, second, third), 64, 1)
    wf[pl.ds(3, groups, stride=4), :] = pltpu.roll(third, 96, 1)

    def piece(name, count, first=0):
        base = ROW[name] + first
        return wf[base : base + count, :]

    vec_rows = [ROW["b_qkv"], ROW["b_proj"], ROW["b_fc2"], ROW["ln1_g"], ROW["ln1_b"], ROW["ln2_g"], ROW["ln2_b"]]
    vec_rows += [ROW["b_fc1"] + k for k in range(4)]
    stacked = jnp.concatenate([wf[r : r + 1, :] for r in vec_rows] + [jnp.zeros((128 - len(vec_rows), 128), f32)], axis=0)
    cols[...] = jnp.transpose(stacked)[:D, :]
    cols_low = cols[...].astype(bf16)
    g1_row, b1_row = piece("ln1_g", 1), piece("ln1_b", 1)
    g2_row, b2_row = piece("ln2_g", 1), piece("ln2_b", 1)

    def through(name, count, first, column):
        return dot(piece(name, count, first)[:, :D].astype(bf16), cols_low)[:, column : column + 1]

    wq_gain = piece("w_qkv", D) * g1_row
    wq[:, 0:D] = piece("w_qkv", D)[:, :D].astype(bf16)
    wq[:, D:] = two_columns(cols[:, 0:1])
    wqt[...] = jnp.transpose(wq_gain)[:D, :].astype(bf16)
    for k, ref in ((1, wkt), (2, wvt)):
        ref[...] = jnp.zeros(ref.shape, bf16)
        ref[0:D, 0:D] = jnp.transpose(piece("w_qkv", D, k * D))[:D, :].astype(bf16)
        ref[D:, 0:D] = two_rows(piece("b_qkv", 1, k)[:, :D])
        wkvg[:, 128 * k - 128 : 128 * k] = jnp.zeros((D, 128), bf16)
        wkvg[:, 128 * k - 128 : 128 * k - 128 + D] = jnp.transpose(piece("w_qkv", D, k * D) * g1_row)[:D, :].astype(bf16)
    wp[:, 0:D] = piece("w_proj", D)[:, :D].astype(bf16)
    wp[:, D:] = two_columns(cols[:, 1:2])
    wpt[...] = jnp.transpose(piece("w_proj", D))[:D, :].astype(bf16)
    w1_gain = piece("w_fc1", HID) * g2_row
    b_fc1 = jnp.concatenate([cols[:, 7 + k : 8 + k] for k in range(4)], axis=0)
    w1[:, 0:D] = w1_gain[:, :D].astype(bf16)
    w1[:, D:] = two_columns((b_fc1 + through("w_fc1", HID, 0, 6)) * math.sqrt(0.5))
    w1t[...] = jnp.transpose(w1_gain)[:D, :].astype(bf16)
    for k in range(4):
        block = wf[pl.ds(ROW["w_fc2"] + k, D, stride=4), :]
        w2t[k * D : (k + 1) * D, :] = jnp.transpose(block)[:D, :].astype(bf16)
    w2[:, 0:HID] = jnp.transpose(w2t[...].astype(f32)).astype(bf16)
    w2[:, HID:] = two_columns(cols[:, 2:3] * math.sqrt(0.5 * math.pi))
    relh[160:, :] = jnp.zeros((8, 128), f32)
    for k in range(4):
        relh[k * 40 : k * 40 + 40, :] = wf[pl.ds(ROW["rel_h"] + 3 + k, 40, stride=4), :]
    rel_w = jnp.concatenate([wf[pl.ds(ROW["rel_w"] + 3 + k, 40, stride=4), :] for k in range(4)], axis=0)
    rel[D:256, :] = rel_w[:, :D].astype(bf16)
    relt[:, D:256] = jnp.transpose(rel_w)[:D, :].astype(bf16)

    def pool_columns(name):
        total = jnp.zeros((D, 128), f32)
        for i in range(9):
            row = wf[ROW[name] + i : ROW[name] + i + 1, :][:, :D]
            total = total + dot((zsel_ref[i].astype(f32) * row).astype(bf16), tsel_ref[i])
        return total

    def pool_rows(name):
        full = jnp.concatenate([pool_columns(name), jnp.zeros((32, 128), f32)], axis=0)
        return jnp.transpose(full)[0:16, :]

    for copy in table_copies:
        copy.wait()
    pooled_kernel = pool_columns("pool_q")
    for k in range(9):
        kq[k] = jnp.broadcast_to(pooled_kernel[:, k : k + 1], (D, 128))

    def tap(k, ch, width):
        return jnp.concatenate([kq[k, ch, :]] * (width // 128), axis=1)

    kk[...] = pool_rows("pool_k")
    kv[...] = pool_rows("pool_v")

    for ref in (fq,):
        ref[:, 0:HALO] = jnp.zeros((D, HALO), f32)
        ref[:, HALO + TOK :] = jnp.zeros((D, HALO), f32)
    for ref in (fk, fv):
        ref[0:LEAD, :] = jnp.zeros((LEAD, 128), f32)
    for ref in (dw2, dw1, dpr, gv, gkr, dwq, dwkv, kqacc):
        ref[...] = jnp.zeros(ref.shape, ref.dtype)
    gr[ROW["rel_h"] : ROW["w_proj"], :] = jnp.zeros((2 * REL, 128), f32)
    tail = ROW["ln2_b"]
    gr[tail:, :] = jnp.zeros((gr.shape[0] - tail, 128), f32)

    un[D:, :] = two_ones(TOK)
    n1aug[D:, :] = two_ones(TILE_PROJECT)
    for slot in slots:
        slot[5][HID:, :] = two_ones(TILE_TWO)
        slot[6][D:, :] = two_ones(TILE_TWO)
        slot[7][D:, :] = two_ones(TILE_TWO)
    rhs[192:208, :] = two_ones(TILE_TWO)

    def window(i, tile):
        return pl.ds(aligned(i * tile, 128), tile + 2 * HALO)

    def inner(i, tile):
        return pl.ds(aligned(i * tile + HALO, 128), tile)

    def plain(i, tile):
        return pl.ds(aligned(i * tile, 128), tile)

    def token_mask(i, tile):
        place = idx_ref[0:2, inner(i, tile)]
        return jnp.where((place[0:1] < side) & (place[1:2] < side), 1.0, 0.0)

    x_copy.wait()

    def project(i, carry):
        here = plain(i, TILE_PROJECT)
        unit, inv = normalize(x_ref[:, here].astype(f32))
        un[0:D, here] = unit.astype(bf16)
        inv_ref[0:1, here] = inv
        n1aug[0:D, :] = (unit * cols[:, 3:4] + cols[:, 4:5]).astype(bf16)
        fq[:, inner(i, TILE_PROJECT)] = dot(wq[...], n1aug[...]) * token_mask(i, TILE_PROJECT)
        field = pl.ds(pl.multiple_of(i * TILE_PROJECT + LEAD, 8), TILE_PROJECT)
        fk[field, :] = dot_tn(n1aug[...], wkt[...])
        fv[field, :] = dot_tn(n1aug[...], wvt[...])
        return carry

    lax.fori_loop(0, TOK // TILE_PROJECT, project, 0)

    unit_copy = pltpu.make_async_copy(un.at[0:D, :], unit_hbm, copy_sem.at[4])
    unit_copy.start()

    def pool_queries(i, carry):
        tile = TILE_ONE
        wide = tile + 2 * HALO
        mid = slice(HALO, HALO + tile)
        col = jnp.broadcast_to(idx_ref[1:2, window(i, tile)], (8, wide))
        first, last = col == 0, col == GRID - 1
        mask = token_mask(i, tile)
        for pair in range(D // 16):
            pooled, moved = [], []
            for half in range(2):
                ch = slice(16 * pair + 8 * half, 16 * pair + 8 * half + 8)
                field = fq[ch, window(i, tile)]
                left = jnp.where(first, 0.0, pltpu.roll(field, 1, 1))
                right = jnp.where(last, 0.0, pltpu.roll(field, wide - 1, 1))

                def row_sum(u):
                    return tap(3 * u, ch, wide) * left + tap(3 * u + 1, ch, wide) * field + tap(3 * u + 2, ch, wide) * right

                total = pltpu.roll(row_sum(0), GRID, 1) + row_sum(1) + pltpu.roll(row_sum(2), wide - GRID, 1)
                pooled.append(total[:, mid] * mask)
                moved.append((left[:, mid], field[:, mid], right[:, mid]))
            qb[16 * pair : 16 * pair + 16, plain(i, tile)] = jnp.concatenate(pooled, axis=0).astype(bf16)
            for v in range(3):
                both = jnp.concatenate([moved[0][v], moved[1][v]], axis=0)
                place = group_row(pair, v)
                fcol[place : place + 16, plain(i, tile)] = both.astype(bf16)
        return carry

    lax.fori_loop(0, TOK // TILE_ONE, pool_queries, 0)

    b_index = key_columns()

    for field, kernel_rows, pooled in ((fk, kk, kp), (fv, kv, vpool)):
        taps = tap_rows(kernel_rows)
        for a in range(KG):
            total = jnp.zeros((KG, 128), f32)
            for k in range(9):
                total = total + taps[k] * field[pl.ds(tap_start(a, k // 3, k % 3), KG, stride=KSTR), :]
            keep = (KSTR * b_index < side) & (KSTR * a < side)
            pooled[KG * a : KG * a + KG, :] = jnp.where(keep, total, 0.0)

    key = lax.broadcasted_iota(jnp.int32, (KK, 112), 0)
    key_a = lax.div(key, KG)
    key_b = key - KG * key_a
    place = lax.broadcasted_iota(jnp.int32, (KK, 112), 1)
    hot = jnp.zeros((KK, 112), f32)
    for base in (0, 48):
        one_a = (place >= base) & (place < base + 24) & (KG - 1 - key_a == place - base)
        one_b = (place >= base + 24) & (place < base + 48) & (KG - 1 - key_b == place - base - 24)
        hot = jnp.where(one_a | one_b, 1.0, hot)
    shut = (place == 96) & ((KSTR * key_a >= side) | (KSTR * key_b >= side))
    a1[:, 0:D] = kp[...][:, :D].astype(bf16)
    a1[:, D:] = jnp.where(shut, -1e30, hot).astype(bf16)
    vbt[:, 0:D] = vpool[...][:, :D].astype(bf16)
    vbt[:, D:] = jnp.where(lax.broadcasted_iota(jnp.int32, (KK, 16), 1) < 2, -1.0, 0.0).astype(bf16)
    a2[0:D, :] = jnp.transpose(kp[...])[:D, :].astype(bf16)
    vb[0:D, :] = jnp.transpose(vpool[...])[:D, :].astype(bf16)
    vb[D:, :] = jnp.ones((16, KK), bf16)
    key_l = lax.broadcasted_iota(jnp.int32, (48, KK), 1)
    a_l = lax.div(key_l, KG)
    b_l = key_l - KG * a_l
    row_l = lax.broadcasted_iota(jnp.int32, (48, KK), 0)
    hot_l = ((row_l < 24) & (KG - 1 - a_l == row_l)) | ((row_l >= 24) & (KG - 1 - b_l == row_l - 24))
    a2[D:, :] = jnp.where(hot_l, 1.0, 0.0).astype(bf16)

    def ahead(i, slot):
        weight_ref, low_ref, mixed_ref, half_ref, slope_ref, aaug, n2aug, oaug, scale_ref = slot
        tile = TILE_TWO
        here = plain(i, tile)
        row, col = idx_ref[0:1, inner(i, tile)] - i * TILE_ROWS, idx_ref[1:2, inner(i, tile)]
        near = [relh[pl.ds(40 * k + ROW_STEPS * i, 24), :] for k in range(4)]
        rel[0:D, :] = jnp.concatenate(near, axis=0)[:, :D].astype(bf16)
        q = qb[:, here]
        seen = dot(rel[...], q)
        rhs[0:D, :] = q
        yield True
        sides = jnp.concatenate([skew_rows(seen[0:D], row), skew_columns(seen[D:256], col)], axis=0)
        sides = sides * math.sqrt(D)
        sides_low = sides.astype(bf16)
        rhs[D : D + 48, :] = sides_low
        rhs[D + 48 : D + 96, :] = (sides - sides_low.astype(f32)).astype(bf16)
        scores = dot(a1[...], rhs[...])
        yield True
        weight = jnp.exp2((scores - jnp.max(scores, axis=0, keepdims=True)) * (SCORE_SCALE * LOG2E))
        weight_ref[...] = weight
        low_ref[...] = weight.astype(bf16)
        yield True
        mixed = dot(vb[...], low_ref[...])
        inv_sum = 1.0 / mixed[D : D + 1]
        scale_ref[0:1, :] = inv_sum
        mixed = mixed[0:D] * inv_sum
        mixed_ref[...] = mixed
        oaug[0:D, :] = (mixed + q.astype(f32)).astype(bf16)
        middle = x_ref[:, here].astype(f32) + dot(wp[...], oaug[...])
        yield True
        center = middle - jnp.sum(middle, axis=0, keepdims=True) * (1.0 / D)
        inv = lax.rsqrt(jnp.sum(center * center, axis=0, keepdims=True) * (1.0 / D) + norm_eps)
        half = center * (inv * math.sqrt(0.5))
        half_ref[...] = half
        scale_ref[1:2, :] = inv
        n2aug[0:D, :] = half.astype(bf16)
        z = dot(w1[...], n2aug[...])
        yield True
        below = lax.erf(z) * (0.5 * math.sqrt(math.pi)) + 0.5 * math.sqrt(math.pi)
        aaug[0:HID, :] = (z * below).astype(bf16)
        slope_ref[...] = below + z * jnp.exp2((z * z) * -LOG2E)
        yield True
        mlp = dot(w2[...], aaug[...])
        out_ref[:, here] = ((middle + mlp * math.sqrt(2.0 / math.pi)) * token_mask(i, tile)).astype(bf16)

    def behind(i, slot):
        weight_ref, low_ref, mixed_ref, half_ref, slope_ref, aaug, n2aug, oaug, scale_ref = slot
        tile = TILE_TWO
        here = plain(i, tile)
        row, col = idx_ref[0:1, inner(i, tile)] - i * TILE_ROWS, idx_ref[1:2, inner(i, tile)]
        near = [relh[pl.ds(40 * k + ROW_STEPS * i, 24), :] for k in range(4)]
        relt[:, 0:D] = jnp.transpose(jnp.concatenate(near, axis=0))[:D, :].astype(bf16)
        inv_sum, inv = scale_ref[0:1, :], scale_ref[1:2, :]
        gy = gy_ref[:, here].astype(f32) * token_mask(i, tile)
        gy_low = gy.astype(bf16)
        pushed = dot(w2t[...], gy_low)
        yield True
        gh_low = (slope_ref[...] * pushed).astype(bf16)
        dw2[:, 0:KK] += dot_nt(gy_low, aaug[...])
        gn = dot(w1t[...], gh_low)
        yield True
        dw1[0:112, :] += dot_nt(n2aug[...], gh_low)
        half = half_ref[...]
        mean = jnp.sum(gn, axis=0, keepdims=True) * (1.0 / D)
        along = jnp.sum(gn * half, axis=0, keepdims=True) * (2.0 / D)
        gmid = gy + (gn - mean - half * along) * (inv * math.sqrt(1.0 / math.pi))
        gm_low = gmid.astype(bf16)
        gm[:, here] = gm_low
        go = dot(wpt[...], gm_low)
        yield True
        dpr[:, 0:112] += dot_nt(gm_low, oaug[...])
        go_low = (go * inv_sum).astype(bf16)
        goaug[0:D, :] = go_low
        goaug[D:, :] = two_rows(jnp.sum(go_low.astype(f32) * mixed_ref[...], axis=0, keepdims=True))
        spread = dot(vbt[...], goaug[...])
        yield True
        gv[0:D, 0:KK] += dot_nt(go_low, low_ref[...])
        gse[0:KK, :] = (weight_ref[...] * spread).astype(bf16)
        back = dot(a2[...], gse[0:KK, :])
        yield True
        gse[KK : KK + D, :] = unskew_rows(back[D : D + 24], row).astype(bf16)
        gse[KK + D : KK + 256, :] = unskew_columns(back[D + 24 : D + 48], col).astype(bf16)
        yield True
        outer = dot_nt(qb[:, here], gse[...])
        gkr[0:D, 0 : KK + 256] += outer
        hacc[i] = outer[:, 384:512]
        gq[:, inner(i, tile)] = go + SCORE_SCALE * back[0:D] + dot(relt[...], gse[KK : KK + 256, :])

    one, two = slots
    gy_copy.wait()

    def attend(k, carry):
        interleave(ahead(2 * k + 1, two), behind(2 * k, one))
        interleave(ahead(2 * k + 2, one), behind(2 * k + 1, two))
        return carry

    interleave(ahead(0, one))
    lax.fori_loop(0, (TILES - 1) // 2, attend, 0)
    if TILES % 2 == 0:
        interleave(ahead(TILES - 1, two), behind(TILES - 2, one))
        interleave(behind(TILES - 1, two))
    else:
        interleave(behind(TILES - 1, one))

    out_copy = pltpu.make_async_copy(out_ref, out_hbm, copy_sem.at[2])
    out_copy.start()
    mid_copy = pltpu.make_async_copy(gm, mid_hbm, copy_sem.at[3])
    mid_copy.start()

    gkt[...] = jnp.transpose(gkr[:, 0:512])[0:KK, :] * SCORE_SCALE
    gvt[...] = jnp.transpose(gv[...])[0:KK, :]

    def pool_gradient(name, columns):
        low = columns.astype(bf16)
        for i in range(9):
            spread = dot_nt(low, tsel_ref[i]) * zsel_ref[i].astype(f32)
            gr[ROW[name] + i : ROW[name] + i + 1, 0:D] = jnp.sum(spread, axis=0, keepdims=True)

    for field, kernel_rows, pooled, gspread, name in ((fk, kk, gkt, gfk, "pool_k"), (fv, kv, gvt, gfv, "pool_v")):
        taps = tap_rows(kernel_rows)
        sums = [jnp.zeros((KG, 128), f32) for _ in range(9)]
        for a in range(KG):
            grad = pooled[KG * a : KG * a + KG, :]
            inside = jnp.where(b_index == 0, 0.0, grad)
            for k in range(9):
                where = pl.ds(tap_start(a, k // 3, k % 3), KG, stride=KSTR)
                sums[k] = sums[k] + (inside if k % 3 == 0 else grad) * field[where, :]
            spread_keys(taps, grad, a, gspread)
            if a == KG - 1:
                gspread[LEAD + TOK - GRID : LEAD + TOK, :] = jnp.zeros((GRID, 128), f32)
        rows = [jnp.sum(total, axis=0, keepdims=True) for total in sums]
        rows = jnp.concatenate(rows + [jnp.zeros((128 - 9, 128), f32)], axis=0)
        pool_gradient(name, jnp.transpose(rows)[:D, :])

    def finish(i, carry):
        tile = TILE_THREE
        wide = tile + 2 * HALO
        here = plain(i, tile)
        mid = slice(HALO, HALO + tile)
        mask = token_mask(i, tile)
        col = jnp.broadcast_to(idx_ref[1:2, inner(i, tile)], (8, tile))
        first, last = col == 0, col == GRID - 1
        for pair in range(D // 16):
            fields, moved = [], []
            for half in range(2):
                ch = slice(16 * pair + 8 * half, 16 * pair + 8 * half + 8)
                grad = gq[ch, window(i, tile)]
                below, above = pltpu.roll(grad, wide - GRID, 1), pltpu.roll(grad, GRID, 1)

                def col_sum(v):
                    return tap(v, ch, wide) * below + tap(v + 3, ch, wide) * grad + tap(v + 6, ch, wide) * above

                after = jnp.where(last, 0.0, pltpu.roll(col_sum(0), wide - 1, 1)[:, mid])
                before = jnp.where(first, 0.0, pltpu.roll(col_sum(2), 1, 1)[:, mid])
                fields.append((after + col_sum(1)[:, mid] + before) * mask)
                moved.append((below[:, mid], grad[:, mid], above[:, mid]))
            gfield[16 * pair : 16 * pair + 16, here] = jnp.concatenate(fields, axis=0).astype(bf16)
            for u in range(3):
                both = jnp.concatenate([moved[0][u], moved[1][u]], axis=0)
                place = group_row(pair, u)
                gsh[place : place + 16, :] = both.astype(bf16)
        for k in range(3):
            group = slice(k * D, (k + 1) * D)
            kqacc[group, 0:D] += dot_nt(gsh[group, :], fcol[group, here])
        flat = pl.ds(pl.multiple_of(i * tile + LEAD, 8), tile)
        gkv[:, 0:128] = gfk[flat, :].astype(bf16)
        gkv[:, 128:256] = gfv[flat, :].astype(bf16)
        dwq[:, 0:112] += dot_nt(gfield[:, here], un[:, here])
        dwkv[0:112, :] += dot(un[:, here], gkv[...])
        field_copy(i).start()
        return carry

    def field_copy(i):
        here = plain(i, TILE_THREE)
        return pltpu.make_async_copy(gfield.at[:, here], field_hbm.at[:, here], copy_sem.at[5 + i])

    lax.fori_loop(0, TOK // TILE_THREE, finish, 0)
    out_copy.wait()
    mid_copy.wait()
    unit_copy.wait()

    def write(name, rows, first=0):
        base = ROW[name] + first
        gr[base : base + rows.shape[0], 0:D] = rows

    def wide_rows(rows):
        return jnp.concatenate([rows, jnp.zeros((rows.shape[0], 128 - D), f32)], axis=1)

    def through_norm(name, first, outer, bias, gain_row, shift_row):
        raw = piece(name, outer.shape[0], first)[:, :D]
        write(name, outer * gain_row[:, :D] + bias * shift_row[:, :D], first)
        return jnp.sum(raw * outer, axis=0, keepdims=True), jnp.sum(raw * bias, axis=0, keepdims=True)

    gain, shift = through_norm("w_qkv", 0, dwq[:, 0:D], dwq[:, D : D + 1], g1_row, b1_row)
    write("b_qkv", jnp.transpose(dwq[...])[D : D + 1, :])
    for k in (1, 2):
        turned = jnp.transpose(dwkv[:, 128 * k - 128 : 128 * k])[0:D, :]
        more_gain, more_shift = through_norm("w_qkv", k * D, turned[:, 0:D], turned[:, D : D + 1], g1_row, b1_row)
        gain, shift = gain + more_gain, shift + more_shift
        write("b_qkv", dwkv[D : D + 1, 128 * k - 128 : 128 * k - 128 + D], k)
    write("ln1_g", gain)
    write("ln1_b", shift)

    lane = lax.broadcasted_iota(jnp.int32, (D, 128), 1)
    within = lane - lax.rem(lax.broadcasted_iota(jnp.int32, (D, 128), 0), 32)
    columns = jnp.zeros((D, 128), f32)
    for k in range(9):
        u, v = k // 3, k % 3
        picked = jnp.concatenate([kqacc[D * g + 32 * u : D * g + 32 * u + 32, :] for g in range(3)], axis=0)
        one = jnp.where(within == 32 * v, picked, 0.0)
        columns = jnp.where(lane == k, jnp.sum(one, axis=1, keepdims=True), columns)
    pool_gradient("pool_q", columns)

    for i in range(TILES):
        turned = jnp.transpose(hacc[i])
        for k in range(4):
            count = KG + ROW_STEPS - 1
            where = pl.ds(ROW["rel_h"] + 3 + k + TILE_ROWS * i, count, stride=4)
            gr[where, :] = gr[where, :] + wide_rows(turned[16 + 24 * k : 16 + 24 * k + count])
    turned = jnp.transpose(gkr[0:D, 384:768])
    for k in range(4):
        gr[pl.ds(ROW["rel_w"] + 3 + k, 39, stride=4), :] = wide_rows(turned[112 + 40 * k : 151 + 40 * k])

    write("w_proj", dpr[:, 0:D])
    write("b_proj", jnp.transpose(dpr[...])[D : D + 1, :])
    turned = jnp.transpose(dw1[...])
    gain, shift = through_norm(
        "w_fc1", 0, turned[:, 0:D] * math.sqrt(2.0 / math.pi), turned[:, D : D + 1] * math.sqrt(1.0 / math.pi), g2_row, b2_row
    )
    write("ln2_g", gain)
    write("ln2_b", shift)
    for k in range(4):
        write("b_fc1", dw1[D : D + 1, k * D : (k + 1) * D] * math.sqrt(1.0 / math.pi), k)
        gr[pl.ds(ROW["w_fc2"] + k, D, stride=4), :] = wide_rows(dw2[:, k * D : (k + 1) * D] * math.sqrt(2.0 / math.pi))
    write("b_fc2", jnp.transpose(dw2[:, HID:512])[0:1, :])
    for i in range(TOK // TILE_THREE):
        field_copy(i).wait()
    for w, start in enumerate(starts):
        gchunk_ref[w] = gr[start : start + rows_of, 0:D].astype(bf16)


def image_step(shard_len, chunks, pixels, image_side, cotangent):
    starts = tuple((shard_len * w) // D for w in range(chunks.shape[0]))
    rows_of = block_rows(shard_len)
    groups = -(-(shard_len * len(starts)) // (4 * D))
    depth = max(8 * (-(-(starts[-1] + rows_of) // 8)), 4 * groups)
    flat_rows = max(3 * groups, (shard_len * (len(starts) - 1)) // 128 + chunks.shape[1] + 1)
    flat_rows = 8 * (-(-flat_rows // 8))
    zsel, tsel = pool_selectors()
    vm = pltpu.VMEM
    scratch = [
        vm((depth, 128), f32),
        vm((D, 112), bf16), vm((112, 128), bf16), vm((112, 128), bf16),
        vm((D, 112), bf16), vm((D, D), bf16),
        vm((HID, 112), bf16), vm((D, HID), bf16), vm((D, KK), bf16), vm((HID, D), bf16),
        vm((168, 128), f32), vm((256, D), bf16), vm((D, 256), bf16),
        vm((D, 128), f32), vm((9, D, 128), f32),
        vm((D, TOK + 2 * HALO), f32), vm((FIELD, 128), f32), vm((FIELD, 128), f32),
        vm((D, TOK), bf16), vm((D, TOK), bf16),
        vm((112, TOK), bf16), vm((3 * D, TOK), bf16),
        vm((KK, 208), bf16), vm((144, KK), bf16), vm((112, KK), bf16), vm((KK, 112), bf16),
        vm((KK, 128), f32), vm((KK, 128), f32),
        vm((208, TILE_TWO), bf16), vm((KK + 256, TILE_TWO), bf16), vm((112, TILE_PROJECT), bf16), vm((112, TILE_TWO), bf16),
        vm((3 * D, TILE_THREE), bf16), vm((TILE_THREE, 256), bf16),
        vm((D, 512), f32), vm((128, HID), f32), vm((D, 128), f32), vm((128, 512), f32), vm((128, 768), f32),
        vm((TILES, D, 128), f32),
        vm((D, 128), f32), vm((128, 256), f32), vm((3 * D, 128), f32),
        vm((depth, 128), f32),
        vm((D, TOK), bf16), vm((D, TOK), bf16), vm((D, TOK), bf16), vm((D, TOK), bf16),
        pltpu.SemaphoreType.DMA((5 + TOK // TILE_THREE,)),
        vm((flat_rows, 128), f32),
        vm(zsel.shape, bf16), vm(tsel.shape, bf16), vm((8, TOK + 2 * HALO), jnp.int32), pltpu.SemaphoreType.DMA((3,)),
    ]
    slot = [
        vm((KK, TILE_TWO), f32), vm((KK, TILE_TWO), bf16), vm((D, TILE_TWO), f32), vm((D, TILE_TWO), f32), vm((HID, TILE_TWO), f32),
        vm((KK, TILE_TWO), bf16), vm((112, TILE_TWO), bf16), vm((112, TILE_TWO), bf16), vm((8, TILE_TWO), f32),
    ]
    whole = pl.BlockSpec(memory_space=pltpu.VMEM)
    far = pl.BlockSpec(memory_space=pl.ANY)
    shape = jax.ShapeDtypeStruct
    out, grad_chunks, *rest = pl.pallas_call(
        functools.partial(image_kernel, shard_len, starts, rows_of),
        out_shape=(
            shape((D, TOK), bf16), shape((len(starts), rows_of, D), bf16),
            shape((D, TOK), bf16), shape((D, TOK), bf16), shape((D, TOK), bf16), shape((8, TOK), f32),
            shape((KK, 128), f32), shape((KK, 128), f32), shape((16, 128), f32), shape((16, 128), f32),
            shape((D, D), bf16), shape((D, 256), bf16),
        ),
        in_specs=[pl.BlockSpec(memory_space=pltpu.SMEM), whole, far, far, far, far, far],
        out_specs=(far, whole, far, far, far) + (whole,) * 7,
        scratch_shapes=scratch + slot + slot,
        compiler_params=pltpu.CompilerParams(vmem_limit_bytes=54 * 1024 * 1024),
        name="image_step",
    )(image_side, chunks, pixels, cotangent, lane_index(), zsel, tsel)
    return out, grad_chunks, rest


def input_step(rest):
    far = pl.BlockSpec(memory_space=pl.ANY)
    vm = pltpu.VMEM
    scratch = [vm(part.shape, part.dtype) for part in rest]
    scratch += [vm((D, TOK), bf16), vm((FIELD, 128), f32), vm((FIELD, 128), f32), vm((TILE_THREE, 256), bf16)]
    return pl.pallas_call(
        input_kernel,
        out_shape=jax.ShapeDtypeStruct((D, TOK), bf16),
        in_specs=[far] * len(rest),
        out_specs=far,
        scratch_shapes=scratch + [pltpu.SemaphoreType.DMA((10 + TOK // TILE_THREE,))],
        compiler_params=pltpu.CompilerParams(vmem_limit_bytes=60 * 1024 * 1024),
        cost_estimate=pl.CostEstimate(flops=2 * D * 3 * D * TOK, bytes_accessed=16 * 1024 * 1024, transcendentals=0),
        name="input_step",
    )(*rest)


def adam_update(gradient, master_part, first_part, second_part, average_part, step_rates):
    moment_one = beta_first * first_part + (1.0 - beta_first) * gradient
    moment_two = beta_second * second_part + (1.0 - beta_second) * gradient * gradient
    fix_one = 1.0 - beta_first**STEP
    fix_two = 1.0 - beta_second**STEP
    direction = moment_one / fix_one / (jnp.sqrt(moment_two / fix_two) + adam_eps)
    updated = master_part - step_rates * (direction + weight_decay * master_part)
    blended = average_decay * average_part + (1.0 - average_decay) * updated
    return (updated, moment_one, moment_two, blended)


def shards(tokens, image_sides, grad_out, master, first_moment, second_moment, weight_average):
    shard_len = master.shape[0]
    owners = lax.axis_size("wide")
    images_all = tokens.shape[0] * owners * lax.axis_size("narrow")
    rows_of = block_rows(shard_len)
    inset = lax.rem(lax.axis_index("wide") * shard_len, D)

    filled = 1024 * (-(-shard_len // 1024))
    own = jnp.pad(master, (0, filled - shard_len)).reshape(1, filled // 128, 128).astype(bf16)
    chunks = lax.all_to_all(jnp.broadcast_to(own, (owners, filled // 128, 128)), "wide", 0, 0)

    outs, grads_in, grad_chunks = [], [], None
    for k in range(tokens.shape[0]):
        out, chunk, rest = image_step(shard_len, chunks, tokens[k], image_sides[k : k + 1], grad_out[k])
        outs.append(out)
        grads_in.append(input_step(rest))
        grad_chunks = chunk if k == 0 else (grad_chunks.astype(f32) + chunk.astype(f32)).astype(bf16)
    block_out = jnp.stack(outs)
    grad_in = jnp.stack(grads_in)

    parts = lax.all_to_all(grad_chunks, "wide", 0, 0)
    step_rates = lax.dynamic_slice_in_dim(
        jnp.asarray(rate_values(shard_len * owners)), lax.axis_index("wide") * shard_len, shard_len
    )
    parts, grad_in, step_rates = lax.optimization_barrier((parts, grad_in, step_rates))
    total = jnp.sum(parts.astype(f32), axis=0)
    total = total + lax.ppermute(total, "narrow", [(0, 1), (1, 0)])
    reduced = lax.dynamic_slice(total.reshape(rows_of * D), (inset,), (shard_len,))
    updated, moment_one, moment_two, blended = adam_update(
        reduced / images_all, master, first_moment, second_moment, weight_average, step_rates
    )
    return (block_out, grad_in, updated, moment_one, moment_two, blended)


def solution(mesh):
    return jax.shard_map(
        shards,
        mesh=mesh,
        in_specs=(
            P(("wide", "narrow"), None, None),
            P(("wide", "narrow")),
            P(("wide", "narrow"), None, None),
            P("wide"),
            P("wide"),
            P("wide"),
            P("wide"),
        ),
        out_specs=(
            P(("wide", "narrow"), None, None),
            P(("wide", "narrow"), None, None),
            P("wide"),
            P("wide"),
            P("wide"),
            P("wide"),
        ),
        check_vma=False,
    )
```

```python
import functools
import math

import jax
import jax.numpy as jnp
import numpy as np
from jax import lax
from jax.experimental import pallas as pl
from jax.experimental.pallas import tpu as pltpu
from jax.sharding import PartitionSpec as P

D = 96
HID = 384
KSTR = 4
KG = 20
STEP = 5
GRID = 80
TOK = 6400
KK = 400
REL = 159

norm_eps = 1e-06
beta_first = 0.5
beta_second = 0.5
adam_eps = 1e-08
weight_decay = 0.05
rate_factor = 0.4
average_decay = 0.8

f32 = jnp.float32
bf16 = jnp.bfloat16

HALO = 128
LEAD = 88
FIELD = LEAD + TOK + 8
TILE_PROJECT = 6400
TILE_ONE = 6400
TILE_TWO = 1280
TILE_THREE = 1280
TILES = TOK // TILE_TWO
TILE_ROWS = TILE_TWO // GRID
ROW_STEPS = TILE_ROWS // KSTR
SCORE_SCALE = D ** (-0.5)
LOG2E = 1.4426950408889634


def segment_list():
    return [
        ("w_qkv", (3 * D, D), D ** (-0.5)),
        ("b_qkv", (3 * D,), 0.2),
        ("pool_q", (D, 9), 1.0 / 3.0),
        ("pool_k", (D, 9), 1.0 / 3.0),
        ("pool_v", (D, 9), 1.0 / 3.0),
        ("rel_h", (REL, D), 0.5 * D ** (-0.5)),
        ("rel_w", (REL, D), 0.5 * D ** (-0.5)),
        ("w_proj", (D, D), D ** (-0.5)),
        ("b_proj", (D,), 0.2),
        ("w_fc1", (HID, D), D ** (-0.5)),
        ("b_fc1", (HID,), 0.2),
        ("w_fc2", (D, HID), HID ** (-0.5)),
        ("b_fc2", (D,), 0.2),
        ("ln1_g", (D,), 0.5),
        ("ln1_b", (D,), 0.2),
        ("ln2_g", (D,), 0.5),
        ("ln2_b", (D,), 0.2),
    ]


def row_bases():
    bases = {}
    offset = 0
    for name, shape, _ in segment_list():
        assert offset % D == 0
        bases[name] = offset // D
        offset += math.prod(shape)
    return bases


ROW = row_bases()


def rate_values(full_len):
    rates = np.full((full_len,), rate_factor * D ** (-0.5), np.float32)
    offset = 0
    for _, shape, spread in segment_list():
        length = math.prod(shape)
        rates[offset : offset + length] = rate_factor * spread
        offset += length
    return rates


def block_rows(shard_len):
    return 16 * (-(-(-(-(shard_len + D - 1) // D)) // 16))


def pool_selectors():
    flat = np.arange(9 * D).reshape(9, D)
    channel = (flat[:, None, :] // 9 == np.arange(D)[None, :, None]).astype(np.float32)
    tap = (flat[:, :, None] % 9 == np.arange(128)[None, None, :]).astype(np.float32)
    return jnp.asarray(channel, bf16), jnp.asarray(tap, bf16)


def lane_index():
    place = np.arange(-HALO, TOK + HALO)
    table = np.zeros((8, TOK + 2 * HALO), np.int32)
    table[0] = place // GRID
    table[1] = place % GRID
    return jnp.asarray(table)


def dot(a, b):
    return lax.dot_general(a, b, (((1,), (0,)), ((), ())), preferred_element_type=f32)


def dot_nt(a, b):
    return lax.dot_general(a, b, (((1,), (1,)), ((), ())), preferred_element_type=f32)


def dot_tn(a, b):
    return lax.dot_general(a, b, (((0,), (0,)), ((), ())), preferred_element_type=f32)


def normalize(values):
    mean = jnp.sum(values, axis=0, keepdims=True) * (1.0 / D)
    center = values - mean
    spread = jnp.sum(center * center, axis=0, keepdims=True) * (1.0 / D)
    inv = lax.rsqrt(spread + norm_eps)
    return center * inv, inv


def skew_rows(rows, place):
    width = rows.shape[1]
    where = jnp.broadcast_to(place, (24, width))
    residue = where & 3
    x = jnp.where(
        residue < 2,
        jnp.where(residue == 0, rows[0:24], rows[24:48]),
        jnp.where(residue == 2, rows[48:72], rows[72:96]),
    )
    step = ROW_STEPS // 2
    while step >= 1:
        x = jnp.where((where & (4 * step)) != 0, pltpu.roll(x, 24 - step, 0), x)
        step //= 2
    return x


def skew_columns(rows, place):
    width = rows.shape[1]
    where = jnp.broadcast_to(place, (40, width))
    residue = where & 3
    x = jnp.where(
        residue < 2,
        jnp.where(residue == 0, rows[0:40], rows[40:80]),
        jnp.where(residue == 2, rows[80:120], rows[120:160]),
    )
    x = jnp.concatenate([jnp.where((where[0:24] & 64) != 0, x[16:40], x[0:24]), x[24:40]], axis=0)
    x = jnp.where((where[0:32] & 32) != 0, x[8:40], x[0:32])
    where = where[0:24]
    x = jnp.where((where & 16) != 0, pltpu.roll(x, 28, 0)[0:24], x[0:24])
    x = jnp.where((where & 8) != 0, pltpu.roll(x, 22, 0), x)
    return jnp.where((where & 4) != 0, pltpu.roll(x, 23, 0), x)


def unskew_rows(x, place):
    where = jnp.broadcast_to(place, x.shape)
    step = 1
    while step < ROW_STEPS:
        x = jnp.where((where & (4 * step)) != 0, pltpu.roll(x, step, 0), x)
        step *= 2
    residue = where & 3
    return jnp.concatenate([jnp.where(residue == k, x, 0.0) for k in range(4)], axis=0)


def unskew_columns(x, place):
    width = x.shape[1]
    zero = jnp.zeros((8, width), f32)
    where = jnp.broadcast_to(place, (40, width))
    x = jnp.where((where[0:24] & 4) != 0, pltpu.roll(x, 1, 0), x)
    x = jnp.where((where[0:24] & 8) != 0, pltpu.roll(x, 2, 0), x)
    x = jnp.concatenate([x, zero], axis=0)
    x = jnp.where((where[0:32] & 16) != 0, pltpu.roll(x, 4, 0), x)
    x = jnp.where((where & 32) != 0, jnp.concatenate([zero, x], axis=0), jnp.concatenate([x, zero], axis=0))
    far = (where & 64) != 0
    x = jnp.concatenate([jnp.where(far[0:16], 0.0, x[0:16]), jnp.where(far[16:40], x[0:24], x[16:40])], axis=0)
    residue = where & 3
    return jnp.concatenate([jnp.where(residue == k, x, 0.0) for k in range(4)], axis=0)


def group_row(pair, shift):
    return D * (pair // 2) + 32 * shift + 16 * (pair % 2)


def aligned(value, step):
    return value if isinstance(value, int) else pl.multiple_of(value, step)


def interleave(*parts):
    live = list(parts)
    while live:
        for part in list(live):
            if next(part, None) is None:
                live.remove(part)


def two_columns(column):
    high = column.astype(bf16).astype(f32)
    place = lax.broadcasted_iota(jnp.int32, (column.shape[0], 16), 1)
    return jnp.where(place == 0, high, jnp.where(place == 1, column - high, 0.0)).astype(bf16)


def two_rows(row):
    high = row.astype(bf16).astype(f32)
    place = lax.broadcasted_iota(jnp.int32, (16, row.shape[1]), 0)
    return jnp.where(place == 0, high, jnp.where(place == 1, row - high, 0.0)).astype(bf16)


def two_ones(width):
    return jnp.where(lax.broadcasted_iota(jnp.int32, (16, width), 0) < 2, 1.0, 0.0).astype(bf16)


def key_columns():
    return lax.broadcasted_iota(jnp.int32, (KG, 128), 0)


def tap_start(a, u, v):
    return LEAD + GRID * (KSTR * a + u - 1) + v - 1


def tap_rows(kernel_rows):
    b_index = key_columns()
    taps = [jnp.broadcast_to(kernel_rows[k : k + 1, :], (KG, 128)) for k in range(9)]
    return [jnp.where(b_index == 0, 0.0, tap) if k % 3 == 0 else tap for k, tap in enumerate(taps)]


def spread_keys(taps, grad, a, gfield):
    idle = LEAD + GRID * (KSTR * a + 2)
    gfield[pl.ds(aligned(idle - 8, 8), GRID + 8), :] = jnp.zeros((GRID + 8, 128), f32)
    for u in range(3):
        gfield[pl.ds(tap_start(a, u, 3), KG, stride=KSTR), :] = jnp.zeros((KG, 128), f32)
    for k in range(9):
        gfield[pl.ds(tap_start(a, k // 3, k % 3), KG, stride=KSTR), :] = taps[k] * grad


def input_kernel(*refs):
    sources, gin_hbm, held = refs[:10], refs[10], refs[11:21]
    field_ref, mid_ref, unit_ref, inv_ref, gkt, gvt, kk, kv, wqt, wkvg = held
    gin_ref, gfk, gfv, gkv, copy_sem = refs[21:]
    copies = [pltpu.make_async_copy(a, b, copy_sem.at[k]) for k, (a, b) in enumerate(zip(sources, held))]
    for copy in copies[::-1]:
        copy.start()
    for copy in copies[4:]:
        copy.wait()
    for kernel_rows, pooled, gfield in ((kk, gkt, gfk), (kv, gvt, gfv)):
        taps = tap_rows(kernel_rows)

        def spread(a, carry):
            spread_keys(taps, pooled[pl.ds(KG * a, KG), :], a, gfield)
            return carry

        lax.fori_loop(0, KG, spread, 0)
        gfield[LEAD + TOK - GRID : LEAD + TOK, :] = jnp.zeros((GRID, 128), f32)
    for copy in copies[:4]:
        copy.wait()

    def gin_copy(i):
        here = pl.ds(aligned(i * TILE_THREE, 128), TILE_THREE)
        return pltpu.make_async_copy(gin_ref.at[:, here], gin_hbm.at[:, here], copy_sem.at[10 + i])

    def finish(i, carry):
        tile = TILE_THREE
        here = pl.ds(aligned(i * tile, 128), tile)
        flat = pl.ds(aligned(i * tile + LEAD, 8), tile)
        gkv[:, 0:128] = gfk[flat, :].astype(bf16)
        gkv[:, 128:256] = gfv[flat, :].astype(bf16)
        gn = dot(wqt[...], field_ref[:, here]) + dot_nt(wkvg[...], gkv[...])
        unit = unit_ref[:, here].astype(f32)
        mean = jnp.sum(gn, axis=0, keepdims=True) * (1.0 / D)
        along = jnp.sum(gn * unit, axis=0, keepdims=True) * (1.0 / D)
        total = mid_ref[:, here].astype(f32) + (gn - mean - unit * along) * inv_ref[0:1, here]
        gin_ref[:, here] = total.astype(bf16)
        gin_copy(i).start()
        return carry

    lax.fori_loop(0, TOK // TILE_THREE, finish, 0)
    for i in range(TOK // TILE_THREE):
        gin_copy(i).wait()


def image_kernel(
    shard_len,
    starts,
    rows_of,
    side_ref,
    chunk_ref,
    x_hbm,
    gy_hbm,
    idx_hbm,
    zsel_hbm,
    tsel_hbm,
    out_hbm,
    gchunk_ref,
    field_hbm,
    mid_hbm,
    unit_hbm,
    inv_ref,
    gkt,
    gvt,
    kk,
    kv,
    wqt,
    wkvg,
    wf, wq, wkt, wvt, wp, wpt, w1, w1t, w2, w2t, relh, rel, relt, cols, kq,
    fq, fk, fv, qb, gm, un, fcol,
    a1, a2, vb, vbt, kp, vpool,
    rhs, gse, n1aug, goaug, gsh, gkv,
    dw2, dw1, dpr, gv, gkr, hacc, dwq, dwkv, kqacc, gr, x_ref, gy_ref, out_ref, gfield, copy_sem, flat, zsel_ref, tsel_ref, idx_ref, table_sem,
    *slot_refs,
):
    gq, gfk, gfv = fq, fk, fv
    slots = (slot_refs[: len(slot_refs) // 2], slot_refs[len(slot_refs) // 2 :])
    side = side_ref[0]
    table_copies = [
        pltpu.make_async_copy(source, target, table_sem.at[k])
        for k, (source, target) in enumerate(((zsel_hbm, zsel_ref), (tsel_hbm, tsel_ref), (idx_hbm, idx_ref)))
    ]
    for copy in table_copies:
        copy.start()
    x_copy = pltpu.make_async_copy(x_hbm, x_ref, copy_sem.at[0])
    gy_copy = pltpu.make_async_copy(gy_hbm, gy_ref, copy_sem.at[1])
    x_copy.start()
    gy_copy.start()

    flat[...] = jnp.zeros(flat.shape, f32)
    lane_of = lax.broadcasted_iota(jnp.int32, chunk_ref.shape[1:], 1)
    for w in range(len(starts)):
        base, inset = (shard_len * w) // 128, (shard_len * w) % 128
        part = chunk_ref[w].astype(f32)
        if inset:
            part = pltpu.roll(part, inset, 1)
            flat[base + 1 : base + 1 + part.shape[0], :] += jnp.where(lane_of < inset, part, 0.0)
            part = jnp.where(lane_of < inset, 0.0, part)
        flat[base : base + part.shape[0], :] += part
    groups = -(-(shard_len * len(starts)) // (4 * D))
    lane_of = lax.broadcasted_iota(jnp.int32, (groups, 128), 1)
    first, second, third = (flat[pl.ds(k, groups, stride=3), :] for k in range(3))
    wf[pl.ds(0, groups, stride=4), :] = first
    wf[pl.ds(1, groups, stride=4), :] = pltpu.roll(jnp.where(lane_of >= 96, first, second), 32, 1)
    wf[pl.ds(2, groups, stride=4), :] = pltpu.roll(jnp.where(lane_of >= 64, second, third), 64, 1)
    wf[pl.ds(3, groups, stride=4), :] = pltpu.roll(third, 96, 1)

    def piece(name, count, first=0):
        base = ROW[name] + first
        return wf[base : base + count, :]

    vec_rows = [ROW["b_qkv"], ROW["b_proj"], ROW["b_fc2"], ROW["ln1_g"], ROW["ln1_b"], ROW["ln2_g"], ROW["ln2_b"]]
    vec_rows += [ROW["b_fc1"] + k for k in range(4)]
    stacked = jnp.concatenate([wf[r : r + 1, :] for r in vec_rows] + [jnp.zeros((128 - len(vec_rows), 128), f32)], axis=0)
    cols[...] = jnp.transpose(stacked)[:D, :]
    cols_low = cols[...].astype(bf16)
    g1_row, b1_row = piece("ln1_g", 1), piece("ln1_b", 1)
    g2_row, b2_row = piece("ln2_g", 1), piece("ln2_b", 1)

    def through(name, count, first, column):
        return dot(piece(name, count, first)[:, :D].astype(bf16), cols_low)[:, column : column + 1]

    wq_gain = piece("w_qkv", D) * g1_row
    wq[:, 0:D] = piece("w_qkv", D)[:, :D].astype(bf16)
    wq[:, D:] = two_columns(cols[:, 0:1])
    wqt[...] = jnp.transpose(wq_gain)[:D, :].astype(bf16)
    for k, ref in ((1, wkt), (2, wvt)):
        ref[...] = jnp.zeros(ref.shape, bf16)
        ref[0:D, 0:D] = jnp.transpose(piece("w_qkv", D, k * D))[:D, :].astype(bf16)
        ref[D:, 0:D] = two_rows(piece("b_qkv", 1, k)[:, :D])
        wkvg[:, 128 * k - 128 : 128 * k] = jnp.zeros((D, 128), bf16)
        wkvg[:, 128 * k - 128 : 128 * k - 128 + D] = jnp.transpose(piece("w_qkv", D, k * D) * g1_row)[:D, :].astype(bf16)
    wp[:, 0:D] = piece("w_proj", D)[:, :D].astype(bf16)
    wp[:, D:] = two_columns(cols[:, 1:2])
    wpt[...] = jnp.transpose(piece("w_proj", D))[:D, :].astype(bf16)
    w1_gain = piece("w_fc1", HID) * g2_row
    b_fc1 = jnp.concatenate([cols[:, 7 + k : 8 + k] for k in range(4)], axis=0)
    w1[:, 0:D] = w1_gain[:, :D].astype(bf16)
    w1[:, D:] = two_columns((b_fc1 + through("w_fc1", HID, 0, 6)) * math.sqrt(0.5))
    w1t[...] = jnp.transpose(w1_gain)[:D, :].astype(bf16)
    for k in range(4):
        block = wf[pl.ds(ROW["w_fc2"] + k, D, stride=4), :]
        w2t[k * D : (k + 1) * D, :] = jnp.transpose(block)[:D, :].astype(bf16)
    w2[:, 0:HID] = jnp.transpose(w2t[...].astype(f32)).astype(bf16)
    w2[:, HID:] = two_columns(cols[:, 2:3] * math.sqrt(0.5 * math.pi))
    relh[160:, :] = jnp.zeros((8, 128), f32)
    for k in range(4):
        relh[k * 40 : k * 40 + 40, :] = wf[pl.ds(ROW["rel_h"] + 3 + k, 40, stride=4), :]
    rel_w = jnp.concatenate([wf[pl.ds(ROW["rel_w"] + 3 + k, 40, stride=4), :] for k in range(4)], axis=0)
    rel[D:256, :] = rel_w[:, :D].astype(bf16)
    relt[:, D:256] = jnp.transpose(rel_w)[:D, :].astype(bf16)

    def pool_columns(name):
        total = jnp.zeros((D, 128), f32)
        for i in range(9):
            row = wf[ROW[name] + i : ROW[name] + i + 1, :][:, :D]
            total = total + dot((zsel_ref[i].astype(f32) * row).astype(bf16), tsel_ref[i])
        return total

    def pool_rows(name):
        full = jnp.concatenate([pool_columns(name), jnp.zeros((32, 128), f32)], axis=0)
        return jnp.transpose(full)[0:16, :]

    for copy in table_copies:
        copy.wait()
    pooled_kernel = pool_columns("pool_q")
    for k in range(9):
        kq[k] = jnp.broadcast_to(pooled_kernel[:, k : k + 1], (D, 128))

    def tap(k, ch, width):
        return jnp.concatenate([kq[k, ch, :]] * (width // 128), axis=1)

    kk[...] = pool_rows("pool_k")
    kv[...] = pool_rows("pool_v")

    for ref in (fq,):
        ref[:, 0:HALO] = jnp.zeros((D, HALO), f32)
        ref[:, HALO + TOK :] = jnp.zeros((D, HALO), f32)
    for ref in (fk, fv):
        ref[0:LEAD, :] = jnp.zeros((LEAD, 128), f32)
    for ref in (dw2, dw1, dpr, gv, gkr, dwq, dwkv, kqacc):
        ref[...] = jnp.zeros(ref.shape, ref.dtype)
    gr[ROW["rel_h"] : ROW["w_proj"], :] = jnp.zeros((2 * REL, 128), f32)
    tail = ROW["ln2_b"]
    gr[tail:, :] = jnp.zeros((gr.shape[0] - tail, 128), f32)

    un[D:, :] = two_ones(TOK)
    n1aug[D:, :] = two_ones(TILE_PROJECT)
    for slot in slots:
        slot[5][HID:, :] = two_ones(TILE_TWO)
        slot[6][D:, :] = two_ones(TILE_TWO)
        slot[7][D:, :] = two_ones(TILE_TWO)
    rhs[192:208, :] = two_ones(TILE_TWO)

    def window(i, tile):
        return pl.ds(aligned(i * tile, 128), tile + 2 * HALO)

    def inner(i, tile):
        return pl.ds(aligned(i * tile + HALO, 128), tile)

    def plain(i, tile):
        return pl.ds(aligned(i * tile, 128), tile)

    def token_mask(i, tile):
        place = idx_ref[0:2, inner(i, tile)]
        return jnp.where((place[0:1] < side) & (place[1:2] < side), 1.0, 0.0)

    x_copy.wait()

    def project(i, carry):
        here = plain(i, TILE_PROJECT)
        unit, inv = normalize(x_ref[:, here].astype(f32))
        un[0:D, here] = unit.astype(bf16)
        inv_ref[0:1, here] = inv
        n1aug[0:D, :] = (unit * cols[:, 3:4] + cols[:, 4:5]).astype(bf16)
        fq[:, inner(i, TILE_PROJECT)] = dot(wq[...], n1aug[...]) * token_mask(i, TILE_PROJECT)
        field = pl.ds(pl.multiple_of(i * TILE_PROJECT + LEAD, 8), TILE_PROJECT)
        fk[field, :] = dot_tn(n1aug[...], wkt[...])
        fv[field, :] = dot_tn(n1aug[...], wvt[...])
        return carry

    lax.fori_loop(0, TOK // TILE_PROJECT, project, 0)

    unit_copy = pltpu.make_async_copy(un.at[0:D, :], unit_hbm, copy_sem.at[4])
    unit_copy.start()

    def pool_queries(i, carry):
        tile = TILE_ONE
        wide = tile + 2 * HALO
        mid = slice(HALO, HALO + tile)
        col = jnp.broadcast_to(idx_ref[1:2, window(i, tile)], (8, wide))
        first, last = col == 0, col == GRID - 1
        mask = token_mask(i, tile)
        for pair in range(D // 16):
            pooled, moved = [], []
            for half in range(2):
                ch = slice(16 * pair + 8 * half, 16 * pair + 8 * half + 8)
                field = fq[ch, window(i, tile)]
                left = jnp.where(first, 0.0, pltpu.roll(field, 1, 1))
                right = jnp.where(last, 0.0, pltpu.roll(field, wide - 1, 1))

                def row_sum(u):
                    return tap(3 * u, ch, wide) * left + tap(3 * u + 1, ch, wide) * field + tap(3 * u + 2, ch, wide) * right

                total = pltpu.roll(row_sum(0), GRID, 1) + row_sum(1) + pltpu.roll(row_sum(2), wide - GRID, 1)
                pooled.append(total[:, mid] * mask)
                moved.append((left[:, mid], field[:, mid], right[:, mid]))
            qb[16 * pair : 16 * pair + 16, plain(i, tile)] = jnp.concatenate(pooled, axis=0).astype(bf16)
            for v in range(3):
                both = jnp.concatenate([moved[0][v], moved[1][v]], axis=0)
                place = group_row(pair, v)
                fcol[place : place + 16, plain(i, tile)] = both.astype(bf16)
        return carry

    lax.fori_loop(0, TOK // TILE_ONE, pool_queries, 0)

    b_index = key_columns()

    for field, kernel_rows, pooled in ((fk, kk, kp), (fv, kv, vpool)):
        taps = tap_rows(kernel_rows)
        for a in range(KG):
            total = jnp.zeros((KG, 128), f32)
            for k in range(9):
                total = total + taps[k] * field[pl.ds(tap_start(a, k // 3, k % 3), KG, stride=KSTR), :]
            keep = (KSTR * b_index < side) & (KSTR * a < side)
            pooled[KG * a : KG * a + KG, :] = jnp.where(keep, total, 0.0)

    key = lax.broadcasted_iota(jnp.int32, (KK, 112), 0)
    key_a = lax.div(key, KG)
    key_b = key - KG * key_a
    place = lax.broadcasted_iota(jnp.int32, (KK, 112), 1)
    hot = jnp.zeros((KK, 112), f32)
    for base in (0, 48):
        one_a = (place >= base) & (place < base + 24) & (KG - 1 - key_a == place - base)
        one_b = (place >= base + 24) & (place < base + 48) & (KG - 1 - key_b == place - base - 24)
        hot = jnp.where(one_a | one_b, 1.0, hot)
    shut = (place == 96) & ((KSTR * key_a >= side) | (KSTR * key_b >= side))
    a1[:, 0:D] = kp[...][:, :D].astype(bf16)
    a1[:, D:] = jnp.where(shut, -1e30, hot).astype(bf16)
    vbt[:, 0:D] = vpool[...][:, :D].astype(bf16)
    vbt[:, D:] = jnp.where(lax.broadcasted_iota(jnp.int32, (KK, 16), 1) < 2, -1.0, 0.0).astype(bf16)
    a2[0:D, :] = jnp.transpose(kp[...])[:D, :].astype(bf16)
    vb[0:D, :] = jnp.transpose(vpool[...])[:D, :].astype(bf16)
    vb[D:, :] = jnp.ones((16, KK), bf16)
    key_l = lax.broadcasted_iota(jnp.int32, (48, KK), 1)
    a_l = lax.div(key_l, KG)
    b_l = key_l - KG * a_l
    row_l = lax.broadcasted_iota(jnp.int32, (48, KK), 0)
    hot_l = ((row_l < 24) & (KG - 1 - a_l == row_l)) | ((row_l >= 24) & (KG - 1 - b_l == row_l - 24))
    a2[D:, :] = jnp.where(hot_l, 1.0, 0.0).astype(bf16)

    def ahead(i, slot):
        weight_ref, low_ref, mixed_ref, half_ref, slope_ref, aaug, n2aug, oaug, scale_ref = slot
        tile = TILE_TWO
        here = plain(i, tile)
        row, col = idx_ref[0:1, inner(i, tile)] - i * TILE_ROWS, idx_ref[1:2, inner(i, tile)]
        near = [relh[pl.ds(40 * k + ROW_STEPS * i, 24), :] for k in range(4)]
        rel[0:D, :] = jnp.concatenate(near, axis=0)[:, :D].astype(bf16)
        q = qb[:, here]
        seen = dot(rel[...], q)
        rhs[0:D, :] = q
        yield True
        sides = jnp.concatenate([skew_rows(seen[0:D], row), skew_columns(seen[D:256], col)], axis=0)
        sides = sides * math.sqrt(D)
        sides_low = sides.astype(bf16)
        rhs[D : D + 48, :] = sides_low
        rhs[D + 48 : D + 96, :] = (sides - sides_low.astype(f32)).astype(bf16)
        scores = dot(a1[...], rhs[...])
        yield True
        weight = jnp.exp2((scores - jnp.max(scores, axis=0, keepdims=True)) * (SCORE_SCALE * LOG2E))
        low_ref[...] = weight.astype(bf16)
        yield True
        mixed = dot(vb[...], low_ref[...])
        inv_sum = 1.0 / mixed[D : D + 1]
        scale_ref[0:1, :] = inv_sum
        mixed = mixed[0:D] * inv_sum
        mixed_ref[...] = mixed
        oaug[0:D, :] = (mixed + q.astype(f32)).astype(bf16)
        middle = x_ref[:, here].astype(f32) + dot(wp[...], oaug[...])
        yield True
        center = middle - jnp.sum(middle, axis=0, keepdims=True) * (1.0 / D)
        inv = lax.rsqrt(jnp.sum(center * center, axis=0, keepdims=True) * (1.0 / D) + norm_eps)
        half = center * (inv * math.sqrt(0.5))
        scale_ref[1:2, :] = inv
        n2aug[0:D, :] = half.astype(bf16)
        z = dot(w1[...], n2aug[...])
        yield True
        below = lax.erf(z) * (0.5 * math.sqrt(math.pi)) + 0.5 * math.sqrt(math.pi)
        aaug[0:HID, :] = (z * below).astype(bf16)
        slope_ref[...] = below + z * jnp.exp2((z * z) * -LOG2E)
        yield True
        mlp = dot(w2[...], aaug[...])
        out_ref[:, here] = ((middle + mlp * math.sqrt(2.0 / math.pi)) * token_mask(i, tile)).astype(bf16)

    def behind(i, slot):
        weight_ref, low_ref, mixed_ref, half_ref, slope_ref, aaug, n2aug, oaug, scale_ref = slot
        tile = TILE_TWO
        here = plain(i, tile)
        row, col = idx_ref[0:1, inner(i, tile)] - i * TILE_ROWS, idx_ref[1:2, inner(i, tile)]
        near = [relh[pl.ds(40 * k + ROW_STEPS * i, 24), :] for k in range(4)]
        relt[:, 0:D] = jnp.transpose(jnp.concatenate(near, axis=0))[:D, :].astype(bf16)
        inv_sum, inv = scale_ref[0:1, :], scale_ref[1:2, :]
        gy = gy_ref[:, here].astype(f32) * token_mask(i, tile)
        gy_low = gy.astype(bf16)
        pushed = dot(w2t[...], gy_low)
        yield True
        gh_low = (slope_ref[...] * pushed).astype(bf16)
        dw2[:, 0:KK] += dot_nt(gy_low, aaug[...])
        gn = dot(w1t[...], gh_low)
        yield True
        dw1[0:112, :] += dot_nt(n2aug[...], gh_low)
        half = n2aug[0:D, :].astype(f32)
        mean = jnp.sum(gn, axis=0, keepdims=True) * (1.0 / D)
        along = jnp.sum(gn * half, axis=0, keepdims=True) * (2.0 / D)
        gmid = gy + (gn - mean - half * along) * (inv * math.sqrt(1.0 / math.pi))
        gm_low = gmid.astype(bf16)
        gm[:, here] = gm_low
        go = dot(wpt[...], gm_low)
        yield True
        dpr[:, 0:112] += dot_nt(gm_low, oaug[...])
        go_low = (go * inv_sum).astype(bf16)
        goaug[0:D, :] = go_low
        goaug[D:, :] = two_rows(jnp.sum(go_low.astype(f32) * mixed_ref[...], axis=0, keepdims=True))
        spread = dot(vbt[...], goaug[...])
        yield True
        gv[0:D, 0:KK] += dot_nt(go_low, low_ref[...])
        gse[0:KK, :] = (low_ref[...].astype(f32) * spread).astype(bf16)
        back = dot(a2[...], gse[0:KK, :])
        yield True
        gse[KK : KK + D, :] = unskew_rows(back[D : D + 24], row).astype(bf16)
        gse[KK + D : KK + 256, :] = unskew_columns(back[D + 24 : D + 48], col).astype(bf16)
        yield True
        outer = dot_nt(qb[:, here], gse[...])
        gkr[0:D, 0 : KK + 256] += outer
        hacc[i] = outer[:, 384:512]
        gq[:, inner(i, tile)] = go + SCORE_SCALE * back[0:D] + dot(relt[...], gse[KK : KK + 256, :])

    one, two = slots
    gy_copy.wait()

    def attend(k, carry):
        interleave(ahead(2 * k + 1, two), behind(2 * k, one))
        interleave(ahead(2 * k + 2, one), behind(2 * k + 1, two))
        return carry

    interleave(ahead(0, one))
    lax.fori_loop(0, (TILES - 1) // 2, attend, 0)
    if TILES % 2 == 0:
        interleave(ahead(TILES - 1, two), behind(TILES - 2, one))
        interleave(behind(TILES - 1, two))
    else:
        interleave(behind(TILES - 1, one))

    out_copy = pltpu.make_async_copy(out_ref, out_hbm, copy_sem.at[2])
    out_copy.start()
    mid_copy = pltpu.make_async_copy(gm, mid_hbm, copy_sem.at[3])
    mid_copy.start()

    gkt[...] = jnp.transpose(gkr[:, 0:512])[0:KK, :] * SCORE_SCALE
    gvt[...] = jnp.transpose(gv[...])[0:KK, :]

    def pool_gradient(name, columns):
        low = columns.astype(bf16)
        for i in range(9):
            spread = dot_nt(low, tsel_ref[i]) * zsel_ref[i].astype(f32)
            gr[ROW[name] + i : ROW[name] + i + 1, 0:D] = jnp.sum(spread, axis=0, keepdims=True)

    for field, kernel_rows, pooled, gspread, name in ((fk, kk, gkt, gfk, "pool_k"), (fv, kv, gvt, gfv, "pool_v")):
        taps = tap_rows(kernel_rows)
        sums = [jnp.zeros((KG, 128), f32) for _ in range(9)]
        for a in range(KG):
            grad = pooled[KG * a : KG * a + KG, :]
            inside = jnp.where(b_index == 0, 0.0, grad)
            for k in range(9):
                where = pl.ds(tap_start(a, k // 3, k % 3), KG, stride=KSTR)
                sums[k] = sums[k] + (inside if k % 3 == 0 else grad) * field[where, :]
            spread_keys(taps, grad, a, gspread)
            if a == KG - 1:
                gspread[LEAD + TOK - GRID : LEAD + TOK, :] = jnp.zeros((GRID, 128), f32)
        rows = [jnp.sum(total, axis=0, keepdims=True) for total in sums]
        rows = jnp.concatenate(rows + [jnp.zeros((128 - 9, 128), f32)], axis=0)
        pool_gradient(name, jnp.transpose(rows)[:D, :])

    def finish(i, carry):
        tile = TILE_THREE
        wide = tile + 2 * HALO
        here = plain(i, tile)
        mid = slice(HALO, HALO + tile)
        mask = token_mask(i, tile)
        col = jnp.broadcast_to(idx_ref[1:2, inner(i, tile)], (8, tile))
        first, last = col == 0, col == GRID - 1
        for pair in range(D // 16):
            fields, moved = [], []
            for half in range(2):
                ch = slice(16 * pair + 8 * half, 16 * pair + 8 * half + 8)
                grad = gq[ch, window(i, tile)]
                below, above = pltpu.roll(grad, wide - GRID, 1), pltpu.roll(grad, GRID, 1)

                def col_sum(v):
                    return tap(v, ch, wide) * below + tap(v + 3, ch, wide) * grad + tap(v + 6, ch, wide) * above

                after = jnp.where(last, 0.0, pltpu.roll(col_sum(0), wide - 1, 1)[:, mid])
                before = jnp.where(first, 0.0, pltpu.roll(col_sum(2), 1, 1)[:, mid])
                fields.append((after + col_sum(1)[:, mid] + before) * mask)
                moved.append((below[:, mid], grad[:, mid], above[:, mid]))
            gfield[16 * pair : 16 * pair + 16, here] = jnp.concatenate(fields, axis=0).astype(bf16)
            for u in range(3):
                both = jnp.concatenate([moved[0][u], moved[1][u]], axis=0)
                place = group_row(pair, u)
                gsh[place : place + 16, :] = both.astype(bf16)
        for k in range(3):
            group = slice(k * D, (k + 1) * D)
            kqacc[group, 0:D] += dot_nt(gsh[group, :], fcol[group, here])
        flat = pl.ds(pl.multiple_of(i * tile + LEAD, 8), tile)
        gkv[:, 0:128] = gfk[flat, :].astype(bf16)
        gkv[:, 128:256] = gfv[flat, :].astype(bf16)
        dwq[:, 0:112] += dot_nt(gfield[:, here], un[:, here])
        dwkv[0:112, :] += dot(un[:, here], gkv[...])
        field_copy(i).start()
        return carry

    def field_copy(i):
        here = plain(i, TILE_THREE)
        return pltpu.make_async_copy(gfield.at[:, here], field_hbm.at[:, here], copy_sem.at[5 + i])

    lax.fori_loop(0, TOK // TILE_THREE, finish, 0)
    out_copy.wait()
    mid_copy.wait()
    unit_copy.wait()

    def write(name, rows, first=0):
        base = ROW[name] + first
        gr[base : base + rows.shape[0], 0:D] = rows

    def wide_rows(rows):
        return jnp.concatenate([rows, jnp.zeros((rows.shape[0], 128 - D), f32)], axis=1)

    def through_norm(name, first, outer, bias, gain_row, shift_row):
        raw = piece(name, outer.shape[0], first)[:, :D]
        write(name, outer * gain_row[:, :D] + bias * shift_row[:, :D], first)
        return jnp.sum(raw * outer, axis=0, keepdims=True), jnp.sum(raw * bias, axis=0, keepdims=True)

    gain, shift = through_norm("w_qkv", 0, dwq[:, 0:D], dwq[:, D : D + 1], g1_row, b1_row)
    write("b_qkv", jnp.transpose(dwq[...])[D : D + 1, :])
    for k in (1, 2):
        turned = jnp.transpose(dwkv[:, 128 * k - 128 : 128 * k])[0:D, :]
        more_gain, more_shift = through_norm("w_qkv", k * D, turned[:, 0:D], turned[:, D : D + 1], g1_row, b1_row)
        gain, shift = gain + more_gain, shift + more_shift
        write("b_qkv", dwkv[D : D + 1, 128 * k - 128 : 128 * k - 128 + D], k)
    write("ln1_g", gain)
    write("ln1_b", shift)

    lane = lax.broadcasted_iota(jnp.int32, (D, 128), 1)
    within = lane - lax.rem(lax.broadcasted_iota(jnp.int32, (D, 128), 0), 32)
    columns = jnp.zeros((D, 128), f32)
    for k in range(9):
        u, v = k // 3, k % 3
        picked = jnp.concatenate([kqacc[D * g + 32 * u : D * g + 32 * u + 32, :] for g in range(3)], axis=0)
        one = jnp.where(within == 32 * v, picked, 0.0)
        columns = jnp.where(lane == k, jnp.sum(one, axis=1, keepdims=True), columns)
    pool_gradient("pool_q", columns)

    for i in range(TILES):
        turned = jnp.transpose(hacc[i])
        for k in range(4):
            count = KG + ROW_STEPS - 1
            where = pl.ds(ROW["rel_h"] + 3 + k + TILE_ROWS * i, count, stride=4)
            gr[where, :] = gr[where, :] + wide_rows(turned[16 + 24 * k : 16 + 24 * k + count])
    turned = jnp.transpose(gkr[0:D, 384:768])
    for k in range(4):
        gr[pl.ds(ROW["rel_w"] + 3 + k, 39, stride=4), :] = wide_rows(turned[112 + 40 * k : 151 + 40 * k])

    write("w_proj", dpr[:, 0:D])
    write("b_proj", jnp.transpose(dpr[...])[D : D + 1, :])
    turned = jnp.transpose(dw1[...])
    gain, shift = through_norm(
        "w_fc1", 0, turned[:, 0:D] * math.sqrt(2.0 / math.pi), turned[:, D : D + 1] * math.sqrt(1.0 / math.pi), g2_row, b2_row
    )
    write("ln2_g", gain)
    write("ln2_b", shift)
    for k in range(4):
        write("b_fc1", dw1[D : D + 1, k * D : (k + 1) * D] * math.sqrt(1.0 / math.pi), k)
        gr[pl.ds(ROW["w_fc2"] + k, D, stride=4), :] = wide_rows(dw2[:, k * D : (k + 1) * D] * math.sqrt(2.0 / math.pi))
    write("b_fc2", jnp.transpose(dw2[:, HID:512])[0:1, :])
    for i in range(TOK // TILE_THREE):
        field_copy(i).wait()
    for w, start in enumerate(starts):
        gchunk_ref[w] = gr[start : start + rows_of, 0:D].astype(bf16)


def image_step(shard_len, chunks, pixels, image_side, cotangent):
    starts = tuple((shard_len * w) // D for w in range(chunks.shape[0]))
    rows_of = block_rows(shard_len)
    groups = -(-(shard_len * len(starts)) // (4 * D))
    depth = max(8 * (-(-(starts[-1] + rows_of) // 8)), 4 * groups)
    flat_rows = max(3 * groups, (shard_len * (len(starts) - 1)) // 128 + chunks.shape[1] + 1)
    flat_rows = 8 * (-(-flat_rows // 8))
    zsel, tsel = pool_selectors()
    vm = pltpu.VMEM
    scratch = [
        vm((depth, 128), f32),
        vm((D, 112), bf16), vm((112, 128), bf16), vm((112, 128), bf16),
        vm((D, 112), bf16), vm((D, D), bf16),
        vm((HID, 112), bf16), vm((D, HID), bf16), vm((D, KK), bf16), vm((HID, D), bf16),
        vm((168, 128), f32), vm((256, D), bf16), vm((D, 256), bf16),
        vm((D, 128), f32), vm((9, D, 128), f32),
        vm((D, TOK + 2 * HALO), f32), vm((FIELD, 128), f32), vm((FIELD, 128), f32),
        vm((D, TOK), bf16), vm((D, TOK), bf16),
        vm((112, TOK), bf16), vm((3 * D, TOK), bf16),
        vm((KK, 208), bf16), vm((144, KK), bf16), vm((112, KK), bf16), vm((KK, 112), bf16),
        vm((KK, 128), f32), vm((KK, 128), f32),
        vm((208, TILE_TWO), bf16), vm((KK + 256, TILE_TWO), bf16), vm((112, TILE_PROJECT), bf16), vm((112, TILE_TWO), bf16),
        vm((3 * D, TILE_THREE), bf16), vm((TILE_THREE, 256), bf16),
        vm((D, 512), f32), vm((128, HID), f32), vm((D, 128), f32), vm((128, 512), f32), vm((128, 768), f32),
        vm((TILES, D, 128), f32),
        vm((D, 128), f32), vm((128, 256), f32), vm((3 * D, 128), f32),
        vm((depth, 128), f32),
        vm((D, TOK), bf16), vm((D, TOK), bf16), vm((D, TOK), bf16), vm((D, TOK), bf16),
        pltpu.SemaphoreType.DMA((5 + TOK // TILE_THREE,)),
        vm((flat_rows, 128), f32),
        vm(zsel.shape, bf16), vm(tsel.shape, bf16), vm((8, TOK + 2 * HALO), jnp.int32), pltpu.SemaphoreType.DMA((3,)),
    ]
    slot = [
        vm((KK, TILE_TWO), f32), vm((KK, TILE_TWO), bf16), vm((D, TILE_TWO), f32), vm((D, TILE_TWO), f32), vm((HID, TILE_TWO), f32),
        vm((KK, TILE_TWO), bf16), vm((112, TILE_TWO), bf16), vm((112, TILE_TWO), bf16), vm((8, TILE_TWO), f32),
    ]
    whole = pl.BlockSpec(memory_space=pltpu.VMEM)
    far = pl.BlockSpec(memory_space=pl.ANY)
    shape = jax.ShapeDtypeStruct
    out, grad_chunks, *rest = pl.pallas_call(
        functools.partial(image_kernel, shard_len, starts, rows_of),
        out_shape=(
            shape((D, TOK), bf16), shape((len(starts), rows_of, D), bf16),
            shape((D, TOK), bf16), shape((D, TOK), bf16), shape((D, TOK), bf16), shape((8, TOK), f32),
            shape((KK, 128), f32), shape((KK, 128), f32), shape((16, 128), f32), shape((16, 128), f32),
            shape((D, D), bf16), shape((D, 256), bf16),
        ),
        in_specs=[pl.BlockSpec(memory_space=pltpu.SMEM), whole, far, far, far, far, far],
        out_specs=(far, whole, far, far, far) + (whole,) * 7,
        scratch_shapes=scratch + slot + slot,
        compiler_params=pltpu.CompilerParams(vmem_limit_bytes=54 * 1024 * 1024),
        name="image_step",
    )(image_side, chunks, pixels, cotangent, lane_index(), zsel, tsel)
    return out, grad_chunks, rest


def input_step(rest):
    far = pl.BlockSpec(memory_space=pl.ANY)
    vm = pltpu.VMEM
    scratch = [vm(part.shape, part.dtype) for part in rest]
    scratch += [vm((D, TOK), bf16), vm((FIELD, 128), f32), vm((FIELD, 128), f32), vm((TILE_THREE, 256), bf16)]
    return pl.pallas_call(
        input_kernel,
        out_shape=jax.ShapeDtypeStruct((D, TOK), bf16),
        in_specs=[far] * len(rest),
        out_specs=far,
        scratch_shapes=scratch + [pltpu.SemaphoreType.DMA((10 + TOK // TILE_THREE,))],
        compiler_params=pltpu.CompilerParams(vmem_limit_bytes=60 * 1024 * 1024),
        cost_estimate=pl.CostEstimate(flops=2 * D * 3 * D * TOK, bytes_accessed=16 * 1024 * 1024, transcendentals=0),
        name="input_step",
    )(*rest)


def adam_update(gradient, master_part, first_part, second_part, average_part, step_rates):
    moment_one = beta_first * first_part + (1.0 - beta_first) * gradient
    moment_two = beta_second * second_part + (1.0 - beta_second) * gradient * gradient
    fix_one = 1.0 - beta_first**STEP
    fix_two = 1.0 - beta_second**STEP
    direction = moment_one / fix_one / (jnp.sqrt(moment_two / fix_two) + adam_eps)
    updated = master_part - step_rates * (direction + weight_decay * master_part)
    blended = average_decay * average_part + (1.0 - average_decay) * updated
    return (updated, moment_one, moment_two, blended)


def shards(tokens, image_sides, grad_out, master, first_moment, second_moment, weight_average):
    shard_len = master.shape[0]
    owners = lax.axis_size("wide")
    images_all = tokens.shape[0] * owners * lax.axis_size("narrow")
    rows_of = block_rows(shard_len)
    inset = lax.rem(lax.axis_index("wide") * shard_len, D)

    filled = 1024 * (-(-shard_len // 1024))
    own = jnp.pad(master, (0, filled - shard_len)).reshape(1, filled // 128, 128).astype(bf16)
    chunks = lax.all_to_all(jnp.broadcast_to(own, (owners, filled // 128, 128)), "wide", 0, 0)

    outs, grads_in, grad_chunks = [], [], None
    for k in range(tokens.shape[0]):
        out, chunk, rest = image_step(shard_len, chunks, tokens[k], image_sides[k : k + 1], grad_out[k])
        outs.append(out)
        grads_in.append(input_step(rest))
        grad_chunks = chunk if k == 0 else (grad_chunks.astype(f32) + chunk.astype(f32)).astype(bf16)
    block_out = jnp.stack(outs)
    grad_in = jnp.stack(grads_in)

    parts = lax.all_to_all(grad_chunks, "wide", 0, 0)
    step_rates = lax.dynamic_slice_in_dim(
        jnp.asarray(rate_values(shard_len * owners)), lax.axis_index("wide") * shard_len, shard_len
    )
    parts, grad_in, step_rates = lax.optimization_barrier((parts, grad_in, step_rates))
    total = jnp.sum(parts.astype(f32), axis=0)
    total = total + lax.ppermute(total, "narrow", [(0, 1), (1, 0)])
    reduced = lax.dynamic_slice(total.reshape(rows_of * D), (inset,), (shard_len,))
    updated, moment_one, moment_two, blended = adam_update(
        reduced / images_all, master, first_moment, second_moment, weight_average, step_rates
    )
    return (block_out, grad_in, updated, moment_one, moment_two, blended)


def solution(mesh):
    return jax.shard_map(
        shards,
        mesh=mesh,
        in_specs=(
            P(("wide", "narrow"), None, None),
            P(("wide", "narrow")),
            P(("wide", "narrow"), None, None),
            P("wide"),
            P("wide"),
            P("wide"),
            P("wide"),
        ),
        out_specs=(
            P(("wide", "narrow"), None, None),
            P(("wide", "narrow"), None, None),
            P("wide"),
            P("wide"),
            P("wide"),
            P("wide"),
        ),
        check_vma=False,
    )
```
